512 devices in a mesh: pb: 16 (over x_hi, y, core), ka: 32 (over x_lo, z).
Axes of the slice: x: 4 (x_hi: 2, x_lo: 2; x = x_hi * 2 + x_lo), y: 4, z: 16, core: 2. Of those that a mesh axis runs over, the one named last changes fastest.
Arguments:
- teacher_q: float32 [2, 12288, 256], P(None, 'ka')
- student_q: float32 [2, 12288, 128], P(None, 'ka')
Outputs:
- query_grad: float32 [2, 12288, 128], P(None, 'ka')
- loss: float32 [], replicated
All inputs are finite; a program needn't handle non-finite values.
Results may differ from the reference program's by a relative error of at most 0.00029.
Values sent between devices are 32-bit elements; how exact they have to be, the bound alone decides.
No kernel may reach another device: no remote copies, remote signals or barrier semaphores. Data moves between devices by JAX's collectives and lax.ppermute only.
A program may use at most 64 MiB of HBM per device.

```python
import math
import jax
import jax.numpy as jnp
from jax import lax

BATCH = 2
HEADS = 1
DT = 256
DS = 128
SEQ = 12288


def draw_queries(key, columns, base):
    keys = jax.random.split(key, 3)
    position = jnp.arange(SEQ)
    normal_part = jax.random.truncated_normal(keys[0], -6.0, 6.0, (BATCH, SEQ, columns), jnp.float32)
    token_scale = jnp.exp(jax.random.uniform(keys[2], (BATCH, SEQ, 1), jnp.float32, math.log(0.3), math.log(3.0)))
    rising = 1.0 + 0.8 * position.astype(jnp.float32)[None, :, None] / SEQ
    queries = base * normal_part * token_scale * rising
    return queries


def draw_teacher_q(key, part):
    return draw_queries(jax.random.fold_in(key, 11), HEADS * DT, 0.25)


def draw_student_q(key, part):
    return draw_queries(jax.random.fold_in(key, 23), HEADS * DS, 0.3)


def setup_inputs(seed: int = 0) -> dict:
    streams_of = jax.random.split(jax.random.key(seed), 3)
    return {
        "teacher_q": draw_teacher_q(jax.random.fold_in(streams_of[2], 71), 0),
        "student_q": draw_student_q(jax.random.fold_in(streams_of[2], 71), 0),
    }


precise = lax.Precision.HIGHEST

def relation_head(teacher_head, student_head):
    row_block = math.gcd(SEQ, 512)
    number = SEQ // row_block
    teacher_factor = 1.0 / math.sqrt(DT)
    student_factor = 1.0 / math.sqrt(DS)
    teacher_blocks = teacher_head.reshape(number, row_block, DT)
    student_blocks = student_head.reshape(number, row_block, DS)

    def advance(column_grad, blocks):
        teacher_rows, student_rows = blocks
        teacher_tile = jnp.dot(teacher_rows, teacher_head.T, precision=precise, preferred_element_type=jnp.float32) * teacher_factor
        student_tile = jnp.dot(student_rows, student_head.T, precision=precise, preferred_element_type=jnp.float32) * student_factor
        teacher_max = lax.optimization_barrier(jnp.max(teacher_tile, axis=1))
        student_max = lax.optimization_barrier(jnp.max(student_tile, axis=1))
        teacher_exp = jnp.exp(teacher_tile - teacher_max[:, None])
        student_exp = jnp.exp(student_tile - student_max[:, None])
        teacher_sum = lax.optimization_barrier(jnp.sum(teacher_exp, axis=1))
        student_sum = lax.optimization_barrier(jnp.sum(student_exp, axis=1))
        cross = lax.optimization_barrier(jnp.sum(teacher_exp * (teacher_tile - student_tile), axis=1))
        divergence = cross / teacher_sum - teacher_max - jnp.log(teacher_sum) + student_max + jnp.log(student_sum)
        grad_scores = (student_exp / student_sum[:, None] - teacher_exp / teacher_sum[:, None]) / HEADS
        row_grad = jnp.dot(grad_scores, student_head, precision=precise, preferred_element_type=jnp.float32) * student_factor
        column_grad = column_grad + jnp.dot(grad_scores.T, student_rows, precision=precise, preferred_element_type=jnp.float32) * student_factor
        return (column_grad, (divergence, row_grad))
    column_grad, (divergence, row_grad) = lax.scan(advance, jnp.zeros((SEQ, DS), jnp.float32), (teacher_blocks, student_blocks))
    return (jnp.sum(divergence), row_grad.reshape(SEQ, DS) + column_grad)

def reference(teacher_q, student_q):
    sequences = []
    summed = []
    for seq_index in range(BATCH):
        gradients = []
        for head_index in range(HEADS):
            head_sum, head_grad = relation_head(teacher_q[seq_index, :, head_index * DT:(head_index + 1) * DT], student_q[seq_index, :, head_index * DS:(head_index + 1) * DS])
            gradients.append(head_grad)
            summed.append(head_sum)
        sequences.append(jnp.concatenate(gradients, axis=1))
    loss = sum(summed) / (BATCH * HEADS * SEQ)
    return (jnp.stack(sequences, axis=0), loss)
```

```python
import math

import jax
import jax.numpy as jnp
from jax import lax
from jax.sharding import Mesh, PartitionSpec as P

DT = 256
DS = 128
AXES = ("xh", "y", "c", "xl", "zh", "zl")
SIZES = (2, 4, 2, 2, 8, 2)
PLANE = ("xl", "xh", "y")
COPIES = ("c", "xh", "y")


precise = lax.Precision.HIGHEST


def permute(x, move):
    pairs = []
    for index in range(512):
        rest, where = index, []
        for size in reversed(SIZES):
            where.append(rest % size)
            rest //= size
        xh, y, c, xl, zh, zl = reversed(where)
        target = move(xh, y, c, xl, zh * 2 + zl)
        xh, y, c, xl, z = target
        to = ((((xh * 4 + y) * 2 + c) * 2 + xl) * 8 + z // 2) * 2 + z % 2
        pairs.append((index, to))
    return lax.ppermute(x, AXES, pairs)


def shards(teacher_q, student_q):
    c = lax.axis_index("c")
    xl = lax.axis_index("xl")
    zl = lax.axis_index("zl")
    sub = lax.axis_index("xh") * 4 + lax.axis_index("y")
    own_rows = teacher_q.shape[1]
    share = own_rows // 8
    own = jnp.concatenate(
        [
            lax.dynamic_index_in_dim(teacher_q, c, 0, keepdims=False),
            lax.dynamic_index_in_dim(student_q, c, 0, keepdims=False),
        ],
        axis=1,
    )
    other = permute(own, lambda xh, y, c, xl, z: (xh, y, c, 1 - xl, z))
    shard = lax.dynamic_slice_in_dim(own, sub * share, share, 0)
    near = lax.all_gather(shard, "zh", tiled=True)
    half = near.shape[0] // 2
    above = permute(near[:half], lambda xh, y, c, xl, z: (xh, y, c, xl, (z - 1) % 16))
    below = permute(near[half:], lambda xh, y, c, xl, z: (xh, y, c, xl, (z + 1) % 16))
    rows = jnp.where(
        xl == 0, jnp.concatenate([own, other], 0), jnp.concatenate([other, own], 0)
    )
    keys = jnp.concatenate([near, above, below], 0)
    teacher = jnp.einsum("rd,kd->rk", rows[:, :DT], keys[:, :DT], precision=precise) * (
        1.0 / math.sqrt(DT)
    )
    student = jnp.einsum("rd,kd->rk", rows[:, DT:], keys[:, DT:], precision=precise) * (
        1.0 / math.sqrt(DS)
    )
    teacher_max = jnp.max(teacher, axis=1)
    student_max = jnp.max(student, axis=1)
    teacher_exp = jnp.exp(teacher - teacher_max[:, None])
    student_exp = jnp.exp(student - student_max[:, None])
    local = jnp.stack(
        [
            teacher_max,
            jnp.sum(teacher_exp, axis=1),
            jnp.sum(teacher_exp * (teacher - student), axis=1),
            student_max,
            jnp.sum(student_exp, axis=1),
        ]
    ).reshape(1, -1, 128)
    everyone = lax.all_to_all(
        jnp.broadcast_to(local, (16, *local.shape[1:])), PLANE, 0, 0, tiled=True
    ).reshape(16, 5, -1)
    tm, ts, cr, sm, ss = (everyone[:, i] for i in range(5))
    teacher_top = jnp.max(tm, axis=0)
    student_top = jnp.max(sm, axis=0)
    scale = jnp.exp(tm - teacher_top)
    teacher_sum = jnp.sum(ts * scale, axis=0)
    cross = jnp.sum(cr * scale, axis=0)
    student_sum = jnp.sum(ss * jnp.exp(sm - student_top), axis=0)
    teacher_lse = teacher_top + jnp.log(teacher_sum)
    student_lse = student_top + jnp.log(student_sum)
    divergence = jnp.sum(cross / teacher_sum - teacher_lse + student_lse)
    mine = xl * own_rows + sub * share
    message = jnp.concatenate(
        [
            lax.dynamic_slice_in_dim(teacher_lse, mine, share, 0),
            lax.dynamic_slice_in_dim(student_lse, mine, share, 0),
            jnp.broadcast_to(divergence, (128 - 2 * share,)),
        ]
    ).reshape(1, 1, 128)
    planes = lax.all_to_all(
        jnp.broadcast_to(message, (16, 1, 128)), ("zl", "zh"), 0, 0, tiled=True
    ).reshape(2, 8, 128)
    divergence = jnp.sum(planes[:, :, 127])
    planes = jnp.where(zl == 0, planes, planes[::-1]).reshape(16, 128)
    teacher_key = planes[:, :share].reshape(-1)
    student_key = planes[:, share : 2 * share].reshape(-1)
    mixed = (
        jnp.exp(student - student_lse[:, None])
        + jnp.exp(student - student_key[None, :])
        - jnp.exp(teacher - teacher_lse[:, None])
        - jnp.exp(teacher - teacher_key[None, :])
    )
    partial = jnp.einsum("rk,kd->rd", mixed, keys[:, DT:], precision=precise)
    parts = lax.all_to_all(partial.reshape(16, share, DS), PLANE, 0, 0, tiled=True)
    total = jnp.sum(parts, axis=0) * (1.0 / math.sqrt(DS))
    block = jnp.concatenate([total, jnp.full((8, DS), divergence)], 0)
    blocks = lax.all_to_all(
        jnp.broadcast_to(block[None], (16, share + 8, DS)), COPIES, 0, 0, tiled=True
    )
    query_grad = blocks[:, :share].reshape(2, own_rows, DS)
    tokens = 2 * own_rows * 32
    loss = (blocks[0, share, 0] + blocks[8, share, 0]) / tokens
    return (query_grad, loss)


def solution(mesh):
    fine = Mesh(mesh.devices.reshape(SIZES), AXES)
    in_specs = (P(None, ("xl", "zh", "zl"), None), P(None, ("xl", "zh", "zl"), None))
    out_specs = (P(None, ("xl", "zh", "zl"), None), P())
    return jax.shard_map(shards, mesh=fine, in_specs=in_specs, out_specs=out_specs, check_vma=False)
```

```python
import math

import jax
import jax.numpy as jnp
from jax import lax
from jax.experimental import pallas as pl
from jax.experimental.pallas import tpu as pltpu
from jax.sharding import Mesh, PartitionSpec as P

DT = 256
DS = 128
AXES = ("xh", "y", "c", "xl", "zh", "zl")
SIZES = (2, 4, 2, 2, 4, 4)
PLANE = ("xl", "xh", "y")
COPIES = ("c", "xh", "y")
LINE = ("zh", "zl")
BLOCK = 384
SHARE = 48
ROWS = 768
LOG2E = math.log2(math.e)


F32 = jnp.float32
BF16 = jnp.bfloat16


def shape(*dims, dtype=F32):
    return jax.ShapeDtypeStruct(dims, dtype)


def call(body, outs, ins, scratch=()):
    return pl.pallas_call(
        body,
        out_shape=outs,
        in_specs=[pl.BlockSpec(memory_space=pltpu.VMEM)] * len(ins),
        scratch_shapes=scratch,
        compiler_params=pltpu.CompilerParams(vmem_limit_bytes=24 << 20),
    )(*ins)


def permute(x, move):
    pairs = []
    for index in range(512):
        rest, where = index, []
        for size in reversed(SIZES):
            where.append(rest % size)
            rest //= size
        xh, y, c, xl, zh, zl = reversed(where)
        xh, y, c, xl, z = move(xh, y, c, xl, zh * 4 + zl)
        to = ((((xh * 4 + y) * 2 + c) * 2 + xl) * 4 + z // 4) * 4 + z % 4
        pairs.append((index, to))
    return lax.ppermute(x, AXES, pairs)


def from_plane(x, offset):
    return permute(x, lambda xh, y, c, xl, z: (xh, y, c, xl, (z - offset) % 16))


def sub_index():
    return lax.axis_index("xh") * 4 + lax.axis_index("y")


def split(x):
    high = x.astype(BF16)
    return high, (x - high.astype(F32)).astype(BF16)


def select_kernel(teacher, student, own, shard):
    c = lax.axis_index("c")
    own[:, :DT] = teacher[c]
    own[:, DT:] = student[c]
    start = pl.multiple_of(sub_index() * SHARE, 16)
    shard[...] = own[pl.ds(start, SHARE), :]


def score_kernel(own, other, near, up1, down1, up2, down2, t_out, s_out, kth, ktl, stats, rh, rl, kh, kl):
    xl = lax.axis_index("xl")
    zl = lax.axis_index("zl")
    for ref, place in ((own, xl), (other, 1 - xl)):
        start = pl.multiple_of(place * BLOCK, BLOCK)
        for lo, hi, factor in ((0, DT, LOG2E / math.sqrt(DT)), (DT, DT + DS, LOG2E / math.sqrt(DS))):
            high, low = split(ref[:, lo:hi] * factor)
            rh[pl.ds(start, BLOCK), lo:hi] = high
            rl[pl.ds(start, BLOCK), lo:hi] = low
    for ref, offset, first, count in (
        (near, 0, 0, 4),
        (up1, 1, 0, 4),
        (down1, 3, 0, 4),
        (up2, 2, 0, 2),
        (down2, 2, 2, 2),
    ):
        residue = lax.rem(zl + offset, 4)
        for h in range(count):
            start = pl.multiple_of((4 * (first + h) + residue) * SHARE, 16)
            high, low = split(ref[h * SHARE : (h + 1) * SHARE, :])
            kh[pl.ds(start, SHARE), :] = high
            kl[pl.ds(start, SHARE), :] = low
    kth[...] = kh[:, DT:].astype(F32).T.astype(BF16)
    ktl[...] = kl[:, DT:].astype(F32).T.astype(BF16)

    def product(a, b):
        return lax.dot_general(a, b, (((1,), (1,)), ((), ())), preferred_element_type=F32)

    tops = []
    for out, lo, hi in ((t_out, 0, DT), (s_out, DT, DT + DS)):
        top = None
        for k in range(3):
            keys = slice(256 * k, 256 * k + 256)
            tile = product(kh[keys, lo:hi], rh[:, lo:hi])
            tile += product(kh[keys, lo:hi], rl[:, lo:hi])
            tile += product(kl[keys, lo:hi], rh[:, lo:hi])
            out[keys, :] = tile
            here = jnp.max(tile.reshape(32, 8, ROWS), axis=0)
            top = here if top is None else jnp.maximum(top, here)
        tops.append(jnp.max(top, axis=0, keepdims=True))
    t_top, s_top = tops

    def step(i, sums):
        t_sum, cross, s_sum = sums
        start = pl.multiple_of(i * SHARE, SHARE)
        t = t_out[pl.ds(start, SHARE), :]
        s = s_out[pl.ds(start, SHARE), :]
        te = jnp.exp2(t - t_top)
        se = jnp.exp2(s - s_top)
        t_sum = t_sum + jnp.sum(te.reshape(6, 8, ROWS), axis=0)
        cross = cross + jnp.sum((te * (t - s)).reshape(6, 8, ROWS), axis=0)
        s_sum = s_sum + jnp.sum(se.reshape(6, 8, ROWS), axis=0)
        return t_sum, cross, s_sum

    zero = jnp.zeros((8, ROWS), F32)
    t_sum, cross, s_sum = lax.fori_loop(0, 16, step, (zero, zero, zero))
    t_sum = jnp.sum(t_sum, axis=0, keepdims=True)
    cross = jnp.sum(cross, axis=0, keepdims=True)
    s_sum = jnp.sum(s_sum, axis=0, keepdims=True)
    values = (
        t_top + jnp.log(t_sum) * LOG2E,
        s_top + jnp.log(s_sum) * LOG2E,
        cross / t_sum,
    )
    pad = jnp.zeros((2, 128), F32)
    packed = []
    for v in values:
        packed += [v[:, 128 * j : 128 * j + 128] for j in range(6)] + [pad]
    packed = jnp.concatenate(packed, axis=0)
    for d in range(16):
        stats[d] = packed


def combine_kernel(everyone, lse, message):
    t = everyone[:, 0:8, :]
    s = everyone[:, 8:16, :]
    ratio = everyone[:, 16:24, :]
    t_top = jnp.max(t, axis=0)
    s_top = jnp.max(s, axis=0)
    t_weight = jnp.exp2(t - t_top)
    t_sum = jnp.sum(t_weight, axis=0)
    s_sum = jnp.sum(jnp.exp2(s - s_top), axis=0)
    t_lse = t_top + jnp.log(t_sum) * LOG2E
    s_lse = s_top + jnp.log(s_sum) * LOG2E
    divergence = jnp.sum(t_weight * ratio, axis=0) / t_sum - t_lse + s_lse
    divergence = jnp.sum(divergence[0:6, :])

    def as_row(v):
        return jnp.concatenate([v[j : j + 1, :] for j in range(6)], axis=1)

    both = jnp.concatenate(
        [as_row(t_lse), as_row(s_lse), jnp.zeros((6, ROWS), F32)], axis=0
    )
    lse[...] = both
    mine = lax.axis_index("xl") * BLOCK + sub_index() * SHARE
    turned = pltpu.roll(both, lax.rem(ROWS - mine, ROWS), axis=1)[:, :128]
    line = lax.broadcasted_iota(jnp.int32, (8, 128), 0)
    turned = jnp.where(line == 2, divergence, turned)
    for d in range(16):
        message[d] = turned


def mixed_kernel(t_in, s_in, lse, planes, kth, ktl, partial, square, mh, ml):
    columns = []
    for i in range(2):
        square[...] = jnp.zeros_like(square)
        square[0:16, :] = planes[:, i, :]
        columns.append(square[...].T)
    t_row = lse[0:1, :]
    s_row = lse[1:2, :]
    for p in range(16):
        part = slice(SHARE * p, SHARE * p + SHARE)
        t = t_in[part, :]
        s = s_in[part, :]
        t_key = columns[0][0:SHARE, p : p + 1]
        s_key = columns[1][0:SHARE, p : p + 1]
        mixed = (jnp.exp2(s - s_row) - jnp.exp2(t - t_row)) + (
            jnp.exp2(s - s_key) - jnp.exp2(t - t_key)
        )
        high, low = split(mixed)
        mh[part, :] = high
        ml[part, :] = low

    def product(a, b):
        return lax.dot_general(a, b, (((1,), (0,)), ((), ())), preferred_element_type=F32)

    grad = product(kth[...], mh[...]) + product(kth[...], ml[...]) + product(ktl[...], mh[...])
    partial[...] = grad.T


def total_kernel(parts, planes, blocks):
    total = jnp.sum(parts[...], axis=0) * (1.0 / math.sqrt(DS))
    divergence = jnp.sum(planes[:, 2, :], axis=0, keepdims=True)
    for d in range(16):
        blocks[d, 0:SHARE, :] = total
        blocks[d, SHARE:, :] = jnp.broadcast_to(divergence, (8, 128))


def finish_kernel(factor, blocks, grad, loss):
    grad[...] = blocks[:, 0:SHARE, :]
    loss[0, 0] = jnp.max(blocks[0, SHARE:, :] + blocks[8, SHARE:, :]) * factor


def shards(teacher_q, student_q):
    own, shard = call(
        select_kernel,
        (shape(BLOCK, DT + DS), shape(SHARE, DT + DS)),
        (teacher_q, student_q),
    )
    other = permute(own, lambda xh, y, c, xl, z: (xh, y, c, 1 - xl, z))
    near = lax.all_gather(shard, "zh", tiled=True)
    up1 = from_plane(near, 1)
    down1 = from_plane(near, -1)
    up2 = from_plane(near[: 2 * SHARE], 2)
    down2 = from_plane(near[2 * SHARE :], -2)
    t, s, kth, ktl, stats = call(
        score_kernel,
        (
            shape(ROWS, ROWS),
            shape(ROWS, ROWS),
            shape(DS, ROWS, dtype=BF16),
            shape(DS, ROWS, dtype=BF16),
            shape(16, 24, 128),
        ),
        (own, other, near, up1, down1, up2, down2),
        [pltpu.VMEM((ROWS, DT + DS), BF16)] * 4,
    )
    everyone = lax.all_to_all(stats, PLANE, 0, 0, tiled=True)
    lse, message = call(
        combine_kernel, (shape(8, ROWS), shape(16, 8, 128)), (everyone,)
    )
    planes = lax.all_to_all(message, LINE, 0, 0, tiled=True)
    partial = call(
        mixed_kernel,
        shape(ROWS, DS),
        (t, s, lse, planes, kth, ktl),
        [
            pltpu.VMEM((128, 128), F32),
            pltpu.VMEM((ROWS, ROWS), BF16),
            pltpu.VMEM((ROWS, ROWS), BF16),
        ],
    )
    parts = lax.all_to_all(partial.reshape(16, SHARE, DS), PLANE, 0, 0, tiled=True)
    blocks = call(total_kernel, shape(16, SHARE + 8, DS), (parts, planes))
    blocks = lax.all_to_all(blocks, COPIES, 0, 0, tiled=True)
    factor = 1.0 / (LOG2E * 2 * BLOCK * 32)

    def finish(blocks, grad, loss):
        finish_kernel(factor, blocks, grad, loss)

    grad, loss = pl.pallas_call(
        finish,
        out_shape=(shape(16, SHARE, DS), shape(1, 1)),
        in_specs=[pl.BlockSpec(memory_space=pltpu.VMEM)],
        out_specs=(pl.BlockSpec(memory_space=pltpu.VMEM), pl.BlockSpec(memory_space=pltpu.SMEM)),
    )(blocks)
    return (grad.reshape(2, BLOCK, DS), loss.reshape(()))


def solution(mesh):
    fine = Mesh(mesh.devices.reshape(SIZES), AXES)
    tokens = P(None, ("xl", "zh", "zl"), None)
    return jax.shard_map(
        shards, mesh=fine, in_specs=(tokens, tokens), out_specs=(tokens, P()), check_vma=False
    )
```

```python
import functools
import math

import jax
import jax.numpy as jnp
from jax import lax
from jax.experimental import pallas as pl
from jax.experimental.pallas import tpu as pltpu
from jax.sharding import Mesh, PartitionSpec as P

DT = 256
DS = 128
AXES = ("xh", "y", "c", "xl", "zh", "zl")
SIZES = (2, 4, 2, 2, 4, 4)
PLANE = ("xl", "xh", "y")
COPIES = ("c", "xh", "y")
LINE = ("zh", "zl")
BLOCK = 384
SHARE = 48
ROWS = 768
LOG2E = math.log2(math.e)


F32 = jnp.float32
BF16 = jnp.bfloat16


def shape(*dims, dtype=F32):
    return jax.ShapeDtypeStruct(dims, dtype)


def call(body, outs, ins, scratch=()):
    return pl.pallas_call(
        body,
        out_shape=outs,
        in_specs=[pl.BlockSpec(memory_space=pltpu.VMEM)] * len(ins),
        scratch_shapes=scratch,
        compiler_params=pltpu.CompilerParams(vmem_limit_bytes=24 << 20),
    )(*ins)


def permute(x, move):
    pairs = []
    for index in range(512):
        rest, where = index, []
        for size in reversed(SIZES):
            where.append(rest % size)
            rest //= size
        xh, y, c, xl, zh, zl = reversed(where)
        xh, y, c, xl, z = move(xh, y, c, xl, zh * 4 + zl)
        to = ((((xh * 4 + y) * 2 + c) * 2 + xl) * 4 + z // 4) * 4 + z % 4
        pairs.append((index, to))
    return lax.ppermute(x, AXES, pairs)


def from_plane(x, first, second):
    return permute(
        x, lambda xh, y, c, xl, z: (xh, y, c, xl, (z - (second if c else first)) % 16)
    )


def sub_index():
    return lax.axis_index("xh") * 4 + lax.axis_index("y")


def split(x):
    high = x.astype(BF16)
    return high, (x - high.astype(F32)).astype(BF16)


def select_kernel(teacher, student, own, shard, sems):
    c = lax.axis_index("c")
    mine = pl.ds(pl.multiple_of(sub_index() * SHARE, 8), SHARE)
    copies = (
        pltpu.make_async_copy(teacher.at[c, mine], shard.at[:, :DT], sems.at[0]),
        pltpu.make_async_copy(student.at[c, mine], shard.at[:, DT:], sems.at[1]),
        pltpu.make_async_copy(teacher.at[c], own.at[:, :DT], sems.at[2]),
        pltpu.make_async_copy(student.at[c], own.at[:, DT:], sems.at[3]),
    )
    for copy in copies:
        copy.start()
    for copy in copies:
        copy.wait()


def score_kernel(own, other, near, up, down, far, t_out, s_out, kth, ktl, stats, rh, rl, kh, kl):
    xl = lax.axis_index("xl")
    zl = lax.axis_index("zl")
    for ref, place in ((own, xl), (other, 1 - xl)):
        start = pl.multiple_of(place * BLOCK, BLOCK)
        for lo, hi, factor in ((0, DT, LOG2E / math.sqrt(DT)), (DT, DT + DS, LOG2E / math.sqrt(DS))):
            high, low = split(ref[:, lo:hi] * factor)
            rh[pl.ds(start, BLOCK), lo:hi] = high
            rl[pl.ds(start, BLOCK), lo:hi] = low
    for ref, offset in ((near, 0), (up, 1), (down, 3), (far, 2)):
        residue = lax.rem(zl + offset, 4)
        for h in range(4):
            start = pl.multiple_of((4 * h + residue) * SHARE, 16)
            high, low = split(ref[h * SHARE : (h + 1) * SHARE, :])
            kh[pl.ds(start, SHARE), :] = high
            kl[pl.ds(start, SHARE), :] = low
    kth[...] = kh[:, DT:].astype(F32).T.astype(BF16)
    ktl[...] = kl[:, DT:].astype(F32).T.astype(BF16)

    def product(a, b):
        return lax.dot_general(a, b, (((1,), (1,)), ((), ())), preferred_element_type=F32)

    tops = []
    for out, lo, hi in ((t_out, 0, DT), (s_out, DT, DT + DS)):
        top = None
        for k in range(3):
            keys = slice(256 * k, 256 * k + 256)
            tile = product(kh[keys, lo:hi], rh[:, lo:hi])
            tile += product(kh[keys, lo:hi], rl[:, lo:hi])
            tile += product(kl[keys, lo:hi], rh[:, lo:hi])
            out[keys, :] = tile
            here = jnp.max(tile.reshape(32, 8, ROWS), axis=0)
            top = here if top is None else jnp.maximum(top, here)
        tops.append(jnp.max(top, axis=0, keepdims=True))
    t_top, s_top = tops

    def step(i, sums):
        t_sum, cross, s_sum = sums
        start = pl.multiple_of(i * SHARE, SHARE)
        t = t_out[pl.ds(start, SHARE), :]
        s = s_out[pl.ds(start, SHARE), :]
        te = jnp.exp2(t - t_top)
        se = jnp.exp2(s - s_top)
        t_sum = t_sum + jnp.sum(te.reshape(6, 8, ROWS), axis=0)
        cross = cross + jnp.sum((te * (t - s)).reshape(6, 8, ROWS), axis=0)
        s_sum = s_sum + jnp.sum(se.reshape(6, 8, ROWS), axis=0)
        return t_sum, cross, s_sum

    zero = jnp.zeros((8, ROWS), F32)
    t_sum, cross, s_sum = lax.fori_loop(0, 16, step, (zero, zero, zero))
    t_sum = jnp.sum(t_sum, axis=0, keepdims=True)
    cross = jnp.sum(cross, axis=0, keepdims=True)
    s_sum = jnp.sum(s_sum, axis=0, keepdims=True)
    values = (
        t_top + jnp.log(t_sum) * LOG2E,
        s_top + jnp.log(s_sum) * LOG2E,
        cross / t_sum,
    )
    pad = jnp.zeros((2, 128), F32)
    packed = []
    for v in values:
        packed += [v[:, 128 * j : 128 * j + 128] for j in range(6)] + [pad]
    packed = jnp.concatenate(packed, axis=0)
    for d in range(16):
        stats[d] = packed


def combine_kernel(everyone, lse, message):
    t = everyone[:, 0:8, :]
    s = everyone[:, 8:16, :]
    ratio = everyone[:, 16:24, :]
    t_top = jnp.max(t, axis=0)
    s_top = jnp.max(s, axis=0)
    t_weight = jnp.exp2(t - t_top)
    t_sum = jnp.sum(t_weight, axis=0)
    s_sum = jnp.sum(jnp.exp2(s - s_top), axis=0)
    t_lse = t_top + jnp.log(t_sum) * LOG2E
    s_lse = s_top + jnp.log(s_sum) * LOG2E
    divergence = jnp.sum(t_weight * ratio, axis=0) / t_sum - t_lse + s_lse
    divergence = jnp.sum(divergence[0:6, :])

    def as_row(v):
        return jnp.concatenate([v[j : j + 1, :] for j in range(6)], axis=1)

    both = jnp.concatenate(
        [as_row(t_lse), as_row(s_lse), jnp.zeros((6, ROWS), F32)], axis=0
    )
    lse[...] = both
    mine = lax.axis_index("xl") * BLOCK + sub_index() * SHARE
    turned = pltpu.roll(both, lax.rem(ROWS - mine, ROWS), axis=1)[:, :128]
    line = lax.broadcasted_iota(jnp.int32, (8, 128), 0)
    turned = jnp.where(line == 2, divergence, turned)
    for d in range(16):
        message[d] = turned


def mixed_kernel(t_in, s_in, lse, planes, kth, ktl, partial, square, mh, ml):
    columns = []
    for i in range(2):
        square[...] = jnp.zeros_like(square)
        square[0:16, :] = planes[:, i, :]
        columns.append(square[...].T)
    t_row = lse[0:1, :]
    s_row = lse[1:2, :]
    for p in range(16):
        part = slice(SHARE * p, SHARE * p + SHARE)
        t = t_in[part, :]
        s = s_in[part, :]
        t_key = columns[0][0:SHARE, p : p + 1]
        s_key = columns[1][0:SHARE, p : p + 1]
        mixed = (jnp.exp2(s - s_row) - jnp.exp2(t - t_row)) + (
            jnp.exp2(s - s_key) - jnp.exp2(t - t_key)
        )
        high, low = split(mixed)
        mh[part, :] = high
        ml[part, :] = low

    def product(a, b):
        return lax.dot_general(a, b, (((1,), (0,)), ((), ())), preferred_element_type=F32)

    grad = product(kth[...], mh[...]) + product(kth[...], ml[...]) + product(ktl[...], mh[...])
    partial[...] = grad.T


def total_kernel(parts, planes, blocks):
    total = jnp.sum(parts[...], axis=0) * (1.0 / math.sqrt(DS))
    divergence = jnp.sum(planes[:, 2, :], axis=0, keepdims=True)
    for d in range(16):
        blocks[d, 0:SHARE, :] = total
        blocks[d, SHARE:, :] = jnp.broadcast_to(divergence, (8, 128))


def finish_kernel(factor, blocks, grad, loss, tails, sems):
    body = pltpu.make_async_copy(blocks.at[:, 0:SHARE], grad, sems.at[0])
    body.start()
    ends = [
        pltpu.make_async_copy(blocks.at[8 * c, SHARE:], tails.at[c], sems.at[1 + c])
        for c in range(2)
    ]
    for end in ends:
        end.start()
    for end in ends:
        end.wait()
    loss[0, 0] = jnp.max(tails[0] + tails[1]) * factor
    body.wait()


def shards(teacher_q, student_q):
    own, shard = pl.pallas_call(
        select_kernel,
        out_shape=(shape(BLOCK, DT + DS), shape(SHARE, DT + DS)),
        in_specs=[pl.BlockSpec(memory_space=pltpu.HBM)] * 2,
        out_specs=[pl.BlockSpec(memory_space=pl.ANY)] * 2,
        scratch_shapes=[pltpu.SemaphoreType.DMA((4,))],
        compiler_params=pltpu.CompilerParams(vmem_limit_bytes=1 << 20),
    )(teacher_q, student_q)
    other = permute(own, lambda xh, y, c, xl, z: (xh, y, c, 1 - xl, z))
    near = lax.all_gather(shard, "zh", tiled=True)
    far = from_plane(near, 2, -2)
    up = from_plane(near, 1, 1)
    down = from_plane(near, -1, -1)
    t, s, kth, ktl, stats = call(
        score_kernel,
        (
            shape(ROWS, ROWS),
            shape(ROWS, ROWS),
            shape(DS, ROWS, dtype=BF16),
            shape(DS, ROWS, dtype=BF16),
            shape(16, 24, 128),
        ),
        (own, other, near, up, down, far),
        [pltpu.VMEM((ROWS, DT + DS), BF16)] * 4,
    )
    everyone = lax.all_to_all(stats, PLANE, 0, 0, tiled=True)
    lse, message = call(
        combine_kernel, (shape(8, ROWS), shape(16, 8, 128)), (everyone,)
    )
    planes = lax.all_to_all(message, LINE, 0, 0, tiled=True)
    partial = call(
        mixed_kernel,
        shape(ROWS, DS),
        (t, s, lse, planes, kth, ktl),
        [
            pltpu.VMEM((128, 128), F32),
            pltpu.VMEM((ROWS, ROWS), BF16),
            pltpu.VMEM((ROWS, ROWS), BF16),
        ],
    )
    parts = lax.all_to_all(partial.reshape(16, SHARE, DS), PLANE, 0, 0, tiled=True)
    blocks = call(total_kernel, shape(16, SHARE + 8, DS), (parts, planes))
    blocks = lax.all_to_all(blocks, COPIES, 0, 0, tiled=True)
    factor = 1.0 / (LOG2E * 2 * BLOCK * 32)

    grad, loss = pl.pallas_call(
        functools.partial(finish_kernel, factor),
        out_shape=(shape(16, SHARE, DS), shape(1, 1)),
        in_specs=[pl.BlockSpec(memory_space=pl.ANY)],
        out_specs=(pl.BlockSpec(memory_space=pl.ANY), pl.BlockSpec(memory_space=pltpu.SMEM)),
        scratch_shapes=[pltpu.VMEM((2, 8, 128), F32), pltpu.SemaphoreType.DMA((3,))],
        compiler_params=pltpu.CompilerParams(vmem_limit_bytes=1 << 20),
    )(blocks)
    return (grad.reshape(2, BLOCK, DS), loss.reshape(()))


def solution(mesh):
    fine = Mesh(mesh.devices.reshape(SIZES), AXES)
    tokens = P(None, ("xl", "zh", "zl"), None)
    return jax.shard_map(
        shards, mesh=fine, in_specs=(tokens, tokens), out_specs=(tokens, P()), check_vma=False
    )
```

```python
import functools
import math

import jax
import jax.numpy as jnp
from jax import lax
from jax.experimental import pallas as pl
from jax.experimental.pallas import tpu as pltpu
from jax.sharding import Mesh, PartitionSpec as P

DT = 256
DS = 128
AXES = ("xh", "y", "c", "xl", "zh", "zl")
SIZES = (2, 4, 2, 2, 4, 4)
PLANE = ("xl", "c", "y")
COPIES = ("xh", "c", "y")
LINE = ("zh", "zl")
BLOCK = 384
SHARE = 48
ROWS = 768
SET = 192
OFFSETS = (0, 2, 3, 1)
LOG2E = math.log2(math.e)


F32 = jnp.float32
BF16 = jnp.bfloat16


def shape(*dims, dtype=F32):
    return jax.ShapeDtypeStruct(dims, dtype)


def call(body, outs, ins, scratch=()):
    return pl.pallas_call(
        body,
        out_shape=outs,
        in_specs=[pl.BlockSpec(memory_space=pltpu.VMEM)] * len(ins),
        scratch_shapes=scratch,
        compiler_params=pltpu.CompilerParams(vmem_limit_bytes=24 << 20),
    )(*ins)


def permute(x, move):
    pairs = []
    for index in range(512):
        rest, where = index, []
        for size in reversed(SIZES):
            where.append(rest % size)
            rest //= size
        xh, y, c, xl, zh, zl = reversed(where)
        xh, y, c, xl, z = move(xh, y, c, xl, zh * 4 + zl)
        to = ((((xh * 4 + y) * 2 + c) * 2 + xl) * 4 + z // 4) * 4 + z % 4
        pairs.append((index, to))
    return lax.ppermute(x, AXES, pairs)


def from_plane(x, first, second):
    return permute(
        x, lambda xh, y, c, xl, z: (xh, y, c, xl, (z - (second if c else first)) % 16)
    )


def sub_index():
    return lax.axis_index("c") * 4 + lax.axis_index("y")


def split(x):
    high = x.astype(BF16)
    return high, (x - high.astype(F32)).astype(BF16)


def select_kernel(teacher, student, own, shard, sems):
    seq = lax.axis_index("xh")
    mine = pl.ds(pl.multiple_of(sub_index() * SHARE, 8), SHARE)
    copies = (
        pltpu.make_async_copy(teacher.at[seq, mine], shard.at[:, :DT], sems.at[0]),
        pltpu.make_async_copy(student.at[seq, mine], shard.at[:, DT:], sems.at[1]),
        pltpu.make_async_copy(teacher.at[seq], own.at[:, :DT], sems.at[2]),
        pltpu.make_async_copy(student.at[seq], own.at[:, DT:], sems.at[3]),
    )
    for copy in copies:
        copy.start()
    for copy in copies:
        copy.wait()


def product(a, b):
    return lax.dot_general(a, b, (((1,), (1,)), ((), ())), preferred_element_type=F32)


def scores(kh, kl, rh, rl, keys, outs):
    tops = []
    for out, lo, hi in zip(outs, (0, DT), (DT, DT + DS)):
        tile = product(kh[keys, lo:hi], rh[:, lo:hi])
        tile += product(kh[keys, lo:hi], rl[:, lo:hi])
        tile += product(kl[keys, lo:hi], rh[:, lo:hi])
        out[keys, :] = tile
        tops.append(jnp.max(tile.reshape(-1, 8, ROWS), axis=0))
    return tops


def transposed(x):
    return x[:, DT:].astype(F32).T.astype(BF16)


def first_kernel(own, other, near, rh, rl, t_out, s_out, top, kth, ktl, kh, kl):
    xl = lax.axis_index("xl")
    for ref, place in ((own, xl), (other, 1 - xl)):
        start = pl.multiple_of(place * BLOCK, BLOCK)
        for lo, hi, factor in ((0, DT, LOG2E / math.sqrt(DT)), (DT, DT + DS, LOG2E / math.sqrt(DS))):
            high, low = split(ref[:, lo:hi] * factor)
            rh[pl.ds(start, BLOCK), lo:hi] = high
            rl[pl.ds(start, BLOCK), lo:hi] = low
    kh[...], kl[...] = split(near[...])
    t_top, s_top = scores(kh, kl, rh, rl, slice(0, SET), (t_out, s_out))
    top[0], top[1] = t_top, s_top
    kth[...] = transposed(kh[...])
    ktl[...] = transposed(kl[...])


def second_kernel(rh, rl, far, down, up, t_near, s_near, top, t_out, s_out, kth, ktl, stats, kh, kl):
    t_top, s_top = top[0], top[1]
    for i, ref in enumerate((far, down, up)):
        keys = slice(SET * i, SET * i + SET)
        kh[keys, :], kl[keys, :] = split(ref[...])
        here = scores(kh, kl, rh, rl, keys, (t_out, s_out))
        t_top = jnp.maximum(t_top, here[0])
        s_top = jnp.maximum(s_top, here[1])
    kth[...] = transposed(kh[...])
    ktl[...] = transposed(kl[...])
    t_top = jnp.max(t_top, axis=0, keepdims=True)
    s_top = jnp.max(s_top, axis=0, keepdims=True)

    def step(t_ref, s_ref, i, sums):
        t_sum, cross, s_sum = sums
        start = pl.multiple_of(i * SHARE, SHARE)
        t = t_ref[pl.ds(start, SHARE), :]
        s = s_ref[pl.ds(start, SHARE), :]
        te = jnp.exp2(t - t_top)
        se = jnp.exp2(s - s_top)
        t_sum = t_sum + jnp.sum(te.reshape(6, 8, ROWS), axis=0)
        cross = cross + jnp.sum((te * (t - s)).reshape(6, 8, ROWS), axis=0)
        s_sum = s_sum + jnp.sum(se.reshape(6, 8, ROWS), axis=0)
        return t_sum, cross, s_sum

    sums = (jnp.zeros((8, ROWS), F32),) * 3
    sums = lax.fori_loop(0, 4, functools.partial(step, t_near, s_near), sums)
    sums = lax.fori_loop(0, 12, functools.partial(step, t_out, s_out), sums)
    t_sum, cross, s_sum = (jnp.sum(v, axis=0, keepdims=True) for v in sums)
    values = (
        t_top + jnp.log(t_sum) * LOG2E,
        s_top + jnp.log(s_sum) * LOG2E,
        cross / t_sum,
    )
    pad = jnp.zeros((2, 128), F32)
    packed = []
    for v in values:
        packed += [v[:, 128 * j : 128 * j + 128] for j in range(6)] + [pad]
    packed = jnp.concatenate(packed, axis=0)
    for d in range(16):
        stats[d] = packed


def combine_kernel(everyone, lse, message):
    t = everyone[:, 0:8, :]
    s = everyone[:, 8:16, :]
    ratio = everyone[:, 16:24, :]
    t_top = jnp.max(t, axis=0)
    s_top = jnp.max(s, axis=0)
    t_weight = jnp.exp2(t - t_top)
    t_sum = jnp.sum(t_weight, axis=0)
    s_sum = jnp.sum(jnp.exp2(s - s_top), axis=0)
    t_lse = t_top + jnp.log(t_sum) * LOG2E
    s_lse = s_top + jnp.log(s_sum) * LOG2E
    divergence = jnp.sum(t_weight * ratio, axis=0) / t_sum - t_lse + s_lse
    divergence = jnp.sum(divergence[0:6, :])

    def as_row(v):
        return jnp.concatenate([v[j : j + 1, :] for j in range(6)], axis=1)

    both = jnp.concatenate(
        [as_row(t_lse), as_row(s_lse), jnp.zeros((6, ROWS), F32)], axis=0
    )
    lse[...] = both
    mine = lax.axis_index("xl") * BLOCK + sub_index() * SHARE
    turned = pltpu.roll(both, lax.rem(ROWS - mine, ROWS), axis=1)[:, :128]
    line = lax.broadcasted_iota(jnp.int32, (8, 128), 0)
    turned = jnp.where(line == 2, divergence, turned)
    for d in range(16):
        message[d] = turned


def mixed_kernel(t_near, s_near, t_rest, s_rest, lse, planes, kth0, ktl0, kth1, ktl1, partial, square, mh, ml):
    zl = lax.axis_index("zl")
    columns = []
    for i in range(2):
        square[...] = jnp.zeros_like(square)
        for q in range(16):
            plane = 4 * (q % 4) + lax.rem(zl + OFFSETS[q // 4], 4)
            square[q : q + 1, :] = planes[plane, i : i + 1, :]
        columns.append(square[...].T)
    t_row = lse[0:1, :]
    s_row = lse[1:2, :]
    for q in range(16):
        part = slice(SHARE * q, SHARE * q + SHARE)
        t_ref, s_ref, base = (t_near, s_near, 0) if q < 4 else (t_rest, s_rest, SET)
        t = t_ref[SHARE * q - base : SHARE * q - base + SHARE, :]
        s = s_ref[SHARE * q - base : SHARE * q - base + SHARE, :]
        t_key = columns[0][0:SHARE, q : q + 1]
        s_key = columns[1][0:SHARE, q : q + 1]
        mixed = (jnp.exp2(s - s_row) - jnp.exp2(t - t_row)) + (
            jnp.exp2(s - s_key) - jnp.exp2(t - t_key)
        )
        high, low = split(mixed)
        mh[part, :] = high
        ml[part, :] = low

    def contract(a, b):
        return lax.dot_general(a, b, (((1,), (0,)), ((), ())), preferred_element_type=F32)

    kth = jnp.concatenate([kth0[...], kth1[...]], axis=1)
    ktl = jnp.concatenate([ktl0[...], ktl1[...]], axis=1)
    grad = contract(kth, mh[...]) + contract(kth, ml[...]) + contract(ktl, mh[...])
    partial[...] = grad.T


def total_kernel(parts, planes, blocks):
    total = jnp.sum(parts[...], axis=0) * (1.0 / math.sqrt(DS))
    divergence = jnp.sum(planes[:, 2, :], axis=0, keepdims=True)
    for d in range(16):
        blocks[d, 0:SHARE, :] = total
        blocks[d, SHARE:, :] = jnp.broadcast_to(divergence, (8, 128))


def finish_kernel(factor, blocks, grad, loss, tails, sems):
    body = pltpu.make_async_copy(blocks.at[:, 0:SHARE], grad, sems.at[0])
    body.start()
    ends = [
        pltpu.make_async_copy(blocks.at[8 * c, SHARE:], tails.at[c], sems.at[1 + c])
        for c in range(2)
    ]
    for end in ends:
        end.start()
    for end in ends:
        end.wait()
    loss[0, 0] = jnp.max(tails[0] + tails[1]) * factor
    body.wait()


def shards(teacher_q, student_q):
    own, shard = pl.pallas_call(
        select_kernel,
        out_shape=(shape(BLOCK, DT + DS), shape(SHARE, DT + DS)),
        in_specs=[pl.BlockSpec(memory_space=pl.ANY)] * 2,
        out_specs=[pl.BlockSpec(memory_space=pl.ANY)] * 2,
        scratch_shapes=[pltpu.SemaphoreType.DMA((4,))],
    )(teacher_q, student_q)
    other = permute(own, lambda xh, y, c, xl, z: (xh, y, c, 1 - xl, z))
    near = lax.all_gather(shard, "zh", tiled=True)
    far = from_plane(near, 2, -2)
    up = from_plane(near, 1, 1)
    down = from_plane(near, -1, -1)
    rh, rl, t_near, s_near, top, kth0, ktl0 = call(
        first_kernel,
        (
            shape(ROWS, DT + DS, dtype=BF16),
            shape(ROWS, DT + DS, dtype=BF16),
            shape(SET, ROWS),
            shape(SET, ROWS),
            shape(2, 8, ROWS),
            shape(DS, SET, dtype=BF16),
            shape(DS, SET, dtype=BF16),
        ),
        (own, other, near),
        [pltpu.VMEM((SET, DT + DS), BF16)] * 2,
    )
    t_rest, s_rest, kth1, ktl1, stats = call(
        second_kernel,
        (
            shape(ROWS - SET, ROWS),
            shape(ROWS - SET, ROWS),
            shape(DS, ROWS - SET, dtype=BF16),
            shape(DS, ROWS - SET, dtype=BF16),
            shape(16, 24, 128),
        ),
        (rh, rl, far, down, up, t_near, s_near, top),
        [pltpu.VMEM((ROWS - SET, DT + DS), BF16)] * 2,
    )
    everyone = lax.all_to_all(stats, PLANE, 0, 0, tiled=True)
    lse, message = call(
        combine_kernel, (shape(8, ROWS), shape(16, 8, 128)), (everyone,)
    )
    planes = lax.all_to_all(message, LINE, 0, 0, tiled=True)
    partial = call(
        mixed_kernel,
        shape(ROWS, DS),
        (t_near, s_near, t_rest, s_rest, lse, planes, kth0, ktl0, kth1, ktl1),
        [
            pltpu.VMEM((128, 128), F32),
            pltpu.VMEM((ROWS, ROWS), BF16),
            pltpu.VMEM((ROWS, ROWS), BF16),
        ],
    )
    parts = lax.all_to_all(partial.reshape(16, SHARE, DS), PLANE, 0, 0, tiled=True)
    blocks = call(total_kernel, shape(16, SHARE + 8, DS), (parts, planes))
    blocks = lax.all_to_all(blocks, COPIES, 0, 0, tiled=True)
    factor = 1.0 / (LOG2E * 2 * BLOCK * 32)

    grad, loss = pl.pallas_call(
        functools.partial(finish_kernel, factor),
        out_shape=(shape(16, SHARE, DS), shape(1, 1)),
        in_specs=[pl.BlockSpec(memory_space=pl.ANY)],
        out_specs=(pl.BlockSpec(memory_space=pl.ANY), pl.BlockSpec(memory_space=pltpu.SMEM)),
        scratch_shapes=[pltpu.VMEM((2, 8, 128), F32), pltpu.SemaphoreType.DMA((3,))],
        compiler_params=pltpu.CompilerParams(vmem_limit_bytes=1 << 20),
    )(blocks)
    return (grad.reshape(2, BLOCK, DS), loss.reshape(()))


def solution(mesh):
    fine = Mesh(mesh.devices.reshape(SIZES), AXES)
    tokens = P(None, ("xl", "zh", "zl"), None)
    return jax.shard_map(
        shards, mesh=fine, in_specs=(tokens, tokens), out_specs=(tokens, P()), check_vma=False
    )
```

```python
import functools
import math

import jax
import jax.numpy as jnp
from jax import lax
from jax.experimental import pallas as pl
from jax.experimental.pallas import tpu as pltpu
from jax.sharding import Mesh, PartitionSpec as P

DT = 256
DS = 128
AXES = ("xh", "y", "c", "xl", "zh", "zl")
SIZES = (2, 4, 2, 2, 4, 4)
PLANE = ("xl", "c", "y")
COPIES = ("xh", "c", "y")
LINE = ("zh", "zl")
BLOCK = 384
SHARE = 48
ROWS = 768
SET = 192
OFFSETS = (0, 2, 3, 1)
LOG2E = math.log2(math.e)


F32 = jnp.float32
BF16 = jnp.bfloat16


def shape(*dims, dtype=F32):
    return jax.ShapeDtypeStruct(dims, dtype)


def call(body, outs, ins, scratch=()):
    return pl.pallas_call(
        body,
        out_shape=outs,
        in_specs=[pl.BlockSpec(memory_space=pltpu.VMEM)] * len(ins),
        scratch_shapes=scratch,
        compiler_params=pltpu.CompilerParams(vmem_limit_bytes=24 << 20),
    )(*ins)


def permute(x, move):
    pairs = []
    for index in range(512):
        rest, where = index, []
        for size in reversed(SIZES):
            where.append(rest % size)
            rest //= size
        xh, y, c, xl, zh, zl = reversed(where)
        xh, y, c, xl, z = move(xh, y, c, xl, zh * 4 + zl)
        to = ((((xh * 4 + y) * 2 + c) * 2 + xl) * 4 + z // 4) * 4 + z % 4
        pairs.append((index, to))
    return lax.ppermute(x, AXES, pairs)


def from_plane(x, first, second):
    return permute(
        x, lambda xh, y, c, xl, z: (xh, y, c, xl, (z - (second if c else first)) % 16)
    )


def sub_index():
    return lax.axis_index("c") * 4 + lax.axis_index("y")


def split(x):
    high = x.astype(BF16)
    return high, (x - high.astype(F32)).astype(BF16)


def select_kernel(teacher, student, own, shard, sems):
    seq = lax.axis_index("xh")
    mine = pl.ds(pl.multiple_of(sub_index() * SHARE, 8), SHARE)
    copies = (
        pltpu.make_async_copy(teacher.at[seq, mine], shard.at[:, :DT], sems.at[0]),
        pltpu.make_async_copy(student.at[seq, mine], shard.at[:, DT:], sems.at[1]),
        pltpu.make_async_copy(teacher.at[seq], own.at[:, :DT], sems.at[2]),
        pltpu.make_async_copy(student.at[seq], own.at[:, DT:], sems.at[3]),
    )
    for copy in copies:
        copy.start()
    for copy in copies:
        copy.wait()


def product(a, b):
    return lax.dot_general(a, b, (((1,), (1,)), ((), ())), preferred_element_type=F32)


def scores(kh, kl, rh, rl, keys, outs):
    tops = []
    for out, lo, hi in zip(outs, (0, DT), (DT, DT + DS)):
        tile = product(kh[keys, lo:hi], rh[:, lo:hi])
        tile += product(kh[keys, lo:hi], rl[:, lo:hi])
        tile += product(kl[keys, lo:hi], rh[:, lo:hi])
        out[keys, :] = tile
        tops.append(jnp.max(tile.reshape(-1, 8, ROWS), axis=0))
    return tops


def transposed(x):
    return x[:, DT:].astype(F32).T.astype(BF16)


def first_kernel(own, other, near, rh, rl, t_out, s_out, top, kth, ktl, kh, kl):
    xl = lax.axis_index("xl")
    for ref, place in ((own, xl), (other, 1 - xl)):
        start = pl.multiple_of(place * BLOCK, BLOCK)
        for lo, hi, factor in ((0, DT, LOG2E / math.sqrt(DT)), (DT, DT + DS, LOG2E / math.sqrt(DS))):
            high, low = split(ref[:, lo:hi] * factor)
            rh[pl.ds(start, BLOCK), lo:hi] = high
            rl[pl.ds(start, BLOCK), lo:hi] = low
    kh[...], kl[...] = split(near[...])
    t_top, s_top = scores(kh, kl, rh, rl, slice(0, SET), (t_out, s_out))
    top[0], top[1] = t_top, s_top
    kth[...] = transposed(kh[...])
    ktl[...] = transposed(kl[...])


def second_kernel(rh, rl, far, down, up, t_near, s_near, top, t_out, s_out, kth, ktl, stats, kh, kl):
    t_top, s_top = top[0], top[1]
    for i, ref in enumerate((far, down, up)):
        keys = slice(SET * i, SET * i + SET)
        kh[keys, :], kl[keys, :] = split(ref[...])
        here = scores(kh, kl, rh, rl, keys, (t_out, s_out))
        t_top = jnp.maximum(t_top, here[0])
        s_top = jnp.maximum(s_top, here[1])
    kth[...] = transposed(kh[...])
    ktl[...] = transposed(kl[...])
    t_top = jnp.max(t_top, axis=0, keepdims=True)
    s_top = jnp.max(s_top, axis=0, keepdims=True)

    def step(t_ref, s_ref, i, sums):
        t_sum, cross, s_sum = sums
        start = pl.multiple_of(i * SHARE, SHARE)
        t = t_ref[pl.ds(start, SHARE), :]
        s = s_ref[pl.ds(start, SHARE), :]
        te = jnp.exp2(t - t_top)
        se = jnp.exp2(s - s_top)
        t_sum = t_sum + jnp.sum(te.reshape(6, 8, ROWS), axis=0)
        cross = cross + jnp.sum((te * (t - s)).reshape(6, 8, ROWS), axis=0)
        s_sum = s_sum + jnp.sum(se.reshape(6, 8, ROWS), axis=0)
        return t_sum, cross, s_sum

    sums = (jnp.zeros((8, ROWS), F32),) * 3
    sums = lax.fori_loop(0, 4, functools.partial(step, t_near, s_near), sums)
    sums = lax.fori_loop(0, 12, functools.partial(step, t_out, s_out), sums)
    t_sum, cross, s_sum = (jnp.sum(v, axis=0, keepdims=True) for v in sums)
    values = (
        t_top + jnp.log(t_sum) * LOG2E,
        s_top + jnp.log(s_sum) * LOG2E,
        cross / t_sum,
    )
    pad = jnp.zeros((2, 128), F32)
    packed = []
    for v in values:
        packed += [v[:, 128 * j : 128 * j + 128] for j in range(6)] + [pad]
    packed = jnp.concatenate(packed, axis=0)
    for d in range(16):
        stats[d] = packed


def combine_kernel(everyone, lse, message):
    t = everyone[:, 0:8, :]
    s = everyone[:, 8:16, :]
    ratio = everyone[:, 16:24, :]
    t_top = jnp.max(t, axis=0)
    s_top = jnp.max(s, axis=0)
    t_weight = jnp.exp2(t - t_top)
    t_sum = jnp.sum(t_weight, axis=0)
    s_sum = jnp.sum(jnp.exp2(s - s_top), axis=0)
    t_lse = t_top + jnp.log(t_sum) * LOG2E
    s_lse = s_top + jnp.log(s_sum) * LOG2E
    divergence = jnp.sum(t_weight * ratio, axis=0) / t_sum - t_lse + s_lse
    divergence = jnp.sum(divergence[0:6, :])

    def as_row(v):
        return jnp.concatenate([v[j : j + 1, :] for j in range(6)], axis=1)

    both = jnp.concatenate(
        [as_row(t_lse), as_row(s_lse), jnp.zeros((6, ROWS), F32)], axis=0
    )
    lse[...] = both
    mine = lax.axis_index("xl") * BLOCK + sub_index() * SHARE
    turned = pltpu.roll(both, lax.rem(ROWS - mine, ROWS), axis=1)[:, :128]
    line = lax.broadcasted_iota(jnp.int32, (8, 128), 0)
    turned = jnp.where(line == 2, divergence, turned)
    for d in range(16):
        message[d] = turned


def mixed_kernel(t_near, s_near, t_rest, s_rest, lse, planes, kth0, ktl0, kth1, ktl1, partial, square, mh, ml):
    zl = lax.axis_index("zl")
    columns = []
    for i in range(2):
        square[...] = jnp.zeros_like(square)
        for q in range(16):
            plane = 4 * (q % 4) + lax.rem(zl + OFFSETS[q // 4], 4)
            square[q : q + 1, :] = planes[plane, i : i + 1, :]
        columns.append(square[...].T)
    t_row = lse[0:1, :]
    s_row = lse[1:2, :]
    for q in range(16):
        part = slice(SHARE * q, SHARE * q + SHARE)
        t_ref, s_ref, base = (t_near, s_near, 0) if q < 4 else (t_rest, s_rest, SET)
        t = t_ref[SHARE * q - base : SHARE * q - base + SHARE, :]
        s = s_ref[SHARE * q - base : SHARE * q - base + SHARE, :]
        t_key = columns[0][0:SHARE, q : q + 1]
        s_key = columns[1][0:SHARE, q : q + 1]
        mixed = (jnp.exp2(s - s_row) - jnp.exp2(t - t_row)) + (
            jnp.exp2(s - s_key) - jnp.exp2(t - t_key)
        )
        high, low = split(mixed)
        mh[part, :] = high
        ml[part, :] = low

    def contract(a, b):
        return lax.dot_general(a, b, (((1,), (0,)), ((), ())), preferred_element_type=F32)

    kth = jnp.concatenate([kth0[...], kth1[...]], axis=1)
    ktl = jnp.concatenate([ktl0[...], ktl1[...]], axis=1)
    grad = contract(kth, mh[...]) + contract(kth, ml[...]) + contract(ktl, mh[...])
    partial[...] = grad.T


def total_kernel(parts, planes, blocks):
    total = jnp.sum(parts[...], axis=0) * (1.0 / math.sqrt(DS))
    divergence = jnp.sum(planes[:, 2, :], axis=0, keepdims=True)
    for d in range(16):
        blocks[d, 0:SHARE, :] = total
        blocks[d, SHARE:, :] = jnp.broadcast_to(divergence, (8, 128))


def finish_kernel(factor, blocks, grad, loss, tails, sems):
    body = pltpu.make_async_copy(blocks.at[:, 0:SHARE], grad, sems.at[0])
    body.start()
    ends = [
        pltpu.make_async_copy(blocks.at[8 * c, SHARE:], tails.at[c], sems.at[1 + c])
        for c in range(2)
    ]
    for end in ends:
        end.start()
    for end in ends:
        end.wait()
    loss[0, 0] = jnp.max(tails[0] + tails[1]) * factor
    body.wait()


def shards(teacher_q, student_q):
    own, shard = pl.pallas_call(
        select_kernel,
        out_shape=(shape(BLOCK, DT + DS), shape(SHARE, DT + DS)),
        in_specs=[pl.BlockSpec(memory_space=pl.ANY)] * 2,
        out_specs=[pl.BlockSpec(memory_space=pltpu.VMEM)] * 2,
        scratch_shapes=[pltpu.SemaphoreType.DMA((4,))],
    )(teacher_q, student_q)
    other = permute(own, lambda xh, y, c, xl, z: (xh, y, c, 1 - xl, z))
    near = lax.all_gather(shard, "zh", tiled=True)
    far = from_plane(near, 2, -2)
    up = from_plane(near, 1, 1)
    down = from_plane(near, -1, -1)
    rh, rl, t_near, s_near, top, kth0, ktl0 = call(
        first_kernel,
        (
            shape(ROWS, DT + DS, dtype=BF16),
            shape(ROWS, DT + DS, dtype=BF16),
            shape(SET, ROWS),
            shape(SET, ROWS),
            shape(2, 8, ROWS),
            shape(DS, SET, dtype=BF16),
            shape(DS, SET, dtype=BF16),
        ),
        (own, other, near),
        [pltpu.VMEM((SET, DT + DS), BF16)] * 2,
    )
    t_rest, s_rest, kth1, ktl1, stats = call(
        second_kernel,
        (
            shape(ROWS - SET, ROWS),
            shape(ROWS - SET, ROWS),
            shape(DS, ROWS - SET, dtype=BF16),
            shape(DS, ROWS - SET, dtype=BF16),
            shape(16, 24, 128),
        ),
        (rh, rl, far, down, up, t_near, s_near, top),
        [pltpu.VMEM((ROWS - SET, DT + DS), BF16)] * 2,
    )
    everyone = lax.all_to_all(stats, PLANE, 0, 0, tiled=True)
    lse, message = call(
        combine_kernel, (shape(8, ROWS), shape(16, 8, 128)), (everyone,)
    )
    planes = lax.all_to_all(message, LINE, 0, 0, tiled=True)
    partial = call(
        mixed_kernel,
        shape(ROWS, DS),
        (t_near, s_near, t_rest, s_rest, lse, planes, kth0, ktl0, kth1, ktl1),
        [
            pltpu.VMEM((128, 128), F32),
            pltpu.VMEM((ROWS, ROWS), BF16),
            pltpu.VMEM((ROWS, ROWS), BF16),
        ],
    )
    parts = lax.all_to_all(partial.reshape(16, SHARE, DS), PLANE, 0, 0, tiled=True)
    blocks = call(total_kernel, shape(16, SHARE + 8, DS), (parts, planes))
    blocks = lax.all_to_all(blocks, COPIES, 0, 0, tiled=True)
    factor = 1.0 / (LOG2E * 2 * BLOCK * 32)

    grad, loss = pl.pallas_call(
        functools.partial(finish_kernel, factor),
        out_shape=(shape(16, SHARE, DS), shape(1, 1)),
        in_specs=[pl.BlockSpec(memory_space=pl.ANY)],
        out_specs=(pl.BlockSpec(memory_space=pl.ANY), pl.BlockSpec(memory_space=pltpu.SMEM)),
        scratch_shapes=[pltpu.VMEM((2, 8, 128), F32), pltpu.SemaphoreType.DMA((3,))],
        compiler_params=pltpu.CompilerParams(vmem_limit_bytes=1 << 20),
    )(blocks)
    return (grad.reshape(2, BLOCK, DS), loss.reshape(()))


def solution(mesh):
    fine = Mesh(mesh.devices.reshape(SIZES), AXES)
    tokens = P(None, ("xl", "zh", "zl"), None)
    return jax.shard_map(
        shards, mesh=fine, in_specs=(tokens, tokens), out_specs=(tokens, P()), check_vma=False
    )
```

```python
import functools
import math

import jax
import jax.numpy as jnp
from jax import lax
from jax.experimental import pallas as pl
from jax.experimental.pallas import tpu as pltpu
from jax.sharding import Mesh, PartitionSpec as P

DT = 256
DS = 128
AXES = ("xh", "y", "c", "xl", "zh", "zl")
SIZES = (2, 4, 2, 2, 4, 4)
PLANE = ("xl", "c", "y")
COPIES = ("xh", "c", "y")
LINE = ("zh", "zl")
BLOCK = 384
SHARE = 48
ROWS = 768
SET = 192
OFFSETS = (0, 2, 3, 1)
LOG2E = math.log2(math.e)


F32 = jnp.float32
BF16 = jnp.bfloat16


def shape(*dims, dtype=F32):
    return jax.ShapeDtypeStruct(dims, dtype)


def call(body, outs, ins, scratch=()):
    return pl.pallas_call(
        body,
        out_shape=outs,
        in_specs=[pl.BlockSpec(memory_space=pltpu.VMEM)] * len(ins),
        scratch_shapes=scratch,
        compiler_params=pltpu.CompilerParams(vmem_limit_bytes=24 << 20),
    )(*ins)


def permute(x, move):
    pairs = []
    for index in range(512):
        rest, where = index, []
        for size in reversed(SIZES):
            where.append(rest % size)
            rest //= size
        xh, y, c, xl, zh, zl = reversed(where)
        xh, y, c, xl, z = move(xh, y, c, xl, zh * 4 + zl)
        to = ((((xh * 4 + y) * 2 + c) * 2 + xl) * 4 + z // 4) * 4 + z % 4
        pairs.append((index, to))
    return lax.ppermute(x, AXES, pairs)


def from_plane(x, first, second):
    return permute(
        x, lambda xh, y, c, xl, z: (xh, y, c, xl, (z - (second if c else first)) % 16)
    )


def sub_index():
    return lax.axis_index("c") * 4 + lax.axis_index("y")


def split(x):
    high = x.astype(BF16)
    return high, (x - high.astype(F32)).astype(BF16)


def select_kernel(teacher, student, own, shard, sems):
    seq = lax.axis_index("xh")
    mine = pl.ds(pl.multiple_of(sub_index() * SHARE, 8), SHARE)
    copies = (
        pltpu.make_async_copy(teacher.at[seq, mine], shard.at[:, :DT], sems.at[0]),
        pltpu.make_async_copy(student.at[seq, mine], shard.at[:, DT:], sems.at[1]),
        pltpu.make_async_copy(teacher.at[seq], own.at[:, :DT], sems.at[2]),
        pltpu.make_async_copy(student.at[seq], own.at[:, DT:], sems.at[3]),
    )
    for copy in copies:
        copy.start()
    for copy in copies:
        copy.wait()


def product(a, b):
    return lax.dot_general(a, b, (((1,), (1,)), ((), ())), preferred_element_type=F32)


def transposed(x):
    return x[:, DT:].astype(F32).T.astype(BF16)


def set_scores(keys, rh, rl, t_out, s_out, kth, ktl):
    kh, kl = split(keys[...])
    kth[...] = transposed(kh)
    ktl[...] = transposed(kl)
    tops = []
    for out, lo, hi in ((t_out, 0, DT), (s_out, DT, DT + DS)):
        tile = product(kh[:, lo:hi], rh[:, lo:hi])
        tile += product(kh[:, lo:hi], rl[:, lo:hi])
        tile += product(kl[:, lo:hi], rh[:, lo:hi])
        out[...] = tile
        tops.append(jnp.max(tile, axis=0, keepdims=True))
    t_top, s_top = tops
    sums = [jnp.zeros((8, ROWS), F32)] * 3
    for i in range(4):
        part = slice(SHARE * i, SHARE * i + SHARE)
        t = t_out[part, :]
        s = s_out[part, :]
        te = jnp.exp2(t - t_top)
        se = jnp.exp2(s - s_top)
        for j, v in enumerate((te, te * (t - s), se)):
            sums[j] = sums[j] + jnp.sum(v.reshape(6, 8, ROWS), axis=0)
    t_sum, cross, s_sum = (jnp.sum(v, axis=0, keepdims=True) for v in sums)
    return t_top, t_sum, cross, s_top, s_sum


def keep(local, values):
    for i, v in enumerate(values):
        local[i : i + 1, :] = v


def first_kernel(own, other, near, rh, rl, t_out, s_out, kth, ktl, local):
    xl = lax.axis_index("xl")
    for ref, place in ((own, xl), (other, 1 - xl)):
        start = pl.multiple_of(place * BLOCK, BLOCK)
        for lo, hi, factor in ((0, DT, LOG2E / math.sqrt(DT)), (DT, DT + DS, LOG2E / math.sqrt(DS))):
            high, low = split(ref[:, lo:hi] * factor)
            rh[pl.ds(start, BLOCK), lo:hi] = high
            rl[pl.ds(start, BLOCK), lo:hi] = low
    keep(local, set_scores(near, rh, rl, t_out, s_out, kth, ktl))


def next_kernel(keys, rh, rl, t_out, s_out, kth, ktl, local):
    keep(local, set_scores(keys, rh, rl, t_out, s_out, kth, ktl))


def last_kernel(keys, rh, rl, local0, local1, local2, t_out, s_out, kth, ktl, stats):
    here = set_scores(keys, rh, rl, t_out, s_out, kth, ktl)
    sets = [here] + [[ref[i : i + 1, :] for i in range(5)] for ref in (local0, local1, local2)]
    t_top = functools.reduce(jnp.maximum, [v[0] for v in sets])
    s_top = functools.reduce(jnp.maximum, [v[3] for v in sets])
    t_scales = [jnp.exp2(v[0] - t_top) for v in sets]
    s_scales = [jnp.exp2(v[3] - s_top) for v in sets]
    t_sum = sum(v[1] * f for v, f in zip(sets, t_scales))
    cross = sum(v[2] * f for v, f in zip(sets, t_scales))
    s_sum = sum(v[4] * f for v, f in zip(sets, s_scales))
    values = (
        t_top + jnp.log(t_sum) * LOG2E,
        s_top + jnp.log(s_sum) * LOG2E,
        cross / t_sum,
    )
    pad = jnp.zeros((2, 128), F32)
    packed = []
    for v in values:
        packed += [v[:, 128 * j : 128 * j + 128] for j in range(6)] + [pad]
    packed = jnp.concatenate(packed, axis=0)
    for d in range(16):
        stats[d] = packed


def combine_kernel(everyone, lse, message):
    t = everyone[:, 0:8, :]
    s = everyone[:, 8:16, :]
    ratio = everyone[:, 16:24, :]
    t_top = jnp.max(t, axis=0)
    s_top = jnp.max(s, axis=0)
    t_weight = jnp.exp2(t - t_top)
    t_sum = jnp.sum(t_weight, axis=0)
    s_sum = jnp.sum(jnp.exp2(s - s_top), axis=0)
    t_lse = t_top + jnp.log(t_sum) * LOG2E
    s_lse = s_top + jnp.log(s_sum) * LOG2E
    divergence = jnp.sum(t_weight * ratio, axis=0) / t_sum - t_lse + s_lse
    divergence = jnp.sum(divergence[0:6, :])

    def as_row(v):
        return jnp.concatenate([v[j : j + 1, :] for j in range(6)], axis=1)

    both = jnp.concatenate(
        [as_row(t_lse), as_row(s_lse), jnp.zeros((6, ROWS), F32)], axis=0
    )
    lse[...] = both
    mine = lax.axis_index("xl") * BLOCK + sub_index() * SHARE
    turned = pltpu.roll(both, lax.rem(ROWS - mine, ROWS), axis=1)[:, :128]
    line = lax.broadcasted_iota(jnp.int32, (8, 128), 0)
    turned = jnp.where(line == 2, divergence, turned)
    for d in range(16):
        message[d] = turned


def mixed_kernel(*refs):
    sets = [refs[4 * i : 4 * i + 4] for i in range(4)]
    lse, planes, partial, square, mh, ml = refs[16:]
    zl = lax.axis_index("zl")
    columns = []
    for i in range(2):
        square[...] = jnp.zeros_like(square)
        for q in range(16):
            plane = 4 * (q % 4) + lax.rem(zl + OFFSETS[q // 4], 4)
            square[q : q + 1, :] = planes[plane, i : i + 1, :]
        columns.append(square[...].T)
    t_row = lse[0:1, :]
    s_row = lse[1:2, :]
    for q in range(16):
        part = slice(SHARE * q, SHARE * q + SHARE)
        inside = slice(SHARE * (q % 4), SHARE * (q % 4) + SHARE)
        t = sets[q // 4][0][inside, :]
        s = sets[q // 4][1][inside, :]
        t_key = columns[0][0:SHARE, q : q + 1]
        s_key = columns[1][0:SHARE, q : q + 1]
        mixed = (jnp.exp2(s - s_row) - jnp.exp2(t - t_row)) + (
            jnp.exp2(s - s_key) - jnp.exp2(t - t_key)
        )
        high, low = split(mixed)
        mh[part, :] = high
        ml[part, :] = low

    def contract(a, b):
        return lax.dot_general(a, b, (((1,), (0,)), ((), ())), preferred_element_type=F32)

    kth = jnp.concatenate([v[2][...] for v in sets], axis=1)
    ktl = jnp.concatenate([v[3][...] for v in sets], axis=1)
    grad = contract(kth, mh[...]) + contract(kth, ml[...]) + contract(ktl, mh[...])
    partial[...] = grad.T


def total_kernel(parts, planes, blocks):
    total = jnp.sum(parts[...], axis=0) * (1.0 / math.sqrt(DS))
    divergence = jnp.sum(planes[:, 2, :], axis=0, keepdims=True)
    for d in range(16):
        blocks[d, 0:SHARE, :] = total
        blocks[d, SHARE:, :] = jnp.broadcast_to(divergence, (8, 128))


def finish_kernel(factor, blocks, grad, loss, tails, sems):
    body = pltpu.make_async_copy(blocks.at[:, 0:SHARE], grad, sems.at[0])
    body.start()
    ends = [
        pltpu.make_async_copy(blocks.at[8 * c, SHARE:], tails.at[c], sems.at[1 + c])
        for c in range(2)
    ]
    for end in ends:
        end.start()
    for end in ends:
        end.wait()
    loss[0, 0] = jnp.max(tails[0] + tails[1]) * factor
    body.wait()


def shards(teacher_q, student_q):
    own, shard = pl.pallas_call(
        select_kernel,
        out_shape=(shape(BLOCK, DT + DS), shape(SHARE, DT + DS)),
        in_specs=[pl.BlockSpec(memory_space=pl.ANY)] * 2,
        out_specs=[pl.BlockSpec(memory_space=pltpu.VMEM)] * 2,
        scratch_shapes=[pltpu.SemaphoreType.DMA((4,))],
    )(teacher_q, student_q)
    other = permute(own, lambda xh, y, c, xl, z: (xh, y, c, 1 - xl, z))
    near = lax.all_gather(shard, "zh", tiled=True)
    far = from_plane(near, 2, -2)
    up = from_plane(near, 1, 1)
    down = from_plane(near, -1, -1)
    tile = (
        shape(SET, ROWS),
        shape(SET, ROWS),
        shape(DS, SET, dtype=BF16),
        shape(DS, SET, dtype=BF16),
    )
    local = shape(8, ROWS)
    halves = (shape(ROWS, DT + DS, dtype=BF16),) * 2
    rh, rl, *near_set, local0 = call(first_kernel, (*halves, *tile, local), (own, other, near))
    *up_set, local1 = call(next_kernel, (*tile, local), (up, rh, rl))
    *down_set, local2 = call(next_kernel, (*tile, local), (down, rh, rl))
    *far_set, stats = call(
        last_kernel, (*tile, shape(16, 24, 128)), (far, rh, rl, local0, local1, local2)
    )
    everyone = lax.all_to_all(stats, PLANE, 0, 0, tiled=True)
    lse, message = call(
        combine_kernel, (shape(8, ROWS), shape(16, 8, 128)), (everyone,)
    )
    planes = lax.all_to_all(message, LINE, 0, 0, tiled=True)
    partial = call(
        mixed_kernel,
        shape(ROWS, DS),
        (*near_set, *far_set, *down_set, *up_set, lse, planes),
        [
            pltpu.VMEM((128, 128), F32),
            pltpu.VMEM((ROWS, ROWS), BF16),
            pltpu.VMEM((ROWS, ROWS), BF16),
        ],
    )
    parts = lax.all_to_all(partial.reshape(16, SHARE, DS), PLANE, 0, 0, tiled=True)
    blocks = call(total_kernel, shape(16, SHARE + 8, DS), (parts, planes))
    blocks = lax.all_to_all(blocks, COPIES, 0, 0, tiled=True)
    factor = 1.0 / (LOG2E * 2 * BLOCK * 32)

    grad, loss = pl.pallas_call(
        functools.partial(finish_kernel, factor),
        out_shape=(shape(16, SHARE, DS), shape(1, 1)),
        in_specs=[pl.BlockSpec(memory_space=pl.ANY)],
        out_specs=(pl.BlockSpec(memory_space=pl.ANY), pl.BlockSpec(memory_space=pltpu.SMEM)),
        scratch_shapes=[pltpu.VMEM((2, 8, 128), F32), pltpu.SemaphoreType.DMA((3,))],
        compiler_params=pltpu.CompilerParams(vmem_limit_bytes=1 << 20),
    )(blocks)
    return (grad.reshape(2, BLOCK, DS), loss.reshape(()))


def solution(mesh):
    fine = Mesh(mesh.devices.reshape(SIZES), AXES)
    tokens = P(None, ("xl", "zh", "zl"), None)
    return jax.shard_map(
        shards, mesh=fine, in_specs=(tokens, tokens), out_specs=(tokens, P()), check_vma=False
    )
```

```python
import functools
import math

import jax
import jax.numpy as jnp
from jax import lax
from jax.experimental import pallas as pl
from jax.experimental.pallas import tpu as pltpu
from jax.sharding import Mesh, PartitionSpec as P

DT = 256
DS = 128
AXES = ("xh", "y", "c", "xl", "zh", "zl")
SIZES = (2, 4, 2, 2, 4, 4)
PLANE = ("xl", "c", "y")
CHIPS = ("xl", "y")
COPIES = ("xh", "y")
PAIR = 96
LINE = ("zh", "zl")
BLOCK = 384
SHARE = 48
ROWS = 768
SET = 192
OFFSETS = (0, 2, 3, 1)
LOG2E = math.log2(math.e)


F32 = jnp.float32
BF16 = jnp.bfloat16


def shape(*dims, dtype=F32):
    return jax.ShapeDtypeStruct(dims, dtype)


def call(body, outs, ins, scratch=()):
    return pl.pallas_call(
        body,
        out_shape=outs,
        in_specs=[pl.BlockSpec(memory_space=pltpu.VMEM)] * len(ins),
        scratch_shapes=scratch,
        compiler_params=pltpu.CompilerParams(vmem_limit_bytes=24 << 20),
    )(*ins)


def permute(x, move):
    pairs = []
    for index in range(512):
        rest, where = index, []
        for size in reversed(SIZES):
            where.append(rest % size)
            rest //= size
        xh, y, c, xl, zh, zl = reversed(where)
        xh, y, c, xl, z = move(xh, y, c, xl, zh * 4 + zl)
        to = ((((xh * 4 + y) * 2 + c) * 2 + xl) * 4 + z // 4) * 4 + z % 4
        pairs.append((index, to))
    return lax.ppermute(x, AXES, pairs)


def from_plane(x, first, second):
    return permute(
        x, lambda xh, y, c, xl, z: (xh, y, c, xl, (z - (second if c else first)) % 16)
    )


def sub_index():
    return lax.axis_index("y") * 2 + lax.axis_index("c")


def split(x):
    high = x.astype(BF16)
    return high, (x - high.astype(F32)).astype(BF16)


def select_kernel(teacher, student, own, shard, sems):
    seq = lax.axis_index("xh")
    mine = pl.ds(pl.multiple_of(sub_index() * SHARE, 8), SHARE)
    copies = (
        pltpu.make_async_copy(teacher.at[seq, mine], shard.at[:, :DT], sems.at[0]),
        pltpu.make_async_copy(student.at[seq, mine], shard.at[:, DT:], sems.at[1]),
        pltpu.make_async_copy(teacher.at[seq], own.at[:, :DT], sems.at[2]),
        pltpu.make_async_copy(student.at[seq], own.at[:, DT:], sems.at[3]),
    )
    for copy in copies:
        copy.start()
    for copy in copies:
        copy.wait()


def product(a, b):
    return lax.dot_general(a, b, (((1,), (1,)), ((), ())), preferred_element_type=F32)


def transposed(x):
    return x[:, DT:].astype(F32).T.astype(BF16)


def set_scores(keys, rh, rl, t_out, s_out, kth, ktl):
    kh, kl = split(keys[...])
    kth[...] = transposed(kh)
    ktl[...] = transposed(kl)
    tops = []
    for out, lo, hi in ((t_out, 0, DT), (s_out, DT, DT + DS)):
        tile = product(kh[:, lo:hi], rh[:, lo:hi])
        tile += product(kh[:, lo:hi], rl[:, lo:hi])
        tile += product(kl[:, lo:hi], rh[:, lo:hi])
        out[...] = tile
        tops.append(jnp.max(tile, axis=0, keepdims=True))
    t_top, s_top = tops
    sums = [jnp.zeros((8, ROWS), F32)] * 3
    for i in range(4):
        part = slice(SHARE * i, SHARE * i + SHARE)
        t = t_out[part, :]
        s = s_out[part, :]
        te = jnp.exp2(t - t_top)
        se = jnp.exp2(s - s_top)
        for j, v in enumerate((te, te * (t - s), se)):
            sums[j] = sums[j] + jnp.sum(v.reshape(6, 8, ROWS), axis=0)
    t_sum, cross, s_sum = (jnp.sum(v, axis=0, keepdims=True) for v in sums)
    return t_top, t_sum, cross, s_top, s_sum


def keep(local, values):
    for i, v in enumerate(values):
        local[i : i + 1, :] = v


def first_kernel(own, other, near, rh, rl, t_out, s_out, kth, ktl, local):
    xl = lax.axis_index("xl")
    for ref, place in ((own, xl), (other, 1 - xl)):
        start = pl.multiple_of(place * BLOCK, BLOCK)
        for lo, hi, factor in ((0, DT, LOG2E / math.sqrt(DT)), (DT, DT + DS, LOG2E / math.sqrt(DS))):
            high, low = split(ref[:, lo:hi] * factor)
            rh[pl.ds(start, BLOCK), lo:hi] = high
            rl[pl.ds(start, BLOCK), lo:hi] = low
    keep(local, set_scores(near, rh, rl, t_out, s_out, kth, ktl))


def next_kernel(keys, rh, rl, t_out, s_out, kth, ktl, local):
    keep(local, set_scores(keys, rh, rl, t_out, s_out, kth, ktl))


def last_kernel(keys, rh, rl, local0, local1, local2, t_out, s_out, kth, ktl, stats):
    here = set_scores(keys, rh, rl, t_out, s_out, kth, ktl)
    sets = [here] + [[ref[i : i + 1, :] for i in range(5)] for ref in (local0, local1, local2)]
    t_top = functools.reduce(jnp.maximum, [v[0] for v in sets])
    s_top = functools.reduce(jnp.maximum, [v[3] for v in sets])
    t_scales = [jnp.exp2(v[0] - t_top) for v in sets]
    s_scales = [jnp.exp2(v[3] - s_top) for v in sets]
    t_sum = sum(v[1] * f for v, f in zip(sets, t_scales))
    cross = sum(v[2] * f for v, f in zip(sets, t_scales))
    s_sum = sum(v[4] * f for v, f in zip(sets, s_scales))
    values = (
        t_top + jnp.log(t_sum) * LOG2E,
        s_top + jnp.log(s_sum) * LOG2E,
        cross / t_sum,
    )
    pad = jnp.zeros((2, 128), F32)
    packed = []
    for v in values:
        packed += [v[:, 128 * j : 128 * j + 128] for j in range(6)] + [pad]
    packed = jnp.concatenate(packed, axis=0)
    for d in range(16):
        stats[d] = packed


def combine_kernel(everyone, lse, message):
    t = everyone[:, 0:8, :]
    s = everyone[:, 8:16, :]
    ratio = everyone[:, 16:24, :]
    t_top = jnp.max(t, axis=0)
    s_top = jnp.max(s, axis=0)
    t_weight = jnp.exp2(t - t_top)
    t_sum = jnp.sum(t_weight, axis=0)
    s_sum = jnp.sum(jnp.exp2(s - s_top), axis=0)
    t_lse = t_top + jnp.log(t_sum) * LOG2E
    s_lse = s_top + jnp.log(s_sum) * LOG2E
    divergence = jnp.sum(t_weight * ratio, axis=0) / t_sum - t_lse + s_lse
    divergence = jnp.sum(divergence[0:6, :])

    def as_row(v):
        return jnp.concatenate([v[j : j + 1, :] for j in range(6)], axis=1)

    both = jnp.concatenate(
        [as_row(t_lse), as_row(s_lse), jnp.zeros((6, ROWS), F32)], axis=0
    )
    lse[...] = both
    mine = lax.axis_index("xl") * BLOCK + sub_index() * SHARE
    turned = pltpu.roll(both, lax.rem(ROWS - mine, ROWS), axis=1)[:, :128]
    line = lax.broadcasted_iota(jnp.int32, (8, 128), 0)
    turned = jnp.where(line == 2, divergence, turned)
    for d in range(16):
        message[d] = turned


def mixed_kernel(*refs):
    sets = [refs[4 * i : 4 * i + 4] for i in range(4)]
    lse, planes, partial, square, mh, ml = refs[16:]
    zl = lax.axis_index("zl")
    columns = []
    for i in range(2):
        square[...] = jnp.zeros_like(square)
        for q in range(16):
            plane = 4 * (q % 4) + lax.rem(zl + OFFSETS[q // 4], 4)
            square[q : q + 1, :] = planes[plane, i : i + 1, :]
        columns.append(square[...].T)
    t_row = lse[0:1, :]
    s_row = lse[1:2, :]
    for q in range(16):
        part = slice(SHARE * q, SHARE * q + SHARE)
        inside = slice(SHARE * (q % 4), SHARE * (q % 4) + SHARE)
        t = sets[q // 4][0][inside, :]
        s = sets[q // 4][1][inside, :]
        t_key = columns[0][0:SHARE, q : q + 1]
        s_key = columns[1][0:SHARE, q : q + 1]
        mixed = (jnp.exp2(s - s_row) - jnp.exp2(t - t_row)) + (
            jnp.exp2(s - s_key) - jnp.exp2(t - t_key)
        )
        high, low = split(mixed)
        mh[part, :] = high
        ml[part, :] = low

    def contract(a, b):
        return lax.dot_general(a, b, (((1,), (0,)), ((), ())), preferred_element_type=F32)

    kth = jnp.concatenate([v[2][...] for v in sets], axis=1)
    ktl = jnp.concatenate([v[3][...] for v in sets], axis=1)
    grad = contract(kth, mh[...]) + contract(kth, ml[...]) + contract(ktl, mh[...])
    partial[...] = grad.T


def total_kernel(parts, planes, blocks):
    total = jnp.sum(parts[...], axis=0) * (1.0 / math.sqrt(DS))
    divergence = jnp.sum(planes[:, 2, :], axis=0, keepdims=True)
    for d in range(8):
        blocks[d, 0:PAIR, :] = total
        blocks[d, PAIR:, :] = jnp.broadcast_to(divergence, (8, 128))


def finish_kernel(factor, mine, partner, grad, loss):
    grad[...] = mine[:, 0:PAIR, :] + partner[:, 0:PAIR, :]
    loss[0, 0] = jnp.max(mine[0, PAIR:, :] + mine[4, PAIR:, :]) * factor


def shards(teacher_q, student_q):
    own, shard = pl.pallas_call(
        select_kernel,
        out_shape=(shape(BLOCK, DT + DS), shape(SHARE, DT + DS)),
        in_specs=[pl.BlockSpec(memory_space=pltpu.HBM)] * 2,
        out_specs=[pl.BlockSpec(memory_space=pl.ANY)] * 2,
        scratch_shapes=[pltpu.SemaphoreType.DMA((4,))],
        compiler_params=pltpu.CompilerParams(vmem_limit_bytes=1 << 20),
    )(
        pltpu.with_memory_space_constraint(teacher_q, pltpu.HBM),
        pltpu.with_memory_space_constraint(student_q, pltpu.HBM),
    )
    other = permute(own, lambda xh, y, c, xl, z: (xh, y, c, 1 - xl, z))
    near = lax.all_gather(shard, "zh", tiled=True)
    far = from_plane(near, 2, -2)
    up = from_plane(near, 1, 1)
    down = from_plane(near, -1, -1)
    tile = (
        shape(SET, ROWS),
        shape(SET, ROWS),
        shape(DS, SET, dtype=BF16),
        shape(DS, SET, dtype=BF16),
    )
    local = shape(8, ROWS)
    halves = (shape(ROWS, DT + DS, dtype=BF16),) * 2
    rh, rl, *near_set, local0 = call(first_kernel, (*halves, *tile, local), (own, other, near))
    *up_set, local1 = call(next_kernel, (*tile, local), (up, rh, rl))
    *down_set, local2 = call(next_kernel, (*tile, local), (down, rh, rl))
    *far_set, stats = call(
        last_kernel, (*tile, shape(16, 24, 128)), (far, rh, rl, local0, local1, local2)
    )
    everyone = lax.all_to_all(stats, PLANE, 0, 0, tiled=True)
    lse, message = call(
        combine_kernel, (shape(8, ROWS), shape(16, 8, 128)), (everyone,)
    )
    planes = lax.all_to_all(message, LINE, 0, 0, tiled=True)
    partial = call(
        mixed_kernel,
        shape(ROWS, DS),
        (*near_set, *far_set, *down_set, *up_set, lse, planes),
        [
            pltpu.VMEM((128, 128), F32),
            pltpu.VMEM((ROWS, ROWS), BF16),
            pltpu.VMEM((ROWS, ROWS), BF16),
        ],
    )
    parts = lax.all_to_all(partial.reshape(8, PAIR, DS), CHIPS, 0, 0, tiled=True)
    blocks = call(total_kernel, shape(8, PAIR + 8, DS), (parts, planes))
    mine = lax.all_to_all(blocks, COPIES, 0, 0, tiled=True)
    partner = permute(mine, lambda xh, y, c, xl, z: (xh, y, 1 - c, xl, z))
    factor = 1.0 / (LOG2E * 2 * BLOCK * 32)
    grad, loss = pl.pallas_call(
        functools.partial(finish_kernel, factor),
        out_shape=(shape(8, PAIR, DS), shape(1, 1)),
        in_specs=[pl.BlockSpec(memory_space=pltpu.VMEM)] * 2,
        out_specs=(pl.BlockSpec(memory_space=pltpu.VMEM), pl.BlockSpec(memory_space=pltpu.SMEM)),
        compiler_params=pltpu.CompilerParams(vmem_limit_bytes=8 << 20),
    )(mine, partner)
    return (grad.reshape(2, BLOCK, DS), loss.reshape(()))


def solution(mesh):
    fine = Mesh(mesh.devices.reshape(SIZES), AXES)
    tokens = P(None, ("xl", "zh", "zl"), None)
    return jax.shard_map(
        shards, mesh=fine, in_specs=(tokens, tokens), out_specs=(tokens, P()), check_vma=False
    )
```

```python
import functools
import math

import jax
import jax.numpy as jnp
from jax import lax
from jax.experimental import pallas as pl
from jax.experimental.pallas import tpu as pltpu
from jax.sharding import Mesh, PartitionSpec as P

DT = 256
DS = 128
AXES = ("xh", "y", "c", "xl", "zh", "zl")
SIZES = (2, 4, 2, 2, 4, 4)
PLANE = ("xl", "c", "y")
CHIPS = ("xl", "y")
COPIES = ("xh", "y")
PAIR = 96
LINE = ("zh", "zl")
BLOCK = 384
SHARE = 48
ROWS = 768
SET = 192
OFFSETS = (0, 2, 3, 1)
LOG2E = math.log2(math.e)


F32 = jnp.float32
BF16 = jnp.bfloat16


def shape(*dims, dtype=F32):
    return jax.ShapeDtypeStruct(dims, dtype)


def call(body, outs, ins, scratch=()):
    return pl.pallas_call(
        body,
        out_shape=outs,
        in_specs=[pl.BlockSpec(memory_space=pltpu.VMEM)] * len(ins),
        scratch_shapes=scratch,
        compiler_params=pltpu.CompilerParams(vmem_limit_bytes=28 << 20),
    )(*ins)


def permute(x, move):
    pairs = []
    for index in range(512):
        rest, where = index, []
        for size in reversed(SIZES):
            where.append(rest % size)
            rest //= size
        xh, y, c, xl, zh, zl = reversed(where)
        xh, y, c, xl, z = move(xh, y, c, xl, zh * 4 + zl)
        to = ((((xh * 4 + y) * 2 + c) * 2 + xl) * 4 + z // 4) * 4 + z % 4
        pairs.append((index, to))
    return lax.ppermute(x, AXES, pairs)


def from_plane(x, first, second):
    return permute(
        x, lambda xh, y, c, xl, z: (xh, y, c, xl, (z - (second if c else first)) % 16)
    )


def sub_index():
    return lax.axis_index("y") * 2 + lax.axis_index("c")


def split(x):
    high = x.astype(BF16)
    return high, (x - high.astype(F32)).astype(BF16)


def select_kernel(teacher, student, own, shard, sems):
    seq = lax.axis_index("xh")
    mine = pl.ds(pl.multiple_of(sub_index() * SHARE, 8), SHARE)
    copies = (
        pltpu.make_async_copy(teacher.at[seq, mine], shard.at[:, :DT], sems.at[0]),
        pltpu.make_async_copy(student.at[seq, mine], shard.at[:, DT:], sems.at[1]),
        pltpu.make_async_copy(teacher.at[seq], own.at[:, :DT], sems.at[2]),
        pltpu.make_async_copy(student.at[seq], own.at[:, DT:], sems.at[3]),
    )
    for copy in copies:
        copy.start()
    for copy in copies:
        copy.wait()


def product(a, b):
    return lax.dot_general(a, b, (((1,), (1,)), ((), ())), preferred_element_type=F32)


def transposed(x):
    return x[:, DT:].astype(F32).T.astype(BF16)


def set_scores(keys, rh, rl, t_out, s_out, te_out, se_out, kt):
    kh, kl = split(keys[...])
    kt[0:DS, :] = transposed(kh)
    kt[DS:, :] = transposed(kl)
    both = jnp.concatenate([kh, kl], axis=0)
    tops = []
    for out, lo, hi in ((t_out, 0, DT), (s_out, DT, DT + DS)):
        tile = product(both[:, lo:hi], rh[:, lo:hi])
        tile = tile[:SET, :] + tile[SET:, :] + product(kh[:, lo:hi], rl[:, lo:hi])
        out[...] = tile
        tops.append(jnp.max(tile, axis=0, keepdims=True))
    t_top, s_top = tops
    sums = [jnp.zeros((8, ROWS), F32)] * 3
    for i in range(4):
        part = slice(SHARE * i, SHARE * i + SHARE)
        t = t_out[part, :]
        s = s_out[part, :]
        te = jnp.exp2(t - t_top)
        se = jnp.exp2(s - s_top)
        te_out[part, :] = te
        se_out[part, :] = se
        for j, v in enumerate((te, te * (t - s), se)):
            sums[j] = sums[j] + jnp.sum(v.reshape(6, 8, ROWS), axis=0)
    t_sum, cross, s_sum = (jnp.sum(v, axis=0, keepdims=True) for v in sums)
    return t_top, t_sum, cross, s_top, s_sum


def keep(local, values):
    for i, v in enumerate(values):
        local[i : i + 1, :] = v


def first_kernel(own, other, near, rh, rl, t_out, s_out, te_out, se_out, kt, local):
    xl = lax.axis_index("xl")
    for ref, place in ((own, xl), (other, 1 - xl)):
        start = pl.multiple_of(place * BLOCK, BLOCK)
        for lo, hi, factor in ((0, DT, LOG2E / math.sqrt(DT)), (DT, DT + DS, LOG2E / math.sqrt(DS))):
            high, low = split(ref[:, lo:hi] * factor)
            rh[pl.ds(start, BLOCK), lo:hi] = high
            rl[pl.ds(start, BLOCK), lo:hi] = low
    keep(local, set_scores(near, rh, rl, t_out, s_out, te_out, se_out, kt))


def next_kernel(keys, rh, rl, t_out, s_out, te_out, se_out, kt, local):
    keep(local, set_scores(keys, rh, rl, t_out, s_out, te_out, se_out, kt))


def last_kernel(keys, rh, rl, local0, local1, local2, t_out, s_out, te_out, se_out, kt, local, stats):
    here = set_scores(keys, rh, rl, t_out, s_out, te_out, se_out, kt)
    keep(local, here)
    sets = [here] + [[ref[i : i + 1, :] for i in range(5)] for ref in (local0, local1, local2)]
    t_top = functools.reduce(jnp.maximum, [v[0] for v in sets])
    s_top = functools.reduce(jnp.maximum, [v[3] for v in sets])
    t_scales = [jnp.exp2(v[0] - t_top) for v in sets]
    s_scales = [jnp.exp2(v[3] - s_top) for v in sets]
    t_sum = sum(v[1] * f for v, f in zip(sets, t_scales))
    cross = sum(v[2] * f for v, f in zip(sets, t_scales))
    s_sum = sum(v[4] * f for v, f in zip(sets, s_scales))
    values = (
        t_top + jnp.log(t_sum) * LOG2E,
        s_top + jnp.log(s_sum) * LOG2E,
        cross / t_sum,
    )
    pad = jnp.zeros((2, 128), F32)
    packed = []
    for v in values:
        packed += [v[:, 128 * j : 128 * j + 128] for j in range(6)] + [pad]
    packed = jnp.concatenate(packed, axis=0)
    for d in range(16):
        stats[d] = packed


def combine_kernel(everyone, lse, message):
    t = everyone[:, 0:8, :]
    s = everyone[:, 8:16, :]
    ratio = everyone[:, 16:24, :]
    t_top = jnp.max(t, axis=0)
    s_top = jnp.max(s, axis=0)
    t_weight = jnp.exp2(t - t_top)
    t_sum = jnp.sum(t_weight, axis=0)
    s_sum = jnp.sum(jnp.exp2(s - s_top), axis=0)
    t_lse = t_top + jnp.log(t_sum) * LOG2E
    s_lse = s_top + jnp.log(s_sum) * LOG2E
    divergence = jnp.sum(t_weight * ratio, axis=0) / t_sum - t_lse + s_lse
    divergence = jnp.sum(divergence[0:6, :])

    def as_row(v):
        return jnp.concatenate([v[j : j + 1, :] for j in range(6)], axis=1)

    both = jnp.concatenate(
        [as_row(t_lse), as_row(s_lse), jnp.zeros((6, ROWS), F32)], axis=0
    )
    lse[...] = both
    mine = lax.axis_index("xl") * BLOCK + sub_index() * SHARE
    turned = pltpu.roll(both, lax.rem(ROWS - mine, ROWS), axis=1)[:, :128]
    line = lax.broadcasted_iota(jnp.int32, (8, 128), 0)
    turned = jnp.where(line == 2, divergence, turned)
    for d in range(16):
        message[d] = turned


def mixed_kernel(*refs):
    sets = [refs[6 * i : 6 * i + 6] for i in range(4)]
    lse, planes, partial, square, mh, ml = refs[24:]
    zl = lax.axis_index("zl")
    columns = []
    for i in range(2):
        square[...] = jnp.zeros_like(square)
        for q in range(16):
            plane = 4 * (q % 4) + lax.rem(zl + OFFSETS[q // 4], 4)
            square[q : q + 1, :] = planes[plane, i : i + 1, :]
        columns.append(square[...].T)
    t_row = lse[0:1, :]
    s_row = lse[1:2, :]
    for q in range(16):
        part = slice(SHARE * q, SHARE * q + SHARE)
        inside = slice(SHARE * (q % 4), SHARE * (q % 4) + SHARE)
        t_ref, s_ref, te_ref, se_ref, _, local = sets[q // 4]
        if q % 4 == 0:
            t_factor = jnp.exp2(local[0:1, :] - t_row)
            s_factor = jnp.exp2(local[3:4, :] - s_row)
        t_key = columns[0][0:SHARE, q : q + 1]
        s_key = columns[1][0:SHARE, q : q + 1]
        mixed = (se_ref[inside, :] * s_factor - te_ref[inside, :] * t_factor) + (
            jnp.exp2(s_ref[inside, :] - s_key) - jnp.exp2(t_ref[inside, :] - t_key)
        )
        high, low = split(mixed)
        mh[part, :] = high
        ml[part, :] = low

    def contract(a, b):
        return lax.dot_general(a, b, (((1,), (0,)), ((), ())), preferred_element_type=F32)

    kt = jnp.concatenate([v[4][...] for v in sets], axis=1)
    grad = contract(kt, mh[...])
    grad = grad[:DS, :] + grad[DS:, :] + contract(kt[:DS, :], ml[...])
    partial[...] = grad.T


def total_kernel(parts, planes, blocks):
    total = jnp.sum(parts[...], axis=0) * (1.0 / math.sqrt(DS))
    divergence = jnp.sum(planes[:, 2, :], axis=0, keepdims=True)
    for d in range(8):
        blocks[d, 0:PAIR, :] = total
        blocks[d, PAIR:, :] = jnp.broadcast_to(divergence, (8, 128))


def finish_kernel(factor, mine, partner, grad, loss):
    grad[...] = mine[:, 0:PAIR, :] + partner[:, 0:PAIR, :]
    loss[0, 0] = jnp.max(mine[0, PAIR:, :] + mine[4, PAIR:, :]) * factor


def shards(teacher_q, student_q):
    own, shard = pl.pallas_call(
        select_kernel,
        out_shape=(shape(BLOCK, DT + DS), shape(SHARE, DT + DS)),
        in_specs=[pl.BlockSpec(memory_space=pltpu.HBM)] * 2,
        out_specs=[pl.BlockSpec(memory_space=pl.ANY)] * 2,
        scratch_shapes=[pltpu.SemaphoreType.DMA((4,))],
        compiler_params=pltpu.CompilerParams(vmem_limit_bytes=1 << 20),
    )(
        pltpu.with_memory_space_constraint(teacher_q, pltpu.HBM),
        pltpu.with_memory_space_constraint(student_q, pltpu.HBM),
    )
    other = permute(own, lambda xh, y, c, xl, z: (xh, y, c, 1 - xl, z))
    near = lax.all_gather(shard, "zh", tiled=True)
    far = from_plane(near, 2, -2)
    up = from_plane(near, 1, 1)
    down = from_plane(near, -1, -1)
    tile = (*[shape(SET, ROWS)] * 4, shape(2 * DS, SET, dtype=BF16), shape(8, ROWS))
    halves = (shape(ROWS, DT + DS, dtype=BF16),) * 2
    rh, rl, *near_set = call(first_kernel, (*halves, *tile), (own, other, near))
    up_set = call(next_kernel, tile, (up, rh, rl))
    down_set = call(next_kernel, tile, (down, rh, rl))
    *far_set, stats = call(
        last_kernel,
        (*tile, shape(16, 24, 128)),
        (far, rh, rl, near_set[-1], up_set[-1], down_set[-1]),
    )
    everyone = lax.all_to_all(stats, PLANE, 0, 0, tiled=True)
    lse, message = call(
        combine_kernel, (shape(8, ROWS), shape(16, 8, 128)), (everyone,)
    )
    planes = lax.all_to_all(message, LINE, 0, 0, tiled=True)
    partial = call(
        mixed_kernel,
        shape(ROWS, DS),
        (*near_set, *far_set, *down_set, *up_set, lse, planes),
        [
            pltpu.VMEM((128, 128), F32),
            pltpu.VMEM((ROWS, ROWS), BF16),
            pltpu.VMEM((ROWS, ROWS), BF16),
        ],
    )
    parts = lax.all_to_all(partial.reshape(8, PAIR, DS), CHIPS, 0, 0, tiled=True)
    blocks = call(total_kernel, shape(8, PAIR + 8, DS), (parts, planes))
    mine = lax.all_to_all(blocks, COPIES, 0, 0, tiled=True)
    partner = permute(mine, lambda xh, y, c, xl, z: (xh, y, 1 - c, xl, z))
    factor = 1.0 / (LOG2E * 2 * BLOCK * 32)
    grad, loss = pl.pallas_call(
        functools.partial(finish_kernel, factor),
        out_shape=(shape(8, PAIR, DS), shape(1, 1)),
        in_specs=[pl.BlockSpec(memory_space=pltpu.VMEM)] * 2,
        out_specs=(pl.BlockSpec(memory_space=pltpu.VMEM), pl.BlockSpec(memory_space=pltpu.SMEM)),
        compiler_params=pltpu.CompilerParams(vmem_limit_bytes=8 << 20),
    )(mine, partner)
    return (grad.reshape(2, BLOCK, DS), loss.reshape(()))


def solution(mesh):
    fine = Mesh(mesh.devices.reshape(SIZES), AXES)
    tokens = P(None, ("xl", "zh", "zl"), None)
    return jax.shard_map(
        shards, mesh=fine, in_specs=(tokens, tokens), out_specs=(tokens, P()), check_vma=False
    )
```

```python
import functools
import math

import jax
import jax.numpy as jnp
from jax import lax
from jax.experimental import pallas as pl
from jax.experimental.pallas import tpu as pltpu
from jax.sharding import Mesh, PartitionSpec as P

DT = 256
DS = 128
AXES = ("xh", "y", "c", "xl", "zh", "zl")
SIZES = (2, 4, 2, 2, 4, 4)
PLANE = ("xl", "c", "y")
CHIPS = ("xl", "y")
COPIES = ("xh", "y")
PAIR = 96
LINE = ("zh", "zl")
BLOCK = 384
SHARE = 48
ROWS = 768
SET = 192
OFFSETS = (0, 2, 3, 1)
LOG2E = math.log2(math.e)


F32 = jnp.float32
BF16 = jnp.bfloat16


def shape(*dims, dtype=F32):
    return jax.ShapeDtypeStruct(dims, dtype)


def call(body, outs, ins, scratch=()):
    return pl.pallas_call(
        body,
        out_shape=outs,
        in_specs=[pl.BlockSpec(memory_space=pltpu.VMEM)] * len(ins),
        scratch_shapes=scratch,
        compiler_params=pltpu.CompilerParams(vmem_limit_bytes=28 << 20),
    )(*ins)


def permute(x, move):
    pairs = []
    for index in range(512):
        rest, where = index, []
        for size in reversed(SIZES):
            where.append(rest % size)
            rest //= size
        xh, y, c, xl, zh, zl = reversed(where)
        xh, y, c, xl, z = move(xh, y, c, xl, zh * 4 + zl)
        to = ((((xh * 4 + y) * 2 + c) * 2 + xl) * 4 + z // 4) * 4 + z % 4
        pairs.append((index, to))
    return lax.ppermute(x, AXES, pairs)


def from_plane(x, first, second):
    return permute(
        x, lambda xh, y, c, xl, z: (xh, y, c, xl, (z - (second if c else first)) % 16)
    )


def sub_index():
    return lax.axis_index("y") * 2 + lax.axis_index("c")


def split(x):
    high = x.astype(BF16)
    return high, (x - high.astype(F32)).astype(BF16)


def select_kernel(teacher, student, own, shard, sems):
    seq = lax.axis_index("xh")
    mine = pl.ds(pl.multiple_of(sub_index() * SHARE, 8), SHARE)
    copies = (
        pltpu.make_async_copy(teacher.at[seq, mine], shard.at[:, :DT], sems.at[0]),
        pltpu.make_async_copy(student.at[seq, mine], shard.at[:, DT:], sems.at[1]),
        pltpu.make_async_copy(teacher.at[seq], own.at[:, :DT], sems.at[2]),
        pltpu.make_async_copy(student.at[seq], own.at[:, DT:], sems.at[3]),
    )
    for copy in copies:
        copy.start()
    for copy in copies:
        copy.wait()


def product(a, b):
    return lax.dot_general(a, b, (((1,), (1,)), ((), ())), preferred_element_type=F32)


def transposed(x):
    return x[:, DT:].astype(F32).T.astype(BF16)


def set_scores(keys, rh, rl, t_out, s_out, te_out, se_out, kt):
    kh, kl = split(keys[...])
    kt[0:DS, :] = transposed(kh)
    kt[DS:, :] = transposed(kl)
    both = jnp.concatenate([kh, kl], axis=0)
    tops = []
    for out, lo, hi in ((t_out, 0, DT), (s_out, DT, DT + DS)):
        tile = product(both[:, lo:hi], rh[:, lo:hi])
        tile = tile[:SET, :] + tile[SET:, :] + product(kh[:, lo:hi], rl[:, lo:hi])
        out[...] = tile
        tops.append(jnp.max(tile, axis=0, keepdims=True))
    t_top, s_top = tops
    sums = [jnp.zeros((8, ROWS), F32)] * 3
    for i in range(4):
        part = slice(SHARE * i, SHARE * i + SHARE)
        t = t_out[part, :]
        s = s_out[part, :]
        te = jnp.exp2(t - t_top)
        se = jnp.exp2(s - s_top)
        te_out[part, :] = te
        se_out[part, :] = se
        for j, v in enumerate((te, te * (t - s), se)):
            sums[j] = sums[j] + jnp.sum(v.reshape(6, 8, ROWS), axis=0)
    t_sum, cross, s_sum = (jnp.sum(v, axis=0, keepdims=True) for v in sums)
    return t_top, t_sum, cross, s_top, s_sum


def keep(local, values):
    for i, v in enumerate(values):
        local[i : i + 1, :] = v


def first_kernel(own, other, near, rh, rl, t_out, s_out, te_out, se_out, kt, local):
    xl = lax.axis_index("xl")
    for ref, place in ((own, xl), (other, 1 - xl)):
        start = pl.multiple_of(place * BLOCK, BLOCK)
        for lo, hi, factor in ((0, DT, LOG2E / math.sqrt(DT)), (DT, DT + DS, LOG2E / math.sqrt(DS))):
            high, low = split(ref[:, lo:hi] * factor)
            rh[pl.ds(start, BLOCK), lo:hi] = high
            rl[pl.ds(start, BLOCK), lo:hi] = low
    keep(local, set_scores(near, rh, rl, t_out, s_out, te_out, se_out, kt))


def next_kernel(keys, rh, rl, t_out, s_out, te_out, se_out, kt, local):
    keep(local, set_scores(keys, rh, rl, t_out, s_out, te_out, se_out, kt))


def last_kernel(keys, rh, rl, local0, local1, local2, t_out, s_out, te_out, se_out, kt, local, stats):
    here = set_scores(keys, rh, rl, t_out, s_out, te_out, se_out, kt)
    keep(local, here)
    sets = [here] + [[ref[i : i + 1, :] for i in range(5)] for ref in (local0, local1, local2)]
    t_top = functools.reduce(jnp.maximum, [v[0] for v in sets])
    s_top = functools.reduce(jnp.maximum, [v[3] for v in sets])
    t_scales = [jnp.exp2(v[0] - t_top) for v in sets]
    s_scales = [jnp.exp2(v[3] - s_top) for v in sets]
    t_sum = sum(v[1] * f for v, f in zip(sets, t_scales))
    cross = sum(v[2] * f for v, f in zip(sets, t_scales))
    s_sum = sum(v[4] * f for v, f in zip(sets, s_scales))
    values = (
        t_top + jnp.log(t_sum) * LOG2E,
        s_top + jnp.log(s_sum) * LOG2E,
        cross / t_sum,
    )
    pad = jnp.zeros((2, 128), F32)
    packed = []
    for v in values:
        packed += [v[:, 128 * j : 128 * j + 128] for j in range(6)] + [pad]
    packed = jnp.concatenate(packed, axis=0)
    for d in range(16):
        stats[d] = packed


def combine_kernel(everyone, lse, message):
    t = everyone[:, 0:8, :]
    s = everyone[:, 8:16, :]
    ratio = everyone[:, 16:24, :]
    t_top = jnp.max(t, axis=0)
    s_top = jnp.max(s, axis=0)
    t_weight = jnp.exp2(t - t_top)
    t_sum = jnp.sum(t_weight, axis=0)
    s_sum = jnp.sum(jnp.exp2(s - s_top), axis=0)
    t_lse = t_top + jnp.log(t_sum) * LOG2E
    s_lse = s_top + jnp.log(s_sum) * LOG2E
    divergence = jnp.sum(t_weight * ratio, axis=0) / t_sum - t_lse + s_lse
    divergence = jnp.sum(divergence[0:6, :])

    def as_row(v):
        return jnp.concatenate([v[j : j + 1, :] for j in range(6)], axis=1)

    both = jnp.concatenate(
        [as_row(t_lse), as_row(s_lse), jnp.zeros((6, ROWS), F32)], axis=0
    )
    lse[...] = both
    mine = lax.axis_index("xl") * BLOCK + sub_index() * SHARE
    turned = pltpu.roll(both, lax.rem(ROWS - mine, ROWS), axis=1)[:, :128]
    line = lax.broadcasted_iota(jnp.int32, (8, 128), 0)
    turned = jnp.where(line == 2, divergence, turned)
    for d in range(16):
        message[d] = turned


def mixed_kernel(*refs):
    sets = [refs[6 * i : 6 * i + 6] for i in range(4)]
    lse, planes, partial, square, mh, ml = refs[24:]
    zl = lax.axis_index("zl")
    columns = []
    for i in range(2):
        square[...] = jnp.zeros_like(square)
        for q in range(16):
            plane = 4 * (q % 4) + lax.rem(zl + OFFSETS[q // 4], 4)
            square[q : q + 1, :] = planes[plane, i : i + 1, :]
        columns.append(square[...].T)
    t_row = lse[0:1, :]
    s_row = lse[1:2, :]
    for q in range(16):
        part = slice(SHARE * q, SHARE * q + SHARE)
        inside = slice(SHARE * (q % 4), SHARE * (q % 4) + SHARE)
        t_ref, s_ref, te_ref, se_ref, _, local = sets[q // 4]
        if q % 4 == 0:
            t_factor = jnp.exp2(local[0:1, :] - t_row)
            s_factor = jnp.exp2(local[3:4, :] - s_row)
        t_key = columns[0][0:SHARE, q : q + 1]
        s_key = columns[1][0:SHARE, q : q + 1]
        mixed = (se_ref[inside, :] * s_factor - te_ref[inside, :] * t_factor) + (
            jnp.exp2(s_ref[inside, :] - s_key) - jnp.exp2(t_ref[inside, :] - t_key)
        )
        high, low = split(mixed)
        mh[part, :] = high
        ml[part, :] = low

    def contract(a, b):
        return lax.dot_general(a, b, (((1,), (0,)), ((), ())), preferred_element_type=F32)

    kt = jnp.concatenate([v[4][...] for v in sets], axis=1)
    grad = contract(kt, mh[...])
    grad = grad[:DS, :] + grad[DS:, :] + contract(kt[:DS, :], ml[...])
    partial[...] = grad.T


def total_kernel(parts, planes, blocks):
    total = jnp.sum(parts[...], axis=0) * (1.0 / math.sqrt(DS))
    divergence = jnp.sum(planes[:, 2, :], axis=0, keepdims=True)
    for d in range(8):
        blocks[d, 0:PAIR, :] = total
        blocks[d, PAIR:, :] = jnp.broadcast_to(divergence, (8, 128))


def finish_kernel(factor, mine, partner, grad, loss):
    grad[...] = mine[:, 0:PAIR, :] + partner[:, 0:PAIR, :]
    loss[0, 0] = jnp.max(mine[0, PAIR:, :] + mine[4, PAIR:, :]) * factor


def shards(teacher_q, student_q):
    own, shard = pl.pallas_call(
        select_kernel,
        out_shape=(shape(BLOCK, DT + DS), shape(SHARE, DT + DS)),
        in_specs=[pl.BlockSpec(memory_space=pltpu.HBM)] * 2,
        out_specs=[pl.BlockSpec(memory_space=pl.ANY)] * 2,
        scratch_shapes=[pltpu.SemaphoreType.DMA((4,))],
        compiler_params=pltpu.CompilerParams(vmem_limit_bytes=1 << 20),
    )(
        pltpu.with_memory_space_constraint(teacher_q, pltpu.HBM),
        pltpu.with_memory_space_constraint(student_q, pltpu.HBM),
    )
    other = permute(own, lambda xh, y, c, xl, z: (xh, y, c, 1 - xl, z))
    near = lax.all_gather(shard, "zh", tiled=True)
    far = from_plane(near, 2, -2)
    up = from_plane(near, 1, 1)
    down = from_plane(near, -1, -1)
    tile = (*[shape(SET, ROWS)] * 4, shape(2 * DS, SET, dtype=BF16), shape(8, ROWS))
    halves = (shape(ROWS, DT + DS, dtype=BF16),) * 2
    rh, rl, *near_set = call(first_kernel, (*halves, *tile), (own, other, near))
    far_set = call(next_kernel, tile, (far, rh, rl))
    down_set = call(next_kernel, tile, (down, rh, rl))
    *up_set, stats = call(
        last_kernel,
        (*tile, shape(16, 24, 128)),
        (up, rh, rl, near_set[-1], far_set[-1], down_set[-1]),
    )
    everyone = lax.all_to_all(stats, PLANE, 0, 0, tiled=True)
    lse, message = call(
        combine_kernel, (shape(8, ROWS), shape(16, 8, 128)), (everyone,)
    )
    planes = lax.all_to_all(message, LINE, 0, 0, tiled=True)
    partial = call(
        mixed_kernel,
        shape(ROWS, DS),
        (*near_set, *far_set, *down_set, *up_set, lse, planes),
        [
            pltpu.VMEM((128, 128), F32),
            pltpu.VMEM((ROWS, ROWS), BF16),
            pltpu.VMEM((ROWS, ROWS), BF16),
        ],
    )
    parts = lax.all_to_all(partial.reshape(8, PAIR, DS), CHIPS, 0, 0, tiled=True)
    blocks = call(total_kernel, shape(8, PAIR + 8, DS), (parts, planes))
    mine = lax.all_to_all(blocks, COPIES, 0, 0, tiled=True)
    partner = permute(mine, lambda xh, y, c, xl, z: (xh, y, 1 - c, xl, z))
    factor = 1.0 / (LOG2E * 2 * BLOCK * 32)
    grad, loss = pl.pallas_call(
        functools.partial(finish_kernel, factor),
        out_shape=(shape(8, PAIR, DS), shape(1, 1)),
        in_specs=[pl.BlockSpec(memory_space=pltpu.VMEM)] * 2,
        out_specs=(pl.BlockSpec(memory_space=pltpu.VMEM), pl.BlockSpec(memory_space=pltpu.SMEM)),
        compiler_params=pltpu.CompilerParams(vmem_limit_bytes=8 << 20),
    )(mine, partner)
    return (grad.reshape(2, BLOCK, DS), loss.reshape(()))


def solution(mesh):
    fine = Mesh(mesh.devices.reshape(SIZES), AXES)
    tokens = P(None, ("xl", "zh", "zl"), None)
    return jax.shard_map(
        shards, mesh=fine, in_specs=(tokens, tokens), out_specs=(tokens, P()), check_vma=False
    )
```

```python
import functools
import math

import jax
import jax.numpy as jnp
from jax import lax
from jax.experimental import pallas as pl
from jax.experimental.pallas import tpu as pltpu
from jax.sharding import Mesh, PartitionSpec as P

DT = 256
DS = 128
AXES = ("xh", "y", "c", "xl", "zh", "zl")
SIZES = (2, 4, 2, 2, 4, 4)
PLANE = ("xl", "c", "y")
CHIPS = ("xl", "y")
COPIES = ("xh", "y")
PAIR = 96
LINE = ("zh", "zl")
BLOCK = 384
SHARE = 48
ROWS = 768
SET = 192
OFFSETS = (0, 2, 3, 1)
LOG2E = math.log2(math.e)


F32 = jnp.float32
BF16 = jnp.bfloat16


def shape(*dims, dtype=F32):
    return jax.ShapeDtypeStruct(dims, dtype)


def call(body, outs, ins, scratch=()):
    return pl.pallas_call(
        body,
        out_shape=outs,
        in_specs=[pl.BlockSpec(memory_space=pltpu.VMEM)] * len(ins),
        scratch_shapes=scratch,
        compiler_params=pltpu.CompilerParams(vmem_limit_bytes=28 << 20),
    )(*ins)


def permute(x, move):
    pairs = []
    for index in range(512):
        rest, where = index, []
        for size in reversed(SIZES):
            where.append(rest % size)
            rest //= size
        xh, y, c, xl, zh, zl = reversed(where)
        xh, y, c, xl, z = move(xh, y, c, xl, zh * 4 + zl)
        to = ((((xh * 4 + y) * 2 + c) * 2 + xl) * 4 + z // 4) * 4 + z % 4
        pairs.append((index, to))
    return lax.ppermute(x, AXES, pairs)


def from_plane(x, first, second):
    return permute(
        x, lambda xh, y, c, xl, z: (xh, y, c, xl, (z - (second if c else first)) % 16)
    )


def sub_index():
    return lax.axis_index("y") * 2 + lax.axis_index("c")


def split(x):
    high = x.astype(BF16)
    return high, (x - high.astype(F32)).astype(BF16)


def select_kernel(teacher, student, own, shard, sems):
    seq = lax.axis_index("xh")
    mine = pl.ds(pl.multiple_of(sub_index() * SHARE, 8), SHARE)
    copies = (
        pltpu.make_async_copy(teacher.at[seq, mine], shard.at[:, :DT], sems.at[0]),
        pltpu.make_async_copy(student.at[seq, mine], shard.at[:, DT:], sems.at[1]),
        pltpu.make_async_copy(teacher.at[seq], own.at[:, :DT], sems.at[2]),
        pltpu.make_async_copy(student.at[seq], own.at[:, DT:], sems.at[3]),
    )
    for copy in copies:
        copy.start()
    for copy in copies:
        copy.wait()


def product(a, b):
    return lax.dot_general(a, b, (((1,), (1,)), ((), ())), preferred_element_type=F32)


def transposed(x):
    return x[:, DT:].astype(F32).T.astype(BF16)


def set_scores(keys, rh, rl, t_out, s_out, te_out, se_out, kt):
    kh, kl = split(keys[...])
    kt[0:DS, :] = transposed(kh)
    kt[DS:, :] = transposed(kl)
    both = jnp.concatenate([kh, kl], axis=0)
    tops = []
    for out, lo, hi in ((t_out, 0, DT), (s_out, DT, DT + DS)):
        tile = product(both[:, lo:hi], rh[:, lo:hi])
        tile = tile[:SET, :] + tile[SET:, :] + product(kh[:, lo:hi], rl[:, lo:hi])
        out[...] = tile
        tops.append(jnp.max(tile, axis=0, keepdims=True))
    t_top, s_top = tops
    sums = [jnp.zeros((8, ROWS), F32)] * 3
    for i in range(4):
        part = slice(SHARE * i, SHARE * i + SHARE)
        t = t_out[part, :]
        s = s_out[part, :]
        te = jnp.exp2(t - t_top)
        se = jnp.exp2(s - s_top)
        te_out[part, :] = te
        se_out[part, :] = se
        for j, v in enumerate((te, te * (t - s), se)):
            sums[j] = sums[j] + jnp.sum(v.reshape(6, 8, ROWS), axis=0)
    t_sum, cross, s_sum = (jnp.sum(v, axis=0, keepdims=True) for v in sums)
    return t_top, t_sum, cross, s_top, s_sum


def keep(local, values):
    for i, v in enumerate(values):
        local[i : i + 1, :] = v


def first_kernel(own, other, near, rh, rl, t_out, s_out, te_out, se_out, kt, local):
    xl = lax.axis_index("xl")
    for ref, place in ((own, xl), (other, 1 - xl)):
        start = pl.multiple_of(place * BLOCK, BLOCK)
        for lo, hi, factor in ((0, DT, LOG2E / math.sqrt(DT)), (DT, DT + DS, LOG2E / math.sqrt(DS))):
            high, low = split(ref[:, lo:hi] * factor)
            rh[pl.ds(start, BLOCK), lo:hi] = high
            rl[pl.ds(start, BLOCK), lo:hi] = low
    keep(local, set_scores(near, rh, rl, t_out, s_out, te_out, se_out, kt))


def next_kernel(keys, rh, rl, t_out, s_out, te_out, se_out, kt, local):
    keep(local, set_scores(keys, rh, rl, t_out, s_out, te_out, se_out, kt))


def last_kernel(keys, rh, rl, local0, local1, local2, t_out, s_out, te_out, se_out, kt, local, stats):
    here = set_scores(keys, rh, rl, t_out, s_out, te_out, se_out, kt)
    keep(local, here)
    sets = [here] + [[ref[i : i + 1, :] for i in range(5)] for ref in (local0, local1, local2)]
    t_top = functools.reduce(jnp.maximum, [v[0] for v in sets])
    s_top = functools.reduce(jnp.maximum, [v[3] for v in sets])
    t_scales = [jnp.exp2(v[0] - t_top) for v in sets]
    s_scales = [jnp.exp2(v[3] - s_top) for v in sets]
    t_sum = sum(v[1] * f for v, f in zip(sets, t_scales))
    cross = sum(v[2] * f for v, f in zip(sets, t_scales))
    s_sum = sum(v[4] * f for v, f in zip(sets, s_scales))
    values = (
        t_top + jnp.log(t_sum) * LOG2E,
        s_top + jnp.log(s_sum) * LOG2E,
        cross / t_sum,
    )
    pad = jnp.zeros((2, 128), F32)
    packed = []
    for v in values:
        packed += [v[:, 128 * j : 128 * j + 128] for j in range(6)] + [pad]
    packed = jnp.concatenate(packed, axis=0)
    for d in range(16):
        stats[d] = packed


def combine_kernel(everyone, lse, message):
    t = everyone[:, 0:8, :]
    s = everyone[:, 8:16, :]
    ratio = everyone[:, 16:24, :]
    t_top = jnp.max(t, axis=0)
    s_top = jnp.max(s, axis=0)
    t_weight = jnp.exp2(t - t_top)
    t_sum = jnp.sum(t_weight, axis=0)
    s_sum = jnp.sum(jnp.exp2(s - s_top), axis=0)
    t_lse = t_top + jnp.log(t_sum) * LOG2E
    s_lse = s_top + jnp.log(s_sum) * LOG2E
    divergence = jnp.sum(t_weight * ratio, axis=0) / t_sum - t_lse + s_lse
    divergence = jnp.sum(divergence[0:6, :])

    def as_row(v):
        return jnp.concatenate([v[j : j + 1, :] for j in range(6)], axis=1)

    both = jnp.concatenate(
        [as_row(t_lse), as_row(s_lse), jnp.zeros((6, ROWS), F32)], axis=0
    )
    lse[...] = both
    mine = lax.axis_index("xl") * BLOCK + sub_index() * SHARE
    turned = pltpu.roll(both, lax.rem(ROWS - mine, ROWS), axis=1)[:, :128]
    line = lax.broadcasted_iota(jnp.int32, (8, 128), 0)
    turned = jnp.where(line == 2, divergence, turned)
    for d in range(16):
        message[d] = turned


def mixed_kernel(*refs):
    sets = [refs[6 * i : 6 * i + 6] for i in range(4)]
    lse, planes, partial, square, mh, ml = refs[24:]
    zl = lax.axis_index("zl")
    columns = []
    for i in range(2):
        square[...] = jnp.zeros_like(square)
        for q in range(16):
            plane = 4 * (q % 4) + lax.rem(zl + OFFSETS[q // 4], 4)
            square[q : q + 1, :] = planes[plane, i : i + 1, :]
        columns.append(square[...].T)
    t_row = lse[0:1, :]
    s_row = lse[1:2, :]
    for q in range(16):
        part = slice(SHARE * q, SHARE * q + SHARE)
        inside = slice(SHARE * (q % 4), SHARE * (q % 4) + SHARE)
        t_ref, s_ref, te_ref, se_ref, _, local = sets[q // 4]
        if q % 4 == 0:
            t_factor = jnp.exp2(local[0:1, :] - t_row)
            s_factor = jnp.exp2(local[3:4, :] - s_row)
        t_key = columns[0][0:SHARE, q : q + 1]
        s_key = columns[1][0:SHARE, q : q + 1]
        mixed = (se_ref[inside, :] * s_factor - te_ref[inside, :] * t_factor) + (
            jnp.exp2(s_ref[inside, :] - s_key) - jnp.exp2(t_ref[inside, :] - t_key)
        )
        high, low = split(mixed)
        mh[part, :] = high
        ml[part, :] = low

    def contract(a, b):
        return lax.dot_general(a, b, (((1,), (0,)), ((), ())), preferred_element_type=F32)

    kt = jnp.concatenate([v[4][...] for v in sets], axis=1)
    grad = contract(kt, mh[...])
    grad = grad[:DS, :] + grad[DS:, :] + contract(kt[:DS, :], ml[...])
    partial[...] = grad.T


def sum_kernel(parts, total):
    total[...] = jnp.sum(parts[...], axis=0)


def total_kernel(mine, partner, planes, blocks):
    total = (mine[...] + partner[...]) * (1.0 / math.sqrt(DS))
    divergence = jnp.sum(planes[:, 2, :], axis=0, keepdims=True)
    for d in range(8):
        blocks[d, 0:PAIR, :] = total
        blocks[d, PAIR:, :] = jnp.broadcast_to(divergence, (8, 128))


def finish_kernel(factor, blocks, grad, loss):
    grad[...] = blocks[:, 0:PAIR, :]
    loss[0, 0] = jnp.max(blocks[0, PAIR:, :] + blocks[4, PAIR:, :]) * factor


def shards(teacher_q, student_q):
    own, shard = pl.pallas_call(
        select_kernel,
        out_shape=(shape(BLOCK, DT + DS), shape(SHARE, DT + DS)),
        in_specs=[pl.BlockSpec(memory_space=pltpu.HBM)] * 2,
        out_specs=[pl.BlockSpec(memory_space=pl.ANY)] * 2,
        scratch_shapes=[pltpu.SemaphoreType.DMA((4,))],
        compiler_params=pltpu.CompilerParams(vmem_limit_bytes=1 << 20),
    )(
        pltpu.with_memory_space_constraint(teacher_q, pltpu.HBM),
        pltpu.with_memory_space_constraint(student_q, pltpu.HBM),
    )
    other = permute(own, lambda xh, y, c, xl, z: (xh, y, c, 1 - xl, z))
    near = lax.all_gather(shard, "zh", tiled=True)
    far = from_plane(near, 2, -2)
    up = from_plane(near, 1, 1)
    down = from_plane(near, -1, -1)
    tile = (*[shape(SET, ROWS)] * 4, shape(2 * DS, SET, dtype=BF16), shape(8, ROWS))
    halves = (shape(ROWS, DT + DS, dtype=BF16),) * 2
    rh, rl, *near_set = call(first_kernel, (*halves, *tile), (own, other, near))
    up_set = call(next_kernel, tile, (up, rh, rl))
    down_set = call(next_kernel, tile, (down, rh, rl))
    *far_set, stats = call(
        last_kernel,
        (*tile, shape(16, 24, 128)),
        (far, rh, rl, near_set[-1], up_set[-1], down_set[-1]),
    )
    everyone = lax.all_to_all(stats, PLANE, 0, 0, tiled=True)
    lse, message = call(
        combine_kernel, (shape(8, ROWS), shape(16, 8, 128)), (everyone,)
    )
    planes = lax.all_to_all(message, LINE, 0, 0, tiled=True)
    partial = call(
        mixed_kernel,
        shape(ROWS, DS),
        (*near_set, *far_set, *down_set, *up_set, lse, planes),
        [
            pltpu.VMEM((128, 128), F32),
            pltpu.VMEM((ROWS, ROWS), BF16),
            pltpu.VMEM((ROWS, ROWS), BF16),
        ],
    )
    parts = lax.all_to_all(partial.reshape(8, PAIR, DS), CHIPS, 0, 0, tiled=True)
    mine = call(sum_kernel, shape(PAIR, DS), (parts,))
    partner = permute(mine, lambda xh, y, c, xl, z: (xh, y, 1 - c, xl, z))
    blocks = call(total_kernel, shape(8, PAIR + 8, DS), (mine, partner, planes))
    blocks = lax.all_to_all(blocks, COPIES, 0, 0, tiled=True)
    factor = 1.0 / (LOG2E * 2 * BLOCK * 32)
    grad, loss = pl.pallas_call(
        functools.partial(finish_kernel, factor),
        out_shape=(shape(8, PAIR, DS), shape(1, 1)),
        in_specs=[pl.BlockSpec(memory_space=pltpu.VMEM)],
        out_specs=(pl.BlockSpec(memory_space=pltpu.VMEM), pl.BlockSpec(memory_space=pltpu.SMEM)),
        compiler_params=pltpu.CompilerParams(vmem_limit_bytes=8 << 20),
    )(blocks)
    return (grad.reshape(2, BLOCK, DS), loss.reshape(()))


def solution(mesh):
    fine = Mesh(mesh.devices.reshape(SIZES), AXES)
    tokens = P(None, ("xl", "zh", "zl"), None)
    return jax.shard_map(
        shards, mesh=fine, in_specs=(tokens, tokens), out_specs=(tokens, P()), check_vma=False
    )
```

```python
import functools
import math

import jax
import jax.numpy as jnp
from jax import lax
from jax.experimental import pallas as pl
from jax.experimental.pallas import tpu as pltpu
from jax.sharding import Mesh, PartitionSpec as P

DT = 256
DS = 128
AXES = ("xh", "y", "c", "xl", "zh", "zl")
SIZES = (2, 4, 2, 2, 4, 4)
PLANE = ("xl", "c", "y")
CHIPS = ("xl", "y")
COPIES = ("xh", "y")
PAIR = 96
LINE = ("zh", "zl")
BLOCK = 384
SHARE = 48
ROWS = 768
SET = 192
LOG2E = math.log2(math.e)


F32 = jnp.float32
BF16 = jnp.bfloat16


def shape(*dims, dtype=F32):
    return jax.ShapeDtypeStruct(dims, dtype)


def call(body, outs, ins, scratch=()):
    return pl.pallas_call(
        body,
        out_shape=outs,
        in_specs=[pl.BlockSpec(memory_space=pltpu.VMEM)] * len(ins),
        scratch_shapes=scratch,
        compiler_params=pltpu.CompilerParams(vmem_limit_bytes=28 << 20),
    )(*ins)


def permute(x, move):
    pairs = []
    for index in range(512):
        rest, where = index, []
        for size in reversed(SIZES):
            where.append(rest % size)
            rest //= size
        xh, y, c, xl, zh, zl = reversed(where)
        xh, y, c, xl, z = move(xh, y, c, xl, zh * 4 + zl)
        to = ((((xh * 4 + y) * 2 + c) * 2 + xl) * 4 + z // 4) * 4 + z % 4
        pairs.append((index, to))
    return lax.ppermute(x, AXES, pairs)


def from_plane(x, first, second):
    return permute(
        x, lambda xh, y, c, xl, z: (xh, y, c, xl, (z - (second if c else first)) % 16)
    )


def sub_index():
    return lax.axis_index("y") * 2 + lax.axis_index("c")


def split(x):
    high = x.astype(BF16)
    return high, (x - high.astype(F32)).astype(BF16)


def select_kernel(teacher, student, own, shard, sems):
    seq = lax.axis_index("xh")
    mine = pl.ds(pl.multiple_of(sub_index() * SHARE, 8), SHARE)
    copies = (
        pltpu.make_async_copy(teacher.at[seq, mine], shard.at[:, :DT], sems.at[0]),
        pltpu.make_async_copy(student.at[seq, mine], shard.at[:, DT:], sems.at[1]),
        pltpu.make_async_copy(teacher.at[seq], own.at[:, :DT], sems.at[2]),
        pltpu.make_async_copy(student.at[seq], own.at[:, DT:], sems.at[3]),
    )
    for copy in copies:
        copy.start()
    for copy in copies:
        copy.wait()


def product(a, b):
    return lax.dot_general(a, b, (((1,), (1,)), ((), ())), preferred_element_type=F32)


def transposed(x):
    return x[:, DT:].astype(F32).T.astype(BF16)


def set_scores(keys, rh, rl, t_out, s_out, te_out, se_out, kt):
    kh, kl = split(keys[...])
    kt[0:DS, :] = transposed(kh)
    kt[DS:, :] = transposed(kl)
    both = jnp.concatenate([kh, kl], axis=0)
    tops = []
    for out, lo, hi in ((t_out, 0, DT), (s_out, DT, DT + DS)):
        tile = product(both[:, lo:hi], rh[:, lo:hi])
        tile = tile[:SET, :] + tile[SET:, :] + product(kh[:, lo:hi], rl[:, lo:hi])
        out[...] = tile
        tops.append(jnp.max(tile, axis=0, keepdims=True))
    t_top, s_top = tops
    sums = [jnp.zeros((8, ROWS), F32)] * 3
    for i in range(4):
        part = slice(SHARE * i, SHARE * i + SHARE)
        t = t_out[part, :]
        s = s_out[part, :]
        te = jnp.exp2(t - t_top)
        se = jnp.exp2(s - s_top)
        te_out[part, :] = te
        se_out[part, :] = se
        for j, v in enumerate((te, te * (t - s), se)):
            sums[j] = sums[j] + jnp.sum(v.reshape(6, 8, ROWS), axis=0)
    t_sum, cross, s_sum = (jnp.sum(v, axis=0, keepdims=True) for v in sums)
    return t_top, t_sum, cross, s_top, s_sum


def keep(local, values):
    for i, v in enumerate(values):
        local[i : i + 1, :] = v


def first_kernel(own, other, near, rh, rl, t_out, s_out, te_out, se_out, kt, local):
    xl = lax.axis_index("xl")
    for ref, place in ((own, xl), (other, 1 - xl)):
        start = pl.multiple_of(place * BLOCK, BLOCK)
        for lo, hi, factor in ((0, DT, LOG2E / math.sqrt(DT)), (DT, DT + DS, LOG2E / math.sqrt(DS))):
            high, low = split(ref[:, lo:hi] * factor)
            rh[pl.ds(start, BLOCK), lo:hi] = high
            rl[pl.ds(start, BLOCK), lo:hi] = low
    keep(local, set_scores(near, rh, rl, t_out, s_out, te_out, se_out, kt))


def next_kernel(keys, rh, rl, t_out, s_out, te_out, se_out, kt, local):
    keep(local, set_scores(keys, rh, rl, t_out, s_out, te_out, se_out, kt))


def last_kernel(keys, rh, rl, local0, local1, local2, t_out, s_out, te_out, se_out, kt, local, stats):
    here = set_scores(keys, rh, rl, t_out, s_out, te_out, se_out, kt)
    keep(local, here)
    sets = [here] + [[ref[i : i + 1, :] for i in range(5)] for ref in (local0, local1, local2)]
    t_top = functools.reduce(jnp.maximum, [v[0] for v in sets])
    s_top = functools.reduce(jnp.maximum, [v[3] for v in sets])
    t_scales = [jnp.exp2(v[0] - t_top) for v in sets]
    s_scales = [jnp.exp2(v[3] - s_top) for v in sets]
    t_sum = sum(v[1] * f for v, f in zip(sets, t_scales))
    cross = sum(v[2] * f for v, f in zip(sets, t_scales))
    s_sum = sum(v[4] * f for v, f in zip(sets, s_scales))
    values = (
        t_top + jnp.log(t_sum) * LOG2E,
        s_top + jnp.log(s_sum) * LOG2E,
        cross / t_sum,
    )
    pad = jnp.zeros((2, 128), F32)
    packed = []
    for v in values:
        packed += [v[:, 128 * j : 128 * j + 128] for j in range(6)] + [pad]
    packed = jnp.concatenate(packed, axis=0)
    for d in range(16):
        stats[d] = packed


def combine_kernel(everyone, lse, message):
    t = everyone[:, 0:8, :]
    s = everyone[:, 8:16, :]
    ratio = everyone[:, 16:24, :]
    t_top = jnp.max(t, axis=0)
    s_top = jnp.max(s, axis=0)
    t_weight = jnp.exp2(t - t_top)
    t_sum = jnp.sum(t_weight, axis=0)
    s_sum = jnp.sum(jnp.exp2(s - s_top), axis=0)
    t_lse = t_top + jnp.log(t_sum) * LOG2E
    s_lse = s_top + jnp.log(s_sum) * LOG2E
    divergence = jnp.sum(t_weight * ratio, axis=0) / t_sum - t_lse + s_lse
    divergence = jnp.sum(divergence[0:6, :])

    def as_row(v):
        return jnp.concatenate([v[j : j + 1, :] for j in range(6)], axis=1)

    both = jnp.concatenate(
        [as_row(t_lse), as_row(s_lse), jnp.zeros((6, ROWS), F32)], axis=0
    )
    lse[...] = both
    mine = lax.axis_index("xl") * BLOCK + sub_index() * SHARE
    turned = pltpu.roll(both, lax.rem(ROWS - mine, ROWS), axis=1)[:, :128]
    line = lax.broadcasted_iota(jnp.int32, (8, 128), 0)
    turned = jnp.where(line == 2, divergence, turned)
    for d in range(16):
        message[d] = turned


def mixed_kernel(*refs):
    sets = [refs[6 * i : 6 * i + 6] for i in range(4)]
    lse, planes, partial, square, mh, ml = refs[24:]
    zl = lax.axis_index("zl")
    turn = 2 * lax.axis_index("c")
    offsets = (0, 2, 3 + turn, 1 + turn)
    columns = []
    for i in range(2):
        square[...] = jnp.zeros_like(square)
        for q in range(16):
            plane = 4 * (q % 4) + lax.rem(zl + offsets[q // 4], 4)
            square[q : q + 1, :] = planes[plane, i : i + 1, :]
        columns.append(square[...].T)
    t_row = lse[0:1, :]
    s_row = lse[1:2, :]
    for q in range(16):
        part = slice(SHARE * q, SHARE * q + SHARE)
        inside = slice(SHARE * (q % 4), SHARE * (q % 4) + SHARE)
        t_ref, s_ref, te_ref, se_ref, _, local = sets[q // 4]
        if q % 4 == 0:
            t_factor = jnp.exp2(local[0:1, :] - t_row)
            s_factor = jnp.exp2(local[3:4, :] - s_row)
        t_key = columns[0][0:SHARE, q : q + 1]
        s_key = columns[1][0:SHARE, q : q + 1]
        mixed = (se_ref[inside, :] * s_factor - te_ref[inside, :] * t_factor) + (
            jnp.exp2(s_ref[inside, :] - s_key) - jnp.exp2(t_ref[inside, :] - t_key)
        )
        high, low = split(mixed)
        mh[part, :] = high
        ml[part, :] = low

    def contract(a, b):
        return lax.dot_general(a, b, (((1,), (0,)), ((), ())), preferred_element_type=F32)

    kt = jnp.concatenate([v[4][...] for v in sets], axis=1)
    grad = contract(kt, mh[...])
    grad = grad[:DS, :] + grad[DS:, :] + contract(kt[:DS, :], ml[...])
    partial[...] = grad.T


def sum_kernel(parts, total):
    total[...] = jnp.sum(parts[...], axis=0)


def total_kernel(mine, partner, planes, blocks):
    total = (mine[...] + partner[...]) * (1.0 / math.sqrt(DS))
    divergence = jnp.sum(planes[:, 2, :], axis=0, keepdims=True)
    for d in range(8):
        blocks[d, 0:PAIR, :] = total
        blocks[d, PAIR:, :] = jnp.broadcast_to(divergence, (8, 128))


def finish_kernel(factor, blocks, grad, loss):
    grad[...] = blocks[:, 0:PAIR, :]
    loss[0, 0] = jnp.max(blocks[0, PAIR:, :] + blocks[4, PAIR:, :]) * factor


def shards(teacher_q, student_q):
    own, shard = pl.pallas_call(
        select_kernel,
        out_shape=(shape(BLOCK, DT + DS), shape(SHARE, DT + DS)),
        in_specs=[pl.BlockSpec(memory_space=pltpu.HBM)] * 2,
        out_specs=[pl.BlockSpec(memory_space=pl.ANY)] * 2,
        scratch_shapes=[pltpu.SemaphoreType.DMA((4,))],
        compiler_params=pltpu.CompilerParams(vmem_limit_bytes=1 << 20),
    )(
        pltpu.with_memory_space_constraint(teacher_q, pltpu.HBM),
        pltpu.with_memory_space_constraint(student_q, pltpu.HBM),
    )
    other = permute(own, lambda xh, y, c, xl, z: (xh, y, c, 1 - xl, z))
    near = lax.all_gather(shard, "zh", tiled=True)
    far = from_plane(near, 2, -2)
    up = from_plane(near, 1, -1)
    down = from_plane(near, -1, 1)
    tile = (*[shape(SET, ROWS)] * 4, shape(2 * DS, SET, dtype=BF16), shape(8, ROWS))
    halves = (shape(ROWS, DT + DS, dtype=BF16),) * 2
    rh, rl, *near_set = call(first_kernel, (*halves, *tile), (own, other, near))
    up_set = call(next_kernel, tile, (up, rh, rl))
    down_set = call(next_kernel, tile, (down, rh, rl))
    *far_set, stats = call(
        last_kernel,
        (*tile, shape(16, 24, 128)),
        (far, rh, rl, near_set[-1], up_set[-1], down_set[-1]),
    )
    everyone = lax.all_to_all(stats, PLANE, 0, 0, tiled=True)
    lse, message = call(
        combine_kernel, (shape(8, ROWS), shape(16, 8, 128)), (everyone,)
    )
    planes = lax.all_to_all(message, LINE, 0, 0, tiled=True)
    partial = call(
        mixed_kernel,
        shape(ROWS, DS),
        (*near_set, *far_set, *down_set, *up_set, lse, planes),
        [
            pltpu.VMEM((128, 128), F32),
            pltpu.VMEM((ROWS, ROWS), BF16),
            pltpu.VMEM((ROWS, ROWS), BF16),
        ],
    )
    parts = lax.all_to_all(partial.reshape(8, PAIR, DS), CHIPS, 0, 0, tiled=True)
    mine = call(sum_kernel, shape(PAIR, DS), (parts,))
    partner = permute(mine, lambda xh, y, c, xl, z: (xh, y, 1 - c, xl, z))
    blocks = call(total_kernel, shape(8, PAIR + 8, DS), (mine, partner, planes))
    blocks = lax.all_to_all(blocks, COPIES, 0, 0, tiled=True)
    factor = 1.0 / (LOG2E * 2 * BLOCK * 32)
    grad, loss = pl.pallas_call(
        functools.partial(finish_kernel, factor),
        out_shape=(shape(8, PAIR, DS), shape(1, 1)),
        in_specs=[pl.BlockSpec(memory_space=pltpu.VMEM)],
        out_specs=(pl.BlockSpec(memory_space=pltpu.VMEM), pl.BlockSpec(memory_space=pltpu.SMEM)),
        compiler_params=pltpu.CompilerParams(vmem_limit_bytes=8 << 20),
    )(blocks)
    return (grad.reshape(2, BLOCK, DS), loss.reshape(()))


def solution(mesh):
    fine = Mesh(mesh.devices.reshape(SIZES), AXES)
    tokens = P(None, ("xl", "zh", "zl"), None)
    return jax.shard_map(
        shards, mesh=fine, in_specs=(tokens, tokens), out_specs=(tokens, P()), check_vma=False
    )
```

```python
import functools
import math

import jax
import jax.numpy as jnp
from jax import lax
from jax.experimental import pallas as pl
from jax.experimental.pallas import tpu as pltpu
from jax.sharding import Mesh, PartitionSpec as P

DT = 256
DS = 128
AXES = ("xh", "y", "c", "xl", "zh", "zl")
SIZES = (2, 4, 2, 2, 4, 4)
PLANE = ("xl", "c", "y")
CHIPS = ("xl", "y")
COPIES = ("xh", "y")
PAIR = 96
LINE = ("zh", "zl")
BLOCK = 384
SHARE = 48
ROWS = 768
SET = 192
OFFSETS = (0, 2, 3, 1)
LOG2E = math.log2(math.e)


F32 = jnp.float32
BF16 = jnp.bfloat16


def shape(*dims, dtype=F32):
    return jax.ShapeDtypeStruct(dims, dtype)


def call(body, outs, ins, scratch=()):
    return pl.pallas_call(
        body,
        out_shape=outs,
        in_specs=[pl.BlockSpec(memory_space=pltpu.VMEM)] * len(ins),
        scratch_shapes=scratch,
        compiler_params=pltpu.CompilerParams(vmem_limit_bytes=28 << 20),
    )(*ins)


def permute(x, move):
    pairs = []
    for index in range(512):
        rest, where = index, []
        for size in reversed(SIZES):
            where.append(rest % size)
            rest //= size
        xh, y, c, xl, zh, zl = reversed(where)
        xh, y, c, xl, z = move(xh, y, c, xl, zh * 4 + zl)
        to = ((((xh * 4 + y) * 2 + c) * 2 + xl) * 4 + z // 4) * 4 + z % 4
        pairs.append((index, to))
    return lax.ppermute(x, AXES, pairs)


def from_plane(x, first, second):
    return permute(
        x, lambda xh, y, c, xl, z: (xh, y, c, xl, (z - (second if c else first)) % 16)
    )


def sub_index():
    return lax.axis_index("y") * 2 + lax.axis_index("c")


def split(x):
    high = x.astype(BF16)
    return high, (x - high.astype(F32)).astype(BF16)


def select_kernel(teacher, student, own, shard, sems):
    seq = lax.axis_index("xh")
    mine = pl.ds(pl.multiple_of(sub_index() * SHARE, 8), SHARE)
    copies = (
        pltpu.make_async_copy(teacher.at[seq, mine], shard.at[:, :DT], sems.at[0]),
        pltpu.make_async_copy(student.at[seq, mine], shard.at[:, DT:], sems.at[1]),
        pltpu.make_async_copy(teacher.at[seq], own.at[:, :DT], sems.at[2]),
        pltpu.make_async_copy(student.at[seq], own.at[:, DT:], sems.at[3]),
    )
    for copy in copies:
        copy.start()
    for copy in copies:
        copy.wait()


def product(a, b):
    return lax.dot_general(a, b, (((1,), (1,)), ((), ())), preferred_element_type=F32)


def transposed(x):
    return x[:, DT:].astype(F32).T.astype(BF16)


def set_scores(keys, rh, rl, t_out, s_out, te_out, se_out, kt):
    kh, kl = split(keys[...])
    kt[0:DS, :] = transposed(kh)
    kt[DS:, :] = transposed(kl)
    both = jnp.concatenate([kh, kl], axis=0)
    tops = []
    for out, lo, hi in ((t_out, 0, DT), (s_out, DT, DT + DS)):
        tile = product(both[:, lo:hi], rh[:, lo:hi])
        tile = tile[:SET, :] + tile[SET:, :] + product(kh[:, lo:hi], rl[:, lo:hi])
        out[...] = tile
        tops.append(jnp.max(tile, axis=0, keepdims=True))
    t_top, s_top = tops
    sums = [jnp.zeros((8, ROWS), F32)] * 3
    for i in range(4):
        part = slice(SHARE * i, SHARE * i + SHARE)
        t = t_out[part, :]
        s = s_out[part, :]
        te = jnp.exp2(t - t_top)
        se = jnp.exp2(s - s_top)
        te_out[part, :] = te
        se_out[part, :] = se
        for j, v in enumerate((te, te * (t - s), se)):
            sums[j] = sums[j] + jnp.sum(v.reshape(6, 8, ROWS), axis=0)
    t_sum, cross, s_sum = (jnp.sum(v, axis=0, keepdims=True) for v in sums)
    return t_top, t_sum, cross, s_top, s_sum


def keep(local, values):
    for i, v in enumerate(values):
        local[i : i + 1, :] = v


def first_kernel(own, other, near, rh, rl, t_out, s_out, te_out, se_out, kt, local):
    xl = lax.axis_index("xl")
    for ref, place in ((own, xl), (other, 1 - xl)):
        start = pl.multiple_of(place * BLOCK, BLOCK)
        for lo, hi, factor in ((0, DT, LOG2E / math.sqrt(DT)), (DT, DT + DS, LOG2E / math.sqrt(DS))):
            high, low = split(ref[:, lo:hi] * factor)
            rh[pl.ds(start, BLOCK), lo:hi] = high
            rl[pl.ds(start, BLOCK), lo:hi] = low
    keep(local, set_scores(near, rh, rl, t_out, s_out, te_out, se_out, kt))


def next_kernel(keys, rh, rl, t_out, s_out, te_out, se_out, kt, local):
    keep(local, set_scores(keys, rh, rl, t_out, s_out, te_out, se_out, kt))


def last_kernel(keys, rh, rl, local0, local1, local2, t_out, s_out, te_out, se_out, kt, local, stats):
    here = set_scores(keys, rh, rl, t_out, s_out, te_out, se_out, kt)
    keep(local, here)
    sets = [here] + [[ref[i : i + 1, :] for i in range(5)] for ref in (local0, local1, local2)]
    t_top = functools.reduce(jnp.maximum, [v[0] for v in sets])
    s_top = functools.reduce(jnp.maximum, [v[3] for v in sets])
    t_scales = [jnp.exp2(v[0] - t_top) for v in sets]
    s_scales = [jnp.exp2(v[3] - s_top) for v in sets]
    t_sum = sum(v[1] * f for v, f in zip(sets, t_scales))
    cross = sum(v[2] * f for v, f in zip(sets, t_scales))
    s_sum = sum(v[4] * f for v, f in zip(sets, s_scales))
    values = (
        t_top + jnp.log(t_sum) * LOG2E,
        s_top + jnp.log(s_sum) * LOG2E,
        cross / t_sum,
    )
    pad = jnp.zeros((2, 128), F32)
    packed = []
    for v in values:
        packed += [v[:, 128 * j : 128 * j + 128] for j in range(6)] + [pad]
    packed = jnp.concatenate(packed, axis=0)
    for d in range(16):
        stats[d] = packed


def combine_kernel(everyone, lse, message):
    t = everyone[:, 0:8, :]
    s = everyone[:, 8:16, :]
    ratio = everyone[:, 16:24, :]
    t_top = jnp.max(t, axis=0)
    s_top = jnp.max(s, axis=0)
    t_weight = jnp.exp2(t - t_top)
    t_sum = jnp.sum(t_weight, axis=0)
    s_sum = jnp.sum(jnp.exp2(s - s_top), axis=0)
    t_lse = t_top + jnp.log(t_sum) * LOG2E
    s_lse = s_top + jnp.log(s_sum) * LOG2E
    divergence = jnp.sum(t_weight * ratio, axis=0) / t_sum - t_lse + s_lse
    divergence = jnp.sum(divergence[0:6, :])

    def as_row(v):
        return jnp.concatenate([v[j : j + 1, :] for j in range(6)], axis=1)

    both = jnp.concatenate(
        [as_row(t_lse), as_row(s_lse), jnp.zeros((6, ROWS), F32)], axis=0
    )
    lse[...] = both
    mine = lax.axis_index("xl") * BLOCK + sub_index() * SHARE
    turned = pltpu.roll(both, lax.rem(ROWS - mine, ROWS), axis=1)[:, :128]
    line = lax.broadcasted_iota(jnp.int32, (8, 128), 0)
    turned = jnp.where(line == 2, divergence, turned)
    for d in range(16):
        message[d] = turned


def mixed_kernel(*refs):
    sets = [refs[6 * i : 6 * i + 6] for i in range(4)]
    lse, planes, partial, square, mh, ml = refs[24:]
    zl = lax.axis_index("zl")
    columns = []
    for i in range(2):
        square[...] = jnp.zeros_like(square)
        for q in range(16):
            plane = 4 * (q % 4) + lax.rem(zl + OFFSETS[q // 4], 4)
            square[q : q + 1, :] = planes[plane, i : i + 1, :]
        columns.append(square[...].T)
    t_row = lse[0:1, :]
    s_row = lse[1:2, :]

    def contract(a, b):
        return lax.dot_general(a, b, (((1,), (0,)), ((), ())), preferred_element_type=F32)

    grad = jnp.zeros((DS, ROWS), F32)
    for o in range(4):
        t_ref, s_ref, te_ref, se_ref, kt, local = sets[o]
        t_factor = jnp.exp2(local[0:1, :] - t_row)
        s_factor = jnp.exp2(local[3:4, :] - s_row)
        for h in range(4):
            q = 4 * o + h
            part = slice(SHARE * h, SHARE * h + SHARE)
            t_key = columns[0][0:SHARE, q : q + 1]
            s_key = columns[1][0:SHARE, q : q + 1]
            mixed = (se_ref[part, :] * s_factor - te_ref[part, :] * t_factor) + (
                jnp.exp2(s_ref[part, :] - s_key) - jnp.exp2(t_ref[part, :] - t_key)
            )
            high, low = split(mixed)
            mh[o, part, :] = high
            ml[o, part, :] = low
        both = contract(kt[...], mh[o])
        grad += both[:DS, :] + both[DS:, :] + contract(kt[:DS, :], ml[o])
    partial[...] = grad.T


def sum_kernel(parts, total):
    total[...] = jnp.sum(parts[...], axis=0)


def total_kernel(mine, partner, planes, blocks):
    total = (mine[...] + partner[...]) * (1.0 / math.sqrt(DS))
    divergence = jnp.sum(planes[:, 2, :], axis=0, keepdims=True)
    for d in range(8):
        blocks[d, 0:PAIR, :] = total
        blocks[d, PAIR:, :] = jnp.broadcast_to(divergence, (8, 128))


def finish_kernel(factor, blocks, grad, loss):
    grad[...] = blocks[:, 0:PAIR, :]
    loss[0, 0] = jnp.max(blocks[0, PAIR:, :] + blocks[4, PAIR:, :]) * factor


def shards(teacher_q, student_q):
    own, shard = pl.pallas_call(
        select_kernel,
        out_shape=(shape(BLOCK, DT + DS), shape(SHARE, DT + DS)),
        in_specs=[pl.BlockSpec(memory_space=pltpu.HBM)] * 2,
        out_specs=[pl.BlockSpec(memory_space=pl.ANY)] * 2,
        scratch_shapes=[pltpu.SemaphoreType.DMA((4,))],
        compiler_params=pltpu.CompilerParams(vmem_limit_bytes=1 << 20),
    )(
        pltpu.with_memory_space_constraint(teacher_q, pltpu.HBM),
        pltpu.with_memory_space_constraint(student_q, pltpu.HBM),
    )
    other = permute(own, lambda xh, y, c, xl, z: (xh, y, c, 1 - xl, z))
    near = lax.all_gather(shard, "zh", tiled=True)
    far = from_plane(near, 2, -2)
    up = from_plane(near, 1, 1)
    down = from_plane(near, -1, -1)
    tile = (*[shape(SET, ROWS)] * 4, shape(2 * DS, SET, dtype=BF16), shape(8, ROWS))
    halves = (shape(ROWS, DT + DS, dtype=BF16),) * 2
    rh, rl, *near_set = call(first_kernel, (*halves, *tile), (own, other, near))
    up_set = call(next_kernel, tile, (up, rh, rl))
    down_set = call(next_kernel, tile, (down, rh, rl))
    *far_set, stats = call(
        last_kernel,
        (*tile, shape(16, 24, 128)),
        (far, rh, rl, near_set[-1], up_set[-1], down_set[-1]),
    )
    everyone = lax.all_to_all(stats, PLANE, 0, 0, tiled=True)
    lse, message = call(
        combine_kernel, (shape(8, ROWS), shape(16, 8, 128)), (everyone,)
    )
    planes = lax.all_to_all(message, LINE, 0, 0, tiled=True)
    partial = call(
        mixed_kernel,
        shape(ROWS, DS),
        (*near_set, *far_set, *down_set, *up_set, lse, planes),
        [
            pltpu.VMEM((128, 128), F32),
            pltpu.VMEM((4, SET, ROWS), BF16),
            pltpu.VMEM((4, SET, ROWS), BF16),
        ],
    )
    parts = lax.all_to_all(partial.reshape(8, PAIR, DS), CHIPS, 0, 0, tiled=True)
    mine = call(sum_kernel, shape(PAIR, DS), (parts,))
    partner = permute(mine, lambda xh, y, c, xl, z: (xh, y, 1 - c, xl, z))
    blocks = call(total_kernel, shape(8, PAIR + 8, DS), (mine, partner, planes))
    blocks = lax.all_to_all(blocks, COPIES, 0, 0, tiled=True)
    factor = 1.0 / (LOG2E * 2 * BLOCK * 32)
    grad, loss = pl.pallas_call(
        functools.partial(finish_kernel, factor),
        out_shape=(shape(8, PAIR, DS), shape(1, 1)),
        in_specs=[pl.BlockSpec(memory_space=pltpu.VMEM)],
        out_specs=(pl.BlockSpec(memory_space=pltpu.VMEM), pl.BlockSpec(memory_space=pltpu.SMEM)),
        compiler_params=pltpu.CompilerParams(vmem_limit_bytes=8 << 20),
    )(blocks)
    return (grad.reshape(2, BLOCK, DS), loss.reshape(()))


def solution(mesh):
    fine = Mesh(mesh.devices.reshape(SIZES), AXES)
    tokens = P(None, ("xl", "zh", "zl"), None)
    return jax.shard_map(
        shards, mesh=fine, in_specs=(tokens, tokens), out_specs=(tokens, P()), check_vma=False
    )
```

```python
import functools
import math

import jax
import jax.numpy as jnp
from jax import lax
from jax.experimental import pallas as pl
from jax.experimental.pallas import tpu as pltpu
from jax.sharding import Mesh, PartitionSpec as P

DT = 256
DS = 128
AXES = ("xh", "y", "c", "xl", "zh", "zl")
SIZES = (2, 4, 2, 2, 4, 4)
PLANE = ("xl", "c", "y")
CHIPS = ("xl", "y")
COPIES = ("xh", "y")
PAIR = 96
LINE = ("zh", "zl")
BLOCK = 384
SHARE = 48
ROWS = 768
SET = 192
OFFSETS = (0, 2, 3, 1)
LOG2E = math.log2(math.e)


F32 = jnp.float32
BF16 = jnp.bfloat16


def shape(*dims, dtype=F32):
    return jax.ShapeDtypeStruct(dims, dtype)


def call(body, outs, ins, scratch=()):
    return pl.pallas_call(
        body,
        out_shape=outs,
        in_specs=[pl.BlockSpec(memory_space=pltpu.VMEM)] * len(ins),
        scratch_shapes=scratch,
        compiler_params=pltpu.CompilerParams(vmem_limit_bytes=28 << 20),
    )(*ins)


def permute(x, move):
    pairs = []
    for index in range(512):
        rest, where = index, []
        for size in reversed(SIZES):
            where.append(rest % size)
            rest //= size
        xh, y, c, xl, zh, zl = reversed(where)
        xh, y, c, xl, z = move(xh, y, c, xl, zh * 4 + zl)
        to = ((((xh * 4 + y) * 2 + c) * 2 + xl) * 4 + z // 4) * 4 + z % 4
        pairs.append((index, to))
    return lax.ppermute(x, AXES, pairs)


def from_plane(x, first, second):
    return permute(
        x, lambda xh, y, c, xl, z: (xh, y, c, xl, (z - (second if c else first)) % 16)
    )


def sub_index():
    return lax.axis_index("y") * 2 + lax.axis_index("c")


def split(x):
    high = x.astype(BF16)
    return high, (x - high.astype(F32)).astype(BF16)


def select_kernel(teacher, student, own, shard, sems):
    seq = lax.axis_index("xh")
    mine = pl.ds(pl.multiple_of(sub_index() * SHARE, 8), SHARE)
    copies = (
        pltpu.make_async_copy(teacher.at[seq, mine], shard.at[:, :DT], sems.at[0]),
        pltpu.make_async_copy(student.at[seq, mine], shard.at[:, DT:], sems.at[1]),
        pltpu.make_async_copy(teacher.at[seq], own.at[:, :DT], sems.at[2]),
        pltpu.make_async_copy(student.at[seq], own.at[:, DT:], sems.at[3]),
    )
    for copy in copies:
        copy.start()
    for copy in copies:
        copy.wait()


def product(a, b):
    return lax.dot_general(a, b, (((1,), (1,)), ((), ())), preferred_element_type=F32)


def transposed(x):
    return x[:, DT:].astype(F32).T.astype(BF16)


def set_scores(keys, rh, rl, t_out, s_out, te_out, se_out, kt):
    kh, kl = split(keys[...])
    kt[0:DS, :] = transposed(kh)
    kt[DS:, :] = transposed(kl)
    both = jnp.concatenate([kh, kl], axis=0)
    tops = []
    for out, lo, hi in ((t_out, 0, DT), (s_out, DT, DT + DS)):
        tile = product(both[:, lo:hi], rl[:, lo:hi])
        tile = tile[SET:, :] + tile[:SET, :]
        head = product(both[:, lo:hi], rh[:, lo:hi])
        tile = head[:SET, :] + (head[SET:, :] + tile)
        out[...] = tile
        tops.append(jnp.max(tile, axis=0, keepdims=True))
    t_top, s_top = tops
    sums = [jnp.zeros((8, ROWS), F32)] * 3
    for i in range(4):
        part = slice(SHARE * i, SHARE * i + SHARE)
        t = t_out[part, :]
        s = s_out[part, :]
        te = jnp.exp2(t - t_top)
        se = jnp.exp2(s - s_top)
        te_out[part, :] = te
        se_out[part, :] = se
        for j, v in enumerate((te, te * (t - s), se)):
            sums[j] = sums[j] + jnp.sum(v.reshape(6, 8, ROWS), axis=0)
    t_sum, cross, s_sum = (jnp.sum(v, axis=0, keepdims=True) for v in sums)
    return t_top, t_sum, cross, s_top, s_sum


def keep(local, values):
    for i, v in enumerate(values):
        local[i : i + 1, :] = v


def first_kernel(own, other, near, rh, rl, t_out, s_out, te_out, se_out, kt, local):
    xl = lax.axis_index("xl")
    for ref, place in ((own, xl), (other, 1 - xl)):
        start = pl.multiple_of(place * BLOCK, BLOCK)
        for lo, hi, factor in ((0, DT, LOG2E / math.sqrt(DT)), (DT, DT + DS, LOG2E / math.sqrt(DS))):
            high, low = split(ref[:, lo:hi] * factor)
            rh[pl.ds(start, BLOCK), lo:hi] = high
            rl[pl.ds(start, BLOCK), lo:hi] = low
    keep(local, set_scores(near, rh, rl, t_out, s_out, te_out, se_out, kt))


def next_kernel(keys, rh, rl, t_out, s_out, te_out, se_out, kt, local):
    keep(local, set_scores(keys, rh, rl, t_out, s_out, te_out, se_out, kt))


def last_kernel(keys, rh, rl, local0, local1, local2, t_out, s_out, te_out, se_out, kt, local, stats):
    here = set_scores(keys, rh, rl, t_out, s_out, te_out, se_out, kt)
    keep(local, here)
    sets = [here] + [[ref[i : i + 1, :] for i in range(5)] for ref in (local0, local1, local2)]
    t_top = functools.reduce(jnp.maximum, [v[0] for v in sets])
    s_top = functools.reduce(jnp.maximum, [v[3] for v in sets])
    t_scales = [jnp.exp2(v[0] - t_top) for v in sets]
    s_scales = [jnp.exp2(v[3] - s_top) for v in sets]
    t_sum = sum(v[1] * f for v, f in zip(sets, t_scales))
    cross = sum(v[2] * f for v, f in zip(sets, t_scales))
    s_sum = sum(v[4] * f for v, f in zip(sets, s_scales))
    values = (
        t_top + jnp.log(t_sum) * LOG2E,
        s_top + jnp.log(s_sum) * LOG2E,
        cross / t_sum,
    )
    pad = jnp.zeros((2, 128), F32)
    packed = []
    for v in values:
        packed += [v[:, 128 * j : 128 * j + 128] for j in range(6)] + [pad]
    packed = jnp.concatenate(packed, axis=0)
    for d in range(16):
        stats[d] = packed


def combine_kernel(everyone, lse, message):
    t = everyone[:, 0:8, :]
    s = everyone[:, 8:16, :]
    ratio = everyone[:, 16:24, :]
    t_top = jnp.max(t, axis=0)
    s_top = jnp.max(s, axis=0)
    t_weight = jnp.exp2(t - t_top)
    t_sum = jnp.sum(t_weight, axis=0)
    s_sum = jnp.sum(jnp.exp2(s - s_top), axis=0)
    t_lse = t_top + jnp.log(t_sum) * LOG2E
    s_lse = s_top + jnp.log(s_sum) * LOG2E
    divergence = jnp.sum(t_weight * ratio, axis=0) / t_sum - t_lse + s_lse
    divergence = jnp.sum(divergence[0:6, :])

    def as_row(v):
        return jnp.concatenate([v[j : j + 1, :] for j in range(6)], axis=1)

    both = jnp.concatenate(
        [as_row(t_lse), as_row(s_lse), jnp.zeros((6, ROWS), F32)], axis=0
    )
    lse[...] = both
    mine = lax.axis_index("xl") * BLOCK + sub_index() * SHARE
    turned = pltpu.roll(both, lax.rem(ROWS - mine, ROWS), axis=1)[:, :128]
    line = lax.broadcasted_iota(jnp.int32, (8, 128), 0)
    turned = jnp.where(line == 2, divergence, turned)
    for d in range(16):
        message[d] = turned


def mixed_kernel(*refs):
    sets = [refs[6 * i : 6 * i + 6] for i in range(4)]
    lse, planes, partial, square, mh, ml = refs[24:]
    zl = lax.axis_index("zl")
    columns = []
    for i in range(2):
        square[...] = jnp.zeros_like(square)
        for q in range(16):
            plane = 4 * (q % 4) + lax.rem(zl + OFFSETS[q // 4], 4)
            square[q : q + 1, :] = planes[plane, i : i + 1, :]
        columns.append(square[...].T)
    t_row = lse[0:1, :]
    s_row = lse[1:2, :]
    for q in range(16):
        part = slice(SHARE * q, SHARE * q + SHARE)
        inside = slice(SHARE * (q % 4), SHARE * (q % 4) + SHARE)
        t_ref, s_ref, te_ref, se_ref, _, local = sets[q // 4]
        if q % 4 == 0:
            t_factor = jnp.exp2(local[0:1, :] - t_row)
            s_factor = jnp.exp2(local[3:4, :] - s_row)
        t_key = columns[0][0:SHARE, q : q + 1]
        s_key = columns[1][0:SHARE, q : q + 1]
        mixed = (se_ref[inside, :] * s_factor - te_ref[inside, :] * t_factor) + (
            jnp.exp2(s_ref[inside, :] - s_key) - jnp.exp2(t_ref[inside, :] - t_key)
        )
        high, low = split(mixed)
        mh[part, :] = high
        ml[part, :] = low

    def contract(a, b):
        return lax.dot_general(a, b, (((1,), (0,)), ((), ())), preferred_element_type=F32)

    kt = jnp.concatenate([v[4][...] for v in sets], axis=1)
    grad = contract(kt, mh[...])
    grad = grad[:DS, :] + grad[DS:, :] + contract(kt[:DS, :], ml[...])
    partial[...] = grad.T


def sum_kernel(parts, total):
    total[...] = jnp.sum(parts[...], axis=0)


def total_kernel(mine, partner, planes, blocks):
    total = (mine[...] + partner[...]) * (1.0 / math.sqrt(DS))
    divergence = jnp.sum(planes[:, 2, :], axis=0, keepdims=True)
    for d in range(8):
        blocks[d, 0:PAIR, :] = total
        blocks[d, PAIR:, :] = jnp.broadcast_to(divergence, (8, 128))


def finish_kernel(factor, blocks, grad, loss):
    grad[...] = blocks[:, 0:PAIR, :]
    loss[0, 0] = jnp.max(blocks[0, PAIR:, :] + blocks[4, PAIR:, :]) * factor


def shards(teacher_q, student_q):
    own, shard = pl.pallas_call(
        select_kernel,
        out_shape=(shape(BLOCK, DT + DS), shape(SHARE, DT + DS)),
        in_specs=[pl.BlockSpec(memory_space=pltpu.HBM)] * 2,
        out_specs=[pl.BlockSpec(memory_space=pl.ANY)] * 2,
        scratch_shapes=[pltpu.SemaphoreType.DMA((4,))],
        compiler_params=pltpu.CompilerParams(vmem_limit_bytes=1 << 20),
    )(
        pltpu.with_memory_space_constraint(teacher_q, pltpu.HBM),
        pltpu.with_memory_space_constraint(student_q, pltpu.HBM),
    )
    other = permute(own, lambda xh, y, c, xl, z: (xh, y, c, 1 - xl, z))
    near = lax.all_gather(shard, "zh", tiled=True)
    far = from_plane(near, 2, -2)
    up = from_plane(near, 1, 1)
    down = from_plane(near, -1, -1)
    tile = (*[shape(SET, ROWS)] * 4, shape(2 * DS, SET, dtype=BF16), shape(8, ROWS))
    halves = (shape(ROWS, DT + DS, dtype=BF16),) * 2
    rh, rl, *near_set = call(first_kernel, (*halves, *tile), (own, other, near))
    up_set = call(next_kernel, tile, (up, rh, rl))
    down_set = call(next_kernel, tile, (down, rh, rl))
    *far_set, stats = call(
        last_kernel,
        (*tile, shape(16, 24, 128)),
        (far, rh, rl, near_set[-1], up_set[-1], down_set[-1]),
    )
    everyone = lax.all_to_all(stats, PLANE, 0, 0, tiled=True)
    lse, message = call(
        combine_kernel, (shape(8, ROWS), shape(16, 8, 128)), (everyone,)
    )
    planes = lax.all_to_all(message, LINE, 0, 0, tiled=True)
    partial = call(
        mixed_kernel,
        shape(ROWS, DS),
        (*near_set, *far_set, *down_set, *up_set, lse, planes),
        [
            pltpu.VMEM((128, 128), F32),
            pltpu.VMEM((ROWS, ROWS), BF16),
            pltpu.VMEM((ROWS, ROWS), BF16),
        ],
    )
    parts = lax.all_to_all(partial.reshape(8, PAIR, DS), CHIPS, 0, 0, tiled=True)
    mine = call(sum_kernel, shape(PAIR, DS), (parts,))
    partner = permute(mine, lambda xh, y, c, xl, z: (xh, y, 1 - c, xl, z))
    blocks = call(total_kernel, shape(8, PAIR + 8, DS), (mine, partner, planes))
    blocks = lax.all_to_all(blocks, COPIES, 0, 0, tiled=True)
    factor = 1.0 / (LOG2E * 2 * BLOCK * 32)
    grad, loss = pl.pallas_call(
        functools.partial(finish_kernel, factor),
        out_shape=(shape(8, PAIR, DS), shape(1, 1)),
        in_specs=[pl.BlockSpec(memory_space=pltpu.VMEM)],
        out_specs=(pl.BlockSpec(memory_space=pltpu.VMEM), pl.BlockSpec(memory_space=pltpu.SMEM)),
        compiler_params=pltpu.CompilerParams(vmem_limit_bytes=8 << 20),
    )(blocks)
    return (grad.reshape(2, BLOCK, DS), loss.reshape(()))


def solution(mesh):
    fine = Mesh(mesh.devices.reshape(SIZES), AXES)
    tokens = P(None, ("xl", "zh", "zl"), None)
    return jax.shard_map(
        shards, mesh=fine, in_specs=(tokens, tokens), out_specs=(tokens, P()), check_vma=False
    )
```

```python
import functools
import math

import jax
import jax.numpy as jnp
from jax import lax
from jax.experimental import pallas as pl
from jax.experimental.pallas import tpu as pltpu
from jax.sharding import Mesh, PartitionSpec as P

DT = 256
DS = 128
AXES = ("xh", "y", "c", "xl", "zh", "zl")
SIZES = (2, 4, 2, 2, 4, 4)
PLANE = ("xl", "c", "y")
CHIPS = ("xl", "y")
COPIES = ("xh", "y")
PAIR = 96
LINE = ("zh", "zl")
BLOCK = 384
SHARE = 48
ROWS = 768
SET = 192
OFFSETS = (0, 2, 3, 1)
LOG2E = math.log2(math.e)


F32 = jnp.float32
BF16 = jnp.bfloat16


def shape(*dims, dtype=F32):
    return jax.ShapeDtypeStruct(dims, dtype)


def call(body, outs, ins, scratch=()):
    return pl.pallas_call(
        body,
        out_shape=outs,
        in_specs=[pl.BlockSpec(memory_space=pltpu.VMEM)] * len(ins),
        scratch_shapes=scratch,
        compiler_params=pltpu.CompilerParams(vmem_limit_bytes=28 << 20),
    )(*ins)


def permute(x, move):
    pairs = []
    for index in range(512):
        rest, where = index, []
        for size in reversed(SIZES):
            where.append(rest % size)
            rest //= size
        xh, y, c, xl, zh, zl = reversed(where)
        xh, y, c, xl, z = move(xh, y, c, xl, zh * 4 + zl)
        to = ((((xh * 4 + y) * 2 + c) * 2 + xl) * 4 + z // 4) * 4 + z % 4
        pairs.append((index, to))
    return lax.ppermute(x, AXES, pairs)


def from_plane(x, first, second):
    return permute(
        x, lambda xh, y, c, xl, z: (xh, y, c, xl, (z - (second if c else first)) % 16)
    )


def sub_index():
    return lax.axis_index("y") * 2 + lax.axis_index("c")


def split(x):
    high = x.astype(BF16)
    return high, (x - high.astype(F32)).astype(BF16)


def select_kernel(teacher, student, own, shard, sems):
    seq = lax.axis_index("xh")
    mine = pl.ds(pl.multiple_of(sub_index() * SHARE, 8), SHARE)
    copies = (
        pltpu.make_async_copy(teacher.at[seq, mine], shard.at[:, :DT], sems.at[0]),
        pltpu.make_async_copy(student.at[seq, mine], shard.at[:, DT:], sems.at[1]),
        pltpu.make_async_copy(teacher.at[seq], own.at[:, :DT], sems.at[2]),
        pltpu.make_async_copy(student.at[seq], own.at[:, DT:], sems.at[3]),
    )
    for copy in copies:
        copy.start()
    for copy in copies:
        copy.wait()


def product(a, b):
    return lax.dot_general(a, b, (((1,), (1,)), ((), ())), preferred_element_type=F32)


def transposed(x):
    return x[:, DT:].astype(F32).T.astype(BF16)


def set_scores(keys, rh, rl, t_out, s_out, te_out, se_out, kt):
    kh, kl = split(keys[...])
    kt[0:DS, :] = transposed(kh)
    kt[DS:, :] = transposed(kl)
    both = jnp.concatenate([kh, kl], axis=0)
    tops = []
    for out, lo, hi in ((t_out, 0, DT), (s_out, DT, DT + DS)):
        tile = product(both[:, lo:hi], rh[:, lo:hi])
        tile = tile[:SET, :] + tile[SET:, :] + product(kh[:, lo:hi], rl[:, lo:hi])
        out[...] = tile
        tops.append(jnp.max(tile, axis=0, keepdims=True))
    t_top, s_top = tops
    sums = [jnp.zeros((8, ROWS), F32)] * 3
    for i in range(4):
        part = slice(SHARE * i, SHARE * i + SHARE)
        t = t_out[part, :]
        s = s_out[part, :]
        te = jnp.exp2(t - t_top)
        se = jnp.exp2(s - s_top)
        te_out[part, :] = te
        se_out[part, :] = se
        for j, v in enumerate((te, te * (t - s), se)):
            sums[j] = sums[j] + jnp.sum(v.reshape(6, 8, ROWS), axis=0)
    t_sum, cross, s_sum = (jnp.sum(v, axis=0, keepdims=True) for v in sums)
    return t_top, t_sum, cross, s_top, s_sum


def keep(local, values):
    for i, v in enumerate(values):
        local[i : i + 1, :] = v


def first_kernel(own, other, near, rh, rl, t_out, s_out, te_out, se_out, kt, local):
    xl = lax.axis_index("xl")
    for ref, place in ((own, xl), (other, 1 - xl)):
        start = pl.multiple_of(place * BLOCK, BLOCK)
        for lo, hi, factor in ((0, DT, LOG2E / math.sqrt(DT)), (DT, DT + DS, LOG2E / math.sqrt(DS))):
            high, low = split(ref[:, lo:hi] * factor)
            rh[pl.ds(start, BLOCK), lo:hi] = high
            rl[pl.ds(start, BLOCK), lo:hi] = low
    keep(local, set_scores(near, rh, rl, t_out, s_out, te_out, se_out, kt))


def next_kernel(keys, rh, rl, t_out, s_out, te_out, se_out, kt, local):
    keep(local, set_scores(keys, rh, rl, t_out, s_out, te_out, se_out, kt))


def last_kernel(keys, rh, rl, local0, local1, local2, t_out, s_out, te_out, se_out, kt, local, stats):
    here = set_scores(keys, rh, rl, t_out, s_out, te_out, se_out, kt)
    keep(local, here)
    sets = [here] + [[ref[i : i + 1, :] for i in range(5)] for ref in (local0, local1, local2)]
    t_top = functools.reduce(jnp.maximum, [v[0] for v in sets])
    s_top = functools.reduce(jnp.maximum, [v[3] for v in sets])
    t_scales = [jnp.exp2(v[0] - t_top) for v in sets]
    s_scales = [jnp.exp2(v[3] - s_top) for v in sets]
    t_sum = sum(v[1] * f for v, f in zip(sets, t_scales))
    cross = sum(v[2] * f for v, f in zip(sets, t_scales))
    s_sum = sum(v[4] * f for v, f in zip(sets, s_scales))
    values = (
        t_top + jnp.log(t_sum) * LOG2E,
        s_top + jnp.log(s_sum) * LOG2E,
        cross / t_sum,
    )
    pad = jnp.zeros((2, 128), F32)
    packed = []
    for v in values:
        packed += [v[:, 128 * j : 128 * j + 128] for j in range(6)] + [pad]
    packed = jnp.concatenate(packed, axis=0)
    for d in range(16):
        stats[d] = packed


def combine_kernel(everyone, lse, message):
    t = everyone[:, 0:8, :]
    s = everyone[:, 8:16, :]
    ratio = everyone[:, 16:24, :]
    t_top = jnp.max(t, axis=0)
    s_top = jnp.max(s, axis=0)
    t_weight = jnp.exp2(t - t_top)
    t_sum = jnp.sum(t_weight, axis=0)
    s_sum = jnp.sum(jnp.exp2(s - s_top), axis=0)
    t_lse = t_top + jnp.log(t_sum) * LOG2E
    s_lse = s_top + jnp.log(s_sum) * LOG2E
    divergence = jnp.sum(t_weight * ratio, axis=0) / t_sum - t_lse + s_lse
    divergence = jnp.sum(divergence[0:6, :])

    def as_row(v):
        return jnp.concatenate([v[j : j + 1, :] for j in range(6)], axis=1)

    both = jnp.concatenate(
        [as_row(t_lse), as_row(s_lse), jnp.zeros((6, ROWS), F32)], axis=0
    )
    lse[...] = both
    mine = lax.axis_index("xl") * BLOCK + sub_index() * SHARE
    turned = pltpu.roll(both, lax.rem(ROWS - mine, ROWS), axis=1)[:, :128]
    shifted = pltpu.roll(turned, SHARE, axis=1)
    lane = lax.broadcasted_iota(jnp.int32, (1, 128), 1)
    row = jnp.where(lane < SHARE, turned[0:1, :], shifted[1:2, :])
    row = jnp.where(lane < 2 * SHARE, row, divergence)
    for d in range(16):
        message[d] = row


def mixed_kernel(*refs):
    sets = [refs[6 * i : 6 * i + 6] for i in range(4)]
    lse, planes, partial, square, mh, ml = refs[24:]
    zl = lax.axis_index("zl")
    square[...] = jnp.zeros_like(square)
    for q in range(16):
        plane = 4 * (q % 4) + lax.rem(zl + OFFSETS[q // 4], 4)
        square[q : q + 1, :] = planes[plane]
    columns = square[...].T
    t_row = lse[0:1, :]
    s_row = lse[1:2, :]
    for q in range(16):
        part = slice(SHARE * q, SHARE * q + SHARE)
        inside = slice(SHARE * (q % 4), SHARE * (q % 4) + SHARE)
        t_ref, s_ref, te_ref, se_ref, _, local = sets[q // 4]
        if q % 4 == 0:
            t_factor = jnp.exp2(local[0:1, :] - t_row)
            s_factor = jnp.exp2(local[3:4, :] - s_row)
        t_key = columns[0:SHARE, q : q + 1]
        s_key = columns[SHARE : 2 * SHARE, q : q + 1]
        mixed = (se_ref[inside, :] * s_factor - te_ref[inside, :] * t_factor) + (
            jnp.exp2(s_ref[inside, :] - s_key) - jnp.exp2(t_ref[inside, :] - t_key)
        )
        high, low = split(mixed)
        mh[part, :] = high
        ml[part, :] = low

    def contract(a, b):
        return lax.dot_general(a, b, (((1,), (0,)), ((), ())), preferred_element_type=F32)

    kt = jnp.concatenate([v[4][...] for v in sets], axis=1)
    grad = contract(kt, mh[...])
    grad = grad[:DS, :] + grad[DS:, :] + contract(kt[:DS, :], ml[...])
    partial[...] = grad.T


def sum_kernel(parts, total):
    total[...] = jnp.sum(parts[...], axis=0)


def total_kernel(mine, partner, planes, blocks):
    total = (mine[...] + partner[...]) * (1.0 / math.sqrt(DS))
    divergence = jnp.max(jnp.sum(planes[...], axis=0)[:, 127:128])
    for d in range(8):
        blocks[d, 0:PAIR, :] = total
        blocks[d, PAIR:, :] = jnp.full((8, 128), divergence, F32)


def finish_kernel(factor, blocks, grad, loss):
    grad[...] = blocks[:, 0:PAIR, :]
    loss[0, 0] = jnp.max(blocks[0, PAIR:, :] + blocks[4, PAIR:, :]) * factor


def shards(teacher_q, student_q):
    own, shard = pl.pallas_call(
        select_kernel,
        out_shape=(shape(BLOCK, DT + DS), shape(SHARE, DT + DS)),
        in_specs=[pl.BlockSpec(memory_space=pltpu.HBM)] * 2,
        out_specs=[pl.BlockSpec(memory_space=pl.ANY)] * 2,
        scratch_shapes=[pltpu.SemaphoreType.DMA((4,))],
        compiler_params=pltpu.CompilerParams(vmem_limit_bytes=1 << 20),
    )(
        pltpu.with_memory_space_constraint(teacher_q, pltpu.HBM),
        pltpu.with_memory_space_constraint(student_q, pltpu.HBM),
    )
    other = permute(own, lambda xh, y, c, xl, z: (xh, y, c, 1 - xl, z))
    near = lax.all_gather(shard, "zh", tiled=True)
    far = from_plane(near, 2, -2)
    up = from_plane(near, 1, 1)
    down = from_plane(near, -1, -1)
    tile = (*[shape(SET, ROWS)] * 4, shape(2 * DS, SET, dtype=BF16), shape(8, ROWS))
    halves = (shape(ROWS, DT + DS, dtype=BF16),) * 2
    rh, rl, *near_set = call(first_kernel, (*halves, *tile), (own, other, near))
    up_set = call(next_kernel, tile, (up, rh, rl))
    down_set = call(next_kernel, tile, (down, rh, rl))
    *far_set, stats = call(
        last_kernel,
        (*tile, shape(16, 24, 128)),
        (far, rh, rl, near_set[-1], up_set[-1], down_set[-1]),
    )
    everyone = lax.all_to_all(stats, PLANE, 0, 0, tiled=True)
    lse, message = call(
        combine_kernel, (shape(8, ROWS), shape(16, 1, 128)), (everyone,)
    )
    planes = lax.all_to_all(message, LINE, 0, 0, tiled=True)
    partial = call(
        mixed_kernel,
        shape(ROWS, DS),
        (*near_set, *far_set, *down_set, *up_set, lse, planes),
        [
            pltpu.VMEM((128, 128), F32),
            pltpu.VMEM((ROWS, ROWS), BF16),
            pltpu.VMEM((ROWS, ROWS), BF16),
        ],
    )
    parts = lax.all_to_all(partial.reshape(8, PAIR, DS), CHIPS, 0, 0, tiled=True)
    mine = call(sum_kernel, shape(PAIR, DS), (parts,))
    partner = permute(mine, lambda xh, y, c, xl, z: (xh, y, 1 - c, xl, z))
    blocks = call(total_kernel, shape(8, PAIR + 8, DS), (mine, partner, planes))
    blocks = lax.all_to_all(blocks, COPIES, 0, 0, tiled=True)
    factor = 1.0 / (LOG2E * 2 * BLOCK * 32)
    grad, loss = pl.pallas_call(
        functools.partial(finish_kernel, factor),
        out_shape=(shape(8, PAIR, DS), shape(1, 1)),
        in_specs=[pl.BlockSpec(memory_space=pltpu.VMEM)],
        out_specs=(pl.BlockSpec(memory_space=pltpu.VMEM), pl.BlockSpec(memory_space=pltpu.SMEM)),
        compiler_params=pltpu.CompilerParams(vmem_limit_bytes=8 << 20),
    )(blocks)
    return (grad.reshape(2, BLOCK, DS), loss.reshape(()))


def solution(mesh):
    fine = Mesh(mesh.devices.reshape(SIZES), AXES)
    tokens = P(None, ("xl", "zh", "zl"), None)
    return jax.shard_map(
        shards, mesh=fine, in_specs=(tokens, tokens), out_specs=(tokens, P()), check_vma=False
    )
```

```python
import functools
import math

import jax
import jax.numpy as jnp
from jax import lax
from jax.experimental import pallas as pl
from jax.experimental.pallas import tpu as pltpu
from jax.sharding import Mesh, PartitionSpec as P

DT = 256
DS = 128
AXES = ("xh", "y", "c", "xl", "zh", "zl")
SIZES = (2, 4, 2, 2, 4, 4)
PLANE = ("xl", "c", "y")
CHIPS = ("xl", "y")
COPIES = ("xh", "y")
PAIR = 96
LINE = ("zh", "zl")
BLOCK = 384
SHARE = 48
ROWS = 768
SET = 192
OFFSETS = (0, 2, 3, 1)
LOG2E = math.log2(math.e)


F32 = jnp.float32
BF16 = jnp.bfloat16


def shape(*dims, dtype=F32):
    return jax.ShapeDtypeStruct(dims, dtype)


def call(body, outs, ins, scratch=()):
    return pl.pallas_call(
        body,
        out_shape=outs,
        in_specs=[pl.BlockSpec(memory_space=pltpu.VMEM)] * len(ins),
        scratch_shapes=scratch,
        compiler_params=pltpu.CompilerParams(vmem_limit_bytes=28 << 20),
    )(*ins)


def permute(x, move):
    pairs = []
    for index in range(512):
        rest, where = index, []
        for size in reversed(SIZES):
            where.append(rest % size)
            rest //= size
        xh, y, c, xl, zh, zl = reversed(where)
        xh, y, c, xl, z = move(xh, y, c, xl, zh * 4 + zl)
        to = ((((xh * 4 + y) * 2 + c) * 2 + xl) * 4 + z // 4) * 4 + z % 4
        pairs.append((index, to))
    return lax.ppermute(x, AXES, pairs)


def from_plane(x, first, second):
    return permute(
        x, lambda xh, y, c, xl, z: (xh, y, c, xl, (z - (second if c else first)) % 16)
    )


def sub_index():
    return lax.axis_index("y") * 2 + lax.axis_index("c")


def split(x):
    high = x.astype(BF16)
    return high, (x - high.astype(F32)).astype(BF16)


def select_kernel(teacher, student, own, shard, sems):
    seq = lax.axis_index("xh")
    mine = pl.ds(pl.multiple_of(sub_index() * SHARE, 8), SHARE)
    copies = (
        pltpu.make_async_copy(teacher.at[seq, mine], shard.at[:, :DT], sems.at[0]),
        pltpu.make_async_copy(student.at[seq, mine], shard.at[:, DT:], sems.at[1]),
        pltpu.make_async_copy(teacher.at[seq], own.at[:, :DT], sems.at[2]),
        pltpu.make_async_copy(student.at[seq], own.at[:, DT:], sems.at[3]),
    )
    for copy in copies:
        copy.start()
    for copy in copies:
        copy.wait()


def product(a, b):
    return lax.dot_general(a, b, (((1,), (1,)), ((), ())), preferred_element_type=F32)


def transposed(x):
    return x[:, DT:].astype(F32).T.astype(BF16)


def set_scores(keys, rh, rl, t_out, s_out, te_out, se_out, kt):
    kh, kl = split(keys[...])
    kt[0:DS, :] = transposed(kh)
    kt[DS:, :] = transposed(kl)
    both = jnp.concatenate([kh, kl], axis=0)
    tops = []
    for out, lo, hi in ((t_out, 0, DT), (s_out, DT, DT + DS)):
        tile = product(both[:, lo:hi], rh[:, lo:hi])
        tile = tile[:SET, :] + tile[SET:, :] + product(kh[:, lo:hi], rl[:, lo:hi])
        out[...] = tile
        tops.append(jnp.max(tile, axis=0, keepdims=True))
    t_top, s_top = tops
    sums = [jnp.zeros((8, ROWS), F32)] * 3
    for i in range(4):
        part = slice(SHARE * i, SHARE * i + SHARE)
        t = t_out[part, :]
        s = s_out[part, :]
        te = jnp.exp2(t - t_top)
        se = jnp.exp2(s - s_top)
        te_out[part, :] = te
        se_out[part, :] = se
        for j, v in enumerate((te, te * (t - s), se)):
            sums[j] = sums[j] + jnp.sum(v.reshape(6, 8, ROWS), axis=0)
    t_sum, cross, s_sum = (jnp.sum(v, axis=0, keepdims=True) for v in sums)
    return t_top, t_sum, cross, s_top, s_sum


def keep(local, values):
    for i, v in enumerate(values):
        local[i : i + 1, :] = v


def first_kernel(own, other, near, rh, rl, t_out, s_out, te_out, se_out, kt, local):
    xl = lax.axis_index("xl")
    for ref, place in ((own, xl), (other, 1 - xl)):
        start = pl.multiple_of(place * BLOCK, BLOCK)
        for lo, hi, factor in ((0, DT, LOG2E / math.sqrt(DT)), (DT, DT + DS, LOG2E / math.sqrt(DS))):
            high, low = split(ref[:, lo:hi] * factor)
            rh[pl.ds(start, BLOCK), lo:hi] = high
            rl[pl.ds(start, BLOCK), lo:hi] = low
    keep(local, set_scores(near, rh, rl, t_out, s_out, te_out, se_out, kt))


def next_kernel(keys, rh, rl, t_out, s_out, te_out, se_out, kt, local):
    keep(local, set_scores(keys, rh, rl, t_out, s_out, te_out, se_out, kt))


def last_kernel(keys, rh, rl, local0, local1, local2, t_out, s_out, te_out, se_out, kt, local, stats):
    here = set_scores(keys, rh, rl, t_out, s_out, te_out, se_out, kt)
    keep(local, here)
    sets = [here] + [[ref[i : i + 1, :] for i in range(5)] for ref in (local0, local1, local2)]
    t_top = functools.reduce(jnp.maximum, [v[0] for v in sets])
    s_top = functools.reduce(jnp.maximum, [v[3] for v in sets])
    t_scales = [jnp.exp2(v[0] - t_top) for v in sets]
    s_scales = [jnp.exp2(v[3] - s_top) for v in sets]
    t_sum = sum(v[1] * f for v, f in zip(sets, t_scales))
    cross = sum(v[2] * f for v, f in zip(sets, t_scales))
    s_sum = sum(v[4] * f for v, f in zip(sets, s_scales))
    values = (
        t_top + jnp.log(t_sum) * LOG2E,
        s_top + jnp.log(s_sum) * LOG2E,
        cross / t_sum,
    )
    row = jnp.concatenate(values, axis=1)
    for d in range(16):
        stats[d] = row


def combine_kernel(everyone, lse, message):
    rows = jnp.concatenate([everyone[d] for d in range(16)], axis=0)
    t = rows[:, 0:ROWS]
    s = rows[:, ROWS : 2 * ROWS]
    ratio = rows[:, 2 * ROWS :]
    t_top = jnp.max(t, axis=0, keepdims=True)
    s_top = jnp.max(s, axis=0, keepdims=True)
    t_weight = jnp.exp2(t - t_top)
    t_sum = jnp.sum(t_weight, axis=0, keepdims=True)
    s_sum = jnp.sum(jnp.exp2(s - s_top), axis=0, keepdims=True)
    t_lse = t_top + jnp.log(t_sum) * LOG2E
    s_lse = s_top + jnp.log(s_sum) * LOG2E
    mean = jnp.sum(t_weight * ratio, axis=0, keepdims=True) / t_sum
    divergence = jnp.sum(mean - t_lse + s_lse)
    both = jnp.concatenate([t_lse, s_lse, jnp.zeros((6, ROWS), F32)], axis=0)
    lse[...] = both
    mine = lax.axis_index("xl") * BLOCK + sub_index() * SHARE
    turned = pltpu.roll(both, lax.rem(ROWS - mine, ROWS), axis=1)[:, :128]
    shifted = pltpu.roll(turned, SHARE, axis=1)
    lane = lax.broadcasted_iota(jnp.int32, (1, 128), 1)
    row = jnp.where(lane < SHARE, turned[0:1, :], shifted[1:2, :])
    row = jnp.where(lane < 2 * SHARE, row, divergence)
    for d in range(16):
        message[d] = row


def mixed_kernel(*refs):
    sets = [refs[6 * i : 6 * i + 6] for i in range(4)]
    lse, planes, partial, square, mh, ml = refs[24:]
    zl = lax.axis_index("zl")
    square[...] = jnp.zeros_like(square)
    for q in range(16):
        plane = 4 * (q % 4) + lax.rem(zl + OFFSETS[q // 4], 4)
        square[q : q + 1, :] = planes[plane]
    columns = square[...].T
    t_row = lse[0:1, :]
    s_row = lse[1:2, :]
    for q in range(16):
        part = slice(SHARE * q, SHARE * q + SHARE)
        inside = slice(SHARE * (q % 4), SHARE * (q % 4) + SHARE)
        t_ref, s_ref, te_ref, se_ref, _, local = sets[q // 4]
        if q % 4 == 0:
            t_factor = jnp.exp2(local[0:1, :] - t_row)
            s_factor = jnp.exp2(local[3:4, :] - s_row)
        t_key = columns[0:SHARE, q : q + 1]
        s_key = columns[SHARE : 2 * SHARE, q : q + 1]
        mixed = (se_ref[inside, :] * s_factor - te_ref[inside, :] * t_factor) + (
            jnp.exp2(s_ref[inside, :] - s_key) - jnp.exp2(t_ref[inside, :] - t_key)
        )
        high, low = split(mixed)
        mh[part, :] = high
        ml[part, :] = low

    def contract(a, b):
        return lax.dot_general(a, b, (((1,), (0,)), ((), ())), preferred_element_type=F32)

    kt = jnp.concatenate([v[4][...] for v in sets], axis=1)
    grad = contract(kt, mh[...])
    grad = grad[:DS, :] + grad[DS:, :] + contract(kt[:DS, :], ml[...])
    partial[...] = grad.T


def sum_kernel(parts, total):
    total[...] = jnp.sum(parts[...], axis=0)


def total_kernel(mine, partner, planes, blocks):
    total = (mine[...] + partner[...]) * (1.0 / math.sqrt(DS))
    divergence = jnp.max(jnp.sum(planes[...], axis=0)[:, 127:128])
    for d in range(8):
        blocks[d, 0:PAIR, :] = total
        blocks[d, PAIR:, :] = jnp.full((8, 128), divergence, F32)


def finish_kernel(factor, blocks, grad, loss):
    grad[...] = blocks[:, 0:PAIR, :]
    loss[0, 0] = jnp.max(blocks[0, PAIR:, :] + blocks[4, PAIR:, :]) * factor


def shards(teacher_q, student_q):
    own, shard = pl.pallas_call(
        select_kernel,
        out_shape=(shape(BLOCK, DT + DS), shape(SHARE, DT + DS)),
        in_specs=[pl.BlockSpec(memory_space=pltpu.HBM)] * 2,
        out_specs=[pl.BlockSpec(memory_space=pl.ANY)] * 2,
        scratch_shapes=[pltpu.SemaphoreType.DMA((4,))],
        compiler_params=pltpu.CompilerParams(vmem_limit_bytes=1 << 20),
    )(
        pltpu.with_memory_space_constraint(teacher_q, pltpu.HBM),
        pltpu.with_memory_space_constraint(student_q, pltpu.HBM),
    )
    other = permute(own, lambda xh, y, c, xl, z: (xh, y, c, 1 - xl, z))
    near = lax.all_gather(shard, "zh", tiled=True)
    far = from_plane(near, 2, -2)
    up = from_plane(near, 1, 1)
    down = from_plane(near, -1, -1)
    tile = (*[shape(SET, ROWS)] * 4, shape(2 * DS, SET, dtype=BF16), shape(8, ROWS))
    halves = (shape(ROWS, DT + DS, dtype=BF16),) * 2
    rh, rl, *near_set = call(first_kernel, (*halves, *tile), (own, other, near))
    up_set = call(next_kernel, tile, (up, rh, rl))
    down_set = call(next_kernel, tile, (down, rh, rl))
    *far_set, stats = call(
        last_kernel,
        (*tile, shape(16, 1, 3 * ROWS)),
        (far, rh, rl, near_set[-1], up_set[-1], down_set[-1]),
    )
    everyone = lax.all_to_all(stats, PLANE, 0, 0, tiled=True)
    lse, message = call(
        combine_kernel, (shape(8, ROWS), shape(16, 1, 128)), (everyone,)
    )
    planes = lax.all_to_all(message, LINE, 0, 0, tiled=True)
    partial = call(
        mixed_kernel,
        shape(ROWS, DS),
        (*near_set, *far_set, *down_set, *up_set, lse, planes),
        [
            pltpu.VMEM((128, 128), F32),
            pltpu.VMEM((ROWS, ROWS), BF16),
            pltpu.VMEM((ROWS, ROWS), BF16),
        ],
    )
    parts = lax.all_to_all(partial.reshape(8, PAIR, DS), CHIPS, 0, 0, tiled=True)
    mine = call(sum_kernel, shape(PAIR, DS), (parts,))
    partner = permute(mine, lambda xh, y, c, xl, z: (xh, y, 1 - c, xl, z))
    blocks = call(total_kernel, shape(8, PAIR + 8, DS), (mine, partner, planes))
    blocks = lax.all_to_all(blocks, COPIES, 0, 0, tiled=True)
    factor = 1.0 / (LOG2E * 2 * BLOCK * 32)
    grad, loss = pl.pallas_call(
        functools.partial(finish_kernel, factor),
        out_shape=(shape(8, PAIR, DS), shape(1, 1)),
        in_specs=[pl.BlockSpec(memory_space=pltpu.VMEM)],
        out_specs=(pl.BlockSpec(memory_space=pltpu.VMEM), pl.BlockSpec(memory_space=pltpu.SMEM)),
        compiler_params=pltpu.CompilerParams(vmem_limit_bytes=8 << 20),
    )(blocks)
    return (grad.reshape(2, BLOCK, DS), loss.reshape(()))


def solution(mesh):
    fine = Mesh(mesh.devices.reshape(SIZES), AXES)
    tokens = P(None, ("xl", "zh", "zl"), None)
    return jax.shard_map(
        shards, mesh=fine, in_specs=(tokens, tokens), out_specs=(tokens, P()), check_vma=False
    )
```

```python
import functools
import math

import jax
import jax.numpy as jnp
from jax import lax
from jax.experimental import pallas as pl
from jax.experimental.pallas import tpu as pltpu
from jax.sharding import Mesh, PartitionSpec as P

DT = 256
DS = 128
AXES = ("xh", "y", "c", "xl", "zh", "zl")
SIZES = (2, 4, 2, 2, 4, 4)
PLANE = ("xl", "c", "y")
CHIPS = ("xl", "y")
COPIES = ("xh", "y")
PAIR = 96
LINE = ("zh", "zl")
BLOCK = 384
SHARE = 48
ROWS = 768
SET = 192
OFFSETS = (0, 2, 3, 1)
LOG2E = math.log2(math.e)


F32 = jnp.float32
BF16 = jnp.bfloat16


def shape(*dims, dtype=F32):
    return jax.ShapeDtypeStruct(dims, dtype)


def call(body, outs, ins, scratch=()):
    return pl.pallas_call(
        body,
        out_shape=outs,
        in_specs=[pl.BlockSpec(memory_space=pltpu.VMEM)] * len(ins),
        scratch_shapes=scratch,
        compiler_params=pltpu.CompilerParams(vmem_limit_bytes=28 << 20),
    )(*ins)


def permute(x, move):
    pairs = []
    for index in range(512):
        rest, where = index, []
        for size in reversed(SIZES):
            where.append(rest % size)
            rest //= size
        xh, y, c, xl, zh, zl = reversed(where)
        xh, y, c, xl, z = move(xh, y, c, xl, zh * 4 + zl)
        to = ((((xh * 4 + y) * 2 + c) * 2 + xl) * 4 + z // 4) * 4 + z % 4
        pairs.append((index, to))
    return lax.ppermute(x, AXES, pairs)


def from_plane(x, first, second):
    return permute(
        x, lambda xh, y, c, xl, z: (xh, y, c, xl, (z - (second if c else first)) % 16)
    )


def sub_index():
    return lax.axis_index("y") * 2 + lax.axis_index("c")


def split(x):
    high = x.astype(BF16)
    return high, (x - high.astype(F32)).astype(BF16)


def select_kernel(teacher, student, own, shard, sems):
    seq = lax.axis_index("xh")
    mine = pl.ds(pl.multiple_of(sub_index() * SHARE, 8), SHARE)
    copies = (
        pltpu.make_async_copy(teacher.at[seq, mine], shard.at[:, :DT], sems.at[0]),
        pltpu.make_async_copy(student.at[seq, mine], shard.at[:, DT:], sems.at[1]),
        pltpu.make_async_copy(teacher.at[seq], own.at[:, :DT], sems.at[2]),
        pltpu.make_async_copy(student.at[seq], own.at[:, DT:], sems.at[3]),
    )
    for copy in copies:
        copy.start()
    for copy in copies:
        copy.wait()


def product(a, b):
    return lax.dot_general(a, b, (((1,), (1,)), ((), ())), preferred_element_type=F32)


def transposed(x):
    return x[:, DT:].astype(F32).T.astype(BF16)


def set_scores(keys, rh, rl, t_out, s_out, te_out, se_out, kt):
    kh, kl = split(keys[...])
    kt[0:DS, :] = transposed(kh)
    kt[DS:, :] = transposed(kl)
    both = jnp.concatenate([kh, kl], axis=0)
    tops = []
    for out, lo, hi in ((t_out, 0, DT), (s_out, DT, DT + DS)):
        tile = product(both[:, lo:hi], rh[:, lo:hi])
        tile = tile[:SET, :] + tile[SET:, :] + product(kh[:, lo:hi], rl[:, lo:hi])
        out[...] = tile
        tops.append(jnp.max(tile, axis=0, keepdims=True))
    t_top, s_top = tops
    sums = [jnp.zeros((8, ROWS), F32)] * 3
    for i in range(4):
        part = slice(SHARE * i, SHARE * i + SHARE)
        t = t_out[part, :]
        s = s_out[part, :]
        te = jnp.exp2(t - t_top)
        se = jnp.exp2(s - s_top)
        te_out[part, :] = te
        se_out[part, :] = se
        for j, v in enumerate((te, te * (t - s), se)):
            sums[j] = sums[j] + jnp.sum(v.reshape(6, 8, ROWS), axis=0)
    t_sum, cross, s_sum = (jnp.sum(v, axis=0, keepdims=True) for v in sums)
    return t_top, t_sum, cross, s_top, s_sum


def keep(local, values):
    for i, v in enumerate(values):
        local[i : i + 1, :] = v


def first_kernel(own, other, near, rh, rl, t_out, s_out, te_out, se_out, kt, local):
    xl = lax.axis_index("xl")
    for ref, place in ((own, xl), (other, 1 - xl)):
        start = pl.multiple_of(place * BLOCK, BLOCK)
        for lo, hi, factor in ((0, DT, LOG2E / math.sqrt(DT)), (DT, DT + DS, LOG2E / math.sqrt(DS))):
            high, low = split(ref[:, lo:hi] * factor)
            rh[pl.ds(start, BLOCK), lo:hi] = high
            rl[pl.ds(start, BLOCK), lo:hi] = low
    keep(local, set_scores(near, rh, rl, t_out, s_out, te_out, se_out, kt))


def next_kernel(keys, rh, rl, t_out, s_out, te_out, se_out, kt, local):
    keep(local, set_scores(keys, rh, rl, t_out, s_out, te_out, se_out, kt))


def last_kernel(keys, rh, rl, local0, local1, local2, t_out, s_out, te_out, se_out, kt, local, stats):
    here = set_scores(keys, rh, rl, t_out, s_out, te_out, se_out, kt)
    keep(local, here)
    sets = [here] + [[ref[i : i + 1, :] for i in range(5)] for ref in (local0, local1, local2)]
    t_top = functools.reduce(jnp.maximum, [v[0] for v in sets])
    s_top = functools.reduce(jnp.maximum, [v[3] for v in sets])
    t_scales = [jnp.exp2(v[0] - t_top) for v in sets]
    s_scales = [jnp.exp2(v[3] - s_top) for v in sets]
    t_sum = sum(v[1] * f for v, f in zip(sets, t_scales))
    cross = sum(v[2] * f for v, f in zip(sets, t_scales))
    s_sum = sum(v[4] * f for v, f in zip(sets, s_scales))
    values = (
        t_top + jnp.log(t_sum) * LOG2E,
        s_top + jnp.log(s_sum) * LOG2E,
        cross / t_sum,
    )
    row = jnp.concatenate(values, axis=1)
    for d in range(16):
        stats[d] = row


def combine_kernel(everyone, lse, message):
    rows = jnp.concatenate([everyone[d] for d in range(16)], axis=0)
    t = rows[:, 0:ROWS]
    s = rows[:, ROWS : 2 * ROWS]
    ratio = rows[:, 2 * ROWS :]
    t_top = jnp.max(t, axis=0, keepdims=True)
    s_top = jnp.max(s, axis=0, keepdims=True)
    t_weight = jnp.exp2(t - t_top)
    t_sum = jnp.sum(t_weight, axis=0, keepdims=True)
    s_sum = jnp.sum(jnp.exp2(s - s_top), axis=0, keepdims=True)
    t_lse = t_top + jnp.log(t_sum) * LOG2E
    s_lse = s_top + jnp.log(s_sum) * LOG2E
    mean = jnp.sum(t_weight * ratio, axis=0, keepdims=True) / t_sum
    divergence = jnp.sum(mean - t_lse + s_lse)
    both = jnp.concatenate([t_lse, s_lse, jnp.zeros((6, ROWS), F32)], axis=0)
    lse[...] = both
    mine = lax.axis_index("xl") * BLOCK + sub_index() * SHARE
    turned = pltpu.roll(both, lax.rem(ROWS - mine, ROWS), axis=1)[:, :128]
    shifted = pltpu.roll(turned, SHARE, axis=1)
    lane = lax.broadcasted_iota(jnp.int32, (1, 128), 1)
    row = jnp.where(lane < SHARE, turned[0:1, :], shifted[1:2, :])
    row = jnp.where(lane < 2 * SHARE, row, divergence)
    for d in range(16):
        message[d] = row


def mixed_kernel(*refs):
    sets = [refs[6 * i : 6 * i + 6] for i in range(4)]
    lse, planes, partial, square, mh, ml = refs[24:]
    zl = lax.axis_index("zl")
    square[...] = jnp.zeros_like(square)
    for q in range(16):
        plane = 4 * (q % 4) + lax.rem(zl + OFFSETS[q // 4], 4)
        square[q : q + 1, :] = planes[plane]
    columns = square[...].T
    t_row = lse[0:1, :]
    s_row = lse[1:2, :]
    for q in range(16):
        part = slice(SHARE * q, SHARE * q + SHARE)
        inside = slice(SHARE * (q % 4), SHARE * (q % 4) + SHARE)
        t_ref, s_ref, te_ref, se_ref, _, local = sets[q // 4]
        if q % 4 == 0:
            t_factor = jnp.exp2(local[0:1, :] - t_row)
            s_factor = jnp.exp2(local[3:4, :] - s_row)
        t_key = columns[0:SHARE, q : q + 1]
        s_key = columns[SHARE : 2 * SHARE, q : q + 1]
        mixed = (se_ref[inside, :] * s_factor - te_ref[inside, :] * t_factor) + (
            jnp.exp2(s_ref[inside, :] - s_key) - jnp.exp2(t_ref[inside, :] - t_key)
        )
        high, low = split(mixed)
        mh[part, :] = high
        ml[part, :] = low

    def contract(a, b):
        return lax.dot_general(a, b, (((1,), (0,)), ((), ())), preferred_element_type=F32)

    kt = jnp.concatenate([v[4][...] for v in sets], axis=1)
    grad = contract(kt, mh[...])
    grad = grad[:DS, :] + grad[DS:, :] + contract(kt[:DS, :], ml[...])
    partial[...] = grad.T


def sum_kernel(parts, total):
    total[...] = jnp.sum(parts[...], axis=0)


def total_kernel(mine, partner, planes, blocks):
    total = (mine[...] + partner[...]) * (1.0 / math.sqrt(DS))
    divergence = jnp.max(jnp.sum(planes[...], axis=0)[:, 127:128])
    for d in range(8):
        blocks[d, 0:PAIR, :] = total
        blocks[d, PAIR:, :] = jnp.full((8, 128), divergence, F32)


def finish_kernel(factor, blocks, grad, loss):
    grad[...] = blocks[:, 0:PAIR, :]
    loss[0, 0] = jnp.max(blocks[0, PAIR:, :] + blocks[4, PAIR:, :]) * factor


def shards(teacher_q, student_q):
    own, shard = pl.pallas_call(
        select_kernel,
        out_shape=(shape(BLOCK, DT + DS), shape(SHARE, DT + DS)),
        in_specs=[pl.BlockSpec(memory_space=pltpu.HBM)] * 2,
        out_specs=[pl.BlockSpec(memory_space=pl.ANY)] * 2,
        scratch_shapes=[pltpu.SemaphoreType.DMA((4,))],
        compiler_params=pltpu.CompilerParams(vmem_limit_bytes=1 << 20),
    )(
        pltpu.with_memory_space_constraint(teacher_q, pltpu.HBM),
        pltpu.with_memory_space_constraint(student_q, pltpu.HBM),
    )
    near = lax.all_gather(shard, "zh", tiled=True)
    own, near = lax.optimization_barrier((own, near))
    other = permute(own, lambda xh, y, c, xl, z: (xh, y, c, 1 - xl, z))
    far = from_plane(near, 2, -2)
    up = from_plane(near, 1, 1)
    down = from_plane(near, -1, -1)
    tile = (*[shape(SET, ROWS)] * 4, shape(2 * DS, SET, dtype=BF16), shape(8, ROWS))
    halves = (shape(ROWS, DT + DS, dtype=BF16),) * 2
    rh, rl, *near_set = call(first_kernel, (*halves, *tile), (own, other, near))
    up_set = call(next_kernel, tile, (up, rh, rl))
    down_set = call(next_kernel, tile, (down, rh, rl))
    *far_set, stats = call(
        last_kernel,
        (*tile, shape(16, 1, 3 * ROWS)),
        (far, rh, rl, near_set[-1], up_set[-1], down_set[-1]),
    )
    everyone = lax.all_to_all(stats, PLANE, 0, 0, tiled=True)
    lse, message = call(
        combine_kernel, (shape(8, ROWS), shape(16, 1, 128)), (everyone,)
    )
    planes = lax.all_to_all(message, LINE, 0, 0, tiled=True)
    partial = call(
        mixed_kernel,
        shape(ROWS, DS),
        (*near_set, *far_set, *down_set, *up_set, lse, planes),
        [
            pltpu.VMEM((128, 128), F32),
            pltpu.VMEM((ROWS, ROWS), BF16),
            pltpu.VMEM((ROWS, ROWS), BF16),
        ],
    )
    parts = lax.all_to_all(partial.reshape(8, PAIR, DS), CHIPS, 0, 0, tiled=True)
    mine = call(sum_kernel, shape(PAIR, DS), (parts,))
    partner = permute(mine, lambda xh, y, c, xl, z: (xh, y, 1 - c, xl, z))
    blocks = call(total_kernel, shape(8, PAIR + 8, DS), (mine, partner, planes))
    blocks = lax.all_to_all(blocks, COPIES, 0, 0, tiled=True)
    factor = 1.0 / (LOG2E * 2 * BLOCK * 32)
    grad, loss = pl.pallas_call(
        functools.partial(finish_kernel, factor),
        out_shape=(shape(8, PAIR, DS), shape(1, 1)),
        in_specs=[pl.BlockSpec(memory_space=pltpu.VMEM)],
        out_specs=(pl.BlockSpec(memory_space=pltpu.VMEM), pl.BlockSpec(memory_space=pltpu.SMEM)),
        compiler_params=pltpu.CompilerParams(vmem_limit_bytes=8 << 20),
    )(blocks)
    return (grad.reshape(2, BLOCK, DS), loss.reshape(()))


def solution(mesh):
    fine = Mesh(mesh.devices.reshape(SIZES), AXES)
    tokens = P(None, ("xl", "zh", "zl"), None)
    return jax.shard_map(
        shards, mesh=fine, in_specs=(tokens, tokens), out_specs=(tokens, P()), check_vma=False
    )
```
